128 devices in a mesh: lat: 8 (over x_lo, y), lon: 16 (over z, x_hi, core).
Axes of the slice: x: 4 (x_hi: 2, x_lo: 2; x = x_hi * 2 + x_lo), y: 4, z: 4, core: 2. Of those that a mesh axis runs over, the one named last changes fastest.
Arguments:
- grad_rows: bfloat16 [131072, 128], P(('lat', 'lon')), may hold values from -6 to 6
- owner: int32 [131072, 1], P(('lat', 'lon')), may hold values from 0 to 127; in each aligned block of 1024 rows (0 to 1023, 1024 to 2047, ...) at most 16 rows name the same one
- lat_offset: int32 [131072], P(('lat', 'lon')), may hold values from 0 to 63
- lon_offset: int32 [131072], P(('lat', 'lon')), may hold values from 0 to 127
- position: bfloat16 [131072, 2], P(('lat', 'lon')), may hold values from 0 to 1
- live_count: int32 [128], P(('lat', 'lon')), may hold values from 512 to 1024
- features: bfloat16 [512, 2048, 128], P('lat', 'lon'), may hold values from -6 to 6
- conv_weight: bfloat16 [3, 3, 128, 128], replicated, may hold values from -0.1875 to 0.1875
Outputs:
- input_grad: bfloat16 [512, 2048, 128], P('lat', 'lon')
- weight_grad: float32 [3, 3, 128, 128], replicated
The draws below stay inside these ranges and needn't reach their ends.
Inputs may be any that keep to these rules, and one draw needn't show every extreme that they name: `owner`: among the 1024 rows of one device no tile is named more than 16 times, a bound that some block reaches. `live_count`: entry k counts the real rows among the rows of device k, which come first.
All inputs are finite; a program needn't handle non-finite values.
Results may differ from the reference program's by a relative error of at most 0.012.
Values may be sent and summed in bfloat16 or wider, within the bound.
No kernel may reach another device: no remote copies, remote signals or barrier semaphores. Data moves between devices by JAX's collectives and lax.ppermute only.
A program may use at most 128 MiB of HBM per device.

```python
import math
import jax
import jax.numpy as jnp
import numpy as np
from jax import lax

C = 128
CLAT = 64
CLON = 128
ROWS_DEV = 1024
CAP = 16
NLAT = 512
NLON = 2048
ROWS = 131072
N_LAT = 8
N_LON = 16


def with_ends(drawn, key, least, largest):
    longest = drawn.shape.index(max(drawn.shape))
    spots = []
    for shift in (0, 1):
        where = [jax.random.randint(jax.random.fold_in(key, axis), (), 0, length) for axis, length in enumerate(drawn.shape)]
        where[longest] = (where[longest] + shift) % drawn.shape[longest]
        spots.append(tuple(where))
    return drawn.at[spots[0]].set(least).at[spots[1]].set(largest)


def block_levels(own_key, shape, pieces, smallest, high):
    def one(dim, blocks):
        steps = jax.random.uniform(jax.random.fold_in(jax.random.fold_in(own_key, 6), dim), (blocks,), jnp.float32, smallest / len(pieces), high / len(pieces))
        return jnp.repeat(jnp.exp(steps), shape[dim] // blocks).reshape((-1,) + (1,) * (len(shape) - dim - 1))

    loudness = one(*pieces[0])
    for cut in pieces[1:]:
        loudness = loudness * one(*cut)
    return loudness


def deal_out(own_key, own, number, rows, number_of, top, limit, skew):
    order = jax.random.permutation(own_key, number_of)
    packed, usual = portions_of(number_of, rows * top, limit, skew, True), portions_of(number_of, rows * top, limit, skew, False)
    places = jnp.arange(number_of)

    def named(tallies, offset_by):
        used = int((tallies > 0).sum())
        fixed = max(1, used // 4)
        moved = fixed + (places - fixed + offset_by * (used - fixed)) % max(1, number_of - fixed)
        return jnp.zeros((number_of,), jnp.int32).at[order[jnp.where(places < fixed, places, moved)]].set(jnp.asarray(tallies, jnp.int32))

    tallies = jnp.where(number % 4 == 0, named(packed, number // 4), named(usual, number - number // 4 - 1))
    mixed = jax.random.permutation(jax.random.fold_in(own, 3), number_of)
    giver, receiver = mixed[0:number_of // 2 * 2:2], mixed[1:number_of // 2 * 2:2]
    room = jnp.minimum(tallies[giver] - 1, limit - tallies[receiver]) // 2
    room = jnp.where((giver == order[0]) | (receiver == order[0]) | (tallies[receiver] == 0), 0, jnp.maximum(room, 0))
    moved = jax.random.randint(jax.random.fold_in(own, 4), (number_of // 2,), 0, 1 << 20) % (room + 1)
    tallies = tallies.at[giver].add(-moved).at[receiver].add(moved)
    labels = jnp.searchsorted(jnp.cumsum(tallies), jnp.arange(rows * top), side="right").astype(jnp.int32)
    grid = labels.reshape(top, rows).T
    grid = grid[jax.random.permutation(jax.random.fold_in(own, 1), rows)]
    offset_by = jax.random.randint(jax.random.fold_in(own, 2), (rows, 1), 0, top)
    return jnp.take_along_axis(grid, (jnp.arange(top)[None, :] + offset_by) % top, axis=1)


def portions_of(number_of, total, reach, skew, full):
    portions = [(1 << 20) // math.isqrt(grade ** skew) + 1 for grade in range(1, number_of + 1)]
    largest = reach if full else min(reach, max(-(-total // number_of), total * portions[0] // sum(portions)))
    least = 1 if total - largest >= number_of - 1 else 0
    counts, rest = [largest] + [least] * (number_of - 1), total - largest - least * (number_of - 1)
    while rest > 0:
        movable = [i for i in range(1, number_of) if counts[i] < largest] or [i for i in range(1, number_of) if counts[i] < reach]
        whole, remaining = sum([portions[i] for i in movable]), rest
        for i in movable:
            more = min(reach - counts[i], max(1, remaining * portions[i] // whole), rest)
            counts[i] = counts[i] + more
            rest = rest - more
    return np.array(counts)


def noise(rng, extent, scale, reach, shards=(), kind=jnp.bfloat16):
    drawn = scale * jax.random.normal(rng, extent, jnp.float32)
    if shards:
        drawn = drawn * block_levels(rng, extent, shards, -0.22, 0.18)
    return jnp.clip(drawn, -reach, reach).astype(kind)


def setup_inputs(seed: int = 0) -> dict:
    key_list = jax.random.split(jax.random.key(seed), 9)
    grad_rows = noise(key_list[0], (ROWS, C), 1.0, 6.0, ((0, 128),))
    owner_keys = jax.random.split(jax.random.fold_in(key_list[1], 1), ROWS // ROWS_DEV)
    owner_turns = jax.random.permutation(jax.random.fold_in(key_list[1], 3), ROWS // ROWS_DEV)
    owner = jax.vmap(lambda own, number: deal_out(jax.random.fold_in(key_list[1], 2), own, number, ROWS_DEV, N_LAT * N_LON, 1, CAP, 2))(owner_keys, owner_turns).reshape((ROWS, 1))
    lat_offset = with_ends(jax.random.randint(key_list[2], (ROWS,), 0, CLAT), jax.random.fold_in(key_list[2], 1), 0, CLAT - 1).astype(jnp.int32)
    lon_offset = with_ends(jax.random.randint(key_list[3], (ROWS,), 0, CLON), jax.random.fold_in(key_list[3], 1), 0, CLON - 1).astype(jnp.int32)
    position = jnp.clip(1.0 * jax.random.uniform(key_list[4], (ROWS, 2), jnp.float32) ** block_levels(key_list[4], (ROWS, 2), ((0, 128),), -0.2, 0.2), 0.0, 1.0).astype(jnp.bfloat16)
    live_count = with_ends(jax.random.randint(key_list[5], (N_LAT * N_LON,), ROWS_DEV // 2, ROWS_DEV + 1), jax.random.fold_in(key_list[5], 1), ROWS_DEV // 2, ROWS_DEV).astype(jnp.int32)
    features = noise(key_list[6], (NLAT, NLON, C), 1.0, 6.0, ((0, 8), (1, 16)))
    conv_weight = noise(key_list[7], (3, 3, C, C), (9 * C) ** -0.5, 0.1875)
    return {"grad_rows": grad_rows, "owner": owner, "lat_offset": lat_offset, "lon_offset": lon_offset, "position": position, "live_count": live_count, "features": features, "conv_weight": conv_weight}


rbf_scale = 1.5


def profile(frac):
    tap_index = jnp.arange(8).astype(frac.dtype)
    return jnp.exp(-jnp.square(tap_index[None, :] - 3.0 - frac[:, None]) / (2.0 * rbf_scale * rbf_scale))


def reference(grad_rows, owner, lat_offset, lon_offset, position, live_count, features, conv_weight):
    row_total = grad_rows.shape[0]
    row_ids = jnp.arange(row_total, dtype=jnp.int32)
    is_live = (row_ids % ROWS_DEV) < live_count[row_ids // ROWS_DEV]
    owner_tile = owner[:, 0]
    base_lat = (owner_tile // N_LON) * CLAT + lat_offset - 3
    base_lon = (owner_tile % N_LON) * CLON + lon_offset - 3
    tap_ints = jnp.arange(8, dtype=jnp.int32)
    lat_cell = base_lat[:, None] + tap_ints[None, :]
    lon_cell = (base_lon[:, None] + tap_ints[None, :]) % NLON
    valid = (lat_cell >= 0) & (lat_cell < NLAT) & is_live[:, None]
    cell_index = jnp.where(valid[:, :, None], lat_cell[:, :, None] * NLON + lon_cell[:, None, :], NLAT * NLON).astype(jnp.int32)
    lat_weight = profile(position[:, 0].astype(jnp.float32)).astype(jnp.bfloat16)
    lon_weight = profile(position[:, 1].astype(jnp.float32)).astype(jnp.bfloat16)
    block_rows = math.gcd(row_total, 8192)
    blocks = row_total // block_rows

    def accumulate(canvas, payload):
        rows_blk, lat_blk, lon_blk, index_blk = payload
        spread = lon_blk[:, :, None] * rows_blk[:, None, :]
        updates = lat_blk.astype(jnp.float32)[:, :, None, None] * spread.astype(jnp.float32)[:, None, :, :]
        canvas = canvas.at[index_blk.reshape(-1)].add(updates.reshape(-1, C), mode="drop")
        return canvas, None

    canvas, _ = lax.scan(accumulate, jnp.zeros((NLAT * NLON, C), jnp.float32),
                         (grad_rows.reshape(blocks, block_rows, C), lat_weight.reshape(blocks, block_rows, 8),
                          lon_weight.reshape(blocks, block_rows, 8), cell_index.reshape(blocks, block_rows, 8, 8)))
    grid_grad = canvas.reshape(NLAT, NLON, C).astype(jnp.bfloat16)

    def pad_grid(field):
        padded = jnp.pad(field, ((1, 1), (0, 0), (0, 0)))
        return jnp.concatenate([padded[:, -1:], padded, padded[:, :1]], axis=1)

    grid_padded = pad_grid(grid_grad)
    input_padded = pad_grid(features)
    flat_grad = grid_grad.reshape(-1, C)
    input_grad = jnp.zeros((NLAT * NLON, C), jnp.float32)
    weight_parts = []
    for a in range(3):
        for b in range(3):
            shifted = grid_padded[2 - a:2 - a + NLAT, 2 - b:2 - b + NLON].reshape(-1, C)
            input_grad = input_grad + jnp.dot(shifted, conv_weight[a, b].T, preferred_element_type=jnp.float32)
            window = input_padded[a:a + NLAT, b:b + NLON].reshape(-1, C)
            weight_parts.append(jnp.dot(window.T, flat_grad, preferred_element_type=jnp.float32))
    weight_grad = jnp.stack(weight_parts).reshape(3, 3, C, C)
    return input_grad.reshape(NLAT, NLON, C).astype(jnp.bfloat16), weight_grad
```

```python
import functools

import jax
import jax.numpy as jnp
from jax import lax
from jax.experimental import pallas as pl
from jax.experimental.pallas import tpu as pltpu
from jax.sharding import PartitionSpec as P

AXES = ("lat", "lon")
BF16 = jnp.bfloat16
F32 = jnp.float32
SLOTS = 16
CHUNK = 24
TILES = 128
GAUSS = 2.0 * 1.5 * 1.5


def nt(lhs, rhs):
    return lax.dot_general(lhs, rhs, (((1,), (1,)), ((), ())), preferred_element_type=F32)


def mm(lhs, rhs):
    return jnp.dot(lhs, rhs, preferred_element_type=F32)


def pack_kernel(live_ref, own_ref, lat_ref, lon_ref, pos_ref, rows_ref, out_ref):
    count = own_ref.shape[1]
    lane = lax.broadcasted_iota(jnp.int32, (1, count), 1)
    own = jnp.where(lane < live_ref[0], own_ref[...], TILES)
    tile_line = lax.broadcasted_iota(jnp.int32, (TILES, count), 0)
    named = jnp.where(own == tile_line, 1.0, 0.0)
    named_b = named.astype(BF16)
    block = 256
    upper = jnp.where(
        lax.broadcasted_iota(jnp.int32, (block, block), 0)
        < lax.broadcasted_iota(jnp.int32, (block, block), 1),
        1.0,
        0.0,
    ).astype(BF16)
    ones = jnp.ones((block, block), BF16)
    before = jnp.zeros((TILES, block), F32)
    ranks = []
    for b in range(count // block):
        part = named_b[:, b * block : (b + 1) * block]
        earlier = mm(part, upper) + before
        ranks.append(
            jnp.sum(earlier * named[:, b * block : (b + 1) * block], axis=0, keepdims=True)
        )
        before = before + mm(part, ones)
    rank = jnp.concatenate(ranks, axis=1).astype(jnp.int32)
    slot = own * SLOTS + rank
    rows = rows_ref[...]
    step = 1024
    for q in range(TILES * SLOTS // step):
        line = lax.broadcasted_iota(jnp.int32, (step, count), 0) + q * step
        picked = jnp.where(slot == line, 1.0, 0.0).astype(BF16)
        moved = mm(picked, rows).astype(BF16)
        out_ref[q * step // SLOTS : (q + 1) * step // SLOTS, 0:SLOTS, :] = moved.reshape(
            step // SLOTS, SLOTS, 128
        )
    at_rank = lax.broadcasted_iota(jnp.int32, (SLOTS, count), 0) == rank
    pos = pos_ref[...].astype(F32)
    fields = (
        lat_ref[...].astype(F32),
        lon_ref[...].astype(F32),
        pos[0:1, :],
        pos[1:2, :],
    )
    spots = [jnp.where(at_rank, f, 0.0) for f in fields]
    spots.append(jnp.zeros((128 - SLOTS * len(fields), count), F32))
    cells = nt(named_b, jnp.concatenate(spots, axis=0).astype(BF16)).astype(BF16)
    out_ref[:, SLOTS:CHUNK, :] = jnp.broadcast_to(
        cells.astype(F32)[:, None, :], (TILES, CHUNK - SLOTS, 128)
    ).astype(BF16)


def pack(live, own, lat, lon, pos, rows):
    vmem = pl.BlockSpec(memory_space=pltpu.VMEM)
    return pl.pallas_call(
        pack_kernel,
        out_shape=jax.ShapeDtypeStruct((TILES, CHUNK, 128), BF16),
        in_specs=[pl.BlockSpec(memory_space=pltpu.SMEM)] + [vmem] * 5,
        out_specs=vmem,
        cost_estimate=pl.CostEstimate(flops=700_000_000, bytes_accessed=1_500_000, transcendentals=0),
        name="pack",
    )(live, own, lat, lon, pos, rows)


def tap_weights(cell, frac, offset):
    tap = offset - cell + 3.0
    dist = tap - 3.0 - frac
    weight = jnp.exp(-(dist * dist) / GAUSS)
    return jnp.where((tap >= 0.0) & (tap <= 7.0), weight, 0.0)


def scatter_kernel(edge_ref, in_ref, canvas_ref, rows_ref, lat_w, lon_w, side_w):
    total = TILES * SLOTS
    rows_ref[...] = in_ref[:, 0:SLOTS, :].reshape(total, 128)
    tail = in_ref[:, SLOTS:CHUNK, :].reshape(TILES * (CHUNK - SLOTS), 128)
    first = jnp.where(
        lax.broadcasted_iota(jnp.int32, (TILES, tail.shape[0]), 1)
        == (CHUNK - SLOTS) * lax.broadcasted_iota(jnp.int32, (TILES, tail.shape[0]), 0),
        1.0,
        0.0,
    ).astype(BF16)
    cells = mm(first, tail)
    cells_t = cells.T.astype(BF16)[: 4 * SLOTS]
    slot_lane = lax.broadcasted_iota(jnp.int32, (TILES, total), 1)
    spread = jnp.where(
        (slot_lane // SLOTS) == lax.broadcasted_iota(jnp.int32, (TILES, total), 0), 1.0, 0.0
    ).astype(BF16)
    wide = mm(cells_t, spread)
    own_slot = (
        lax.broadcasted_iota(jnp.int32, (SLOTS, total), 1) % SLOTS
        == lax.broadcasted_iota(jnp.int32, (SLOTS, total), 0)
    )
    cell_lat, cell_lon, frac_lat, frac_lon = [
        jnp.sum(
            jnp.where(own_slot, wide[f * SLOTS : (f + 1) * SLOTS], 0.0), axis=0, keepdims=True
        )
        for f in range(4)
    ]
    line = lax.broadcasted_iota(jnp.int32, (72, total), 0)
    kept = (line >= edge_ref[0]) & (line < edge_ref[1])
    lat_w[...] = jnp.where(
        kept, tap_weights(cell_lat, frac_lat, line.astype(F32) - 4.0), 0.0
    )
    column = lax.broadcasted_iota(jnp.int32, (128, total), 0).astype(F32)
    lon_w[...] = tap_weights(cell_lon, frac_lon, column).astype(BF16)
    line8 = lax.broadcasted_iota(jnp.int32, (8, total), 0)
    column = jnp.where(line8 < 4, line8 - 4, line8 + 124).astype(F32)
    side_w[...] = tap_weights(cell_lon, frac_lon, column).astype(BF16).astype(F32)

    def eight_lines(step, carry):
        start = pl.multiple_of(step * 8, 8)
        lat8 = lat_w[pl.ds(start, 8), :]
        acc = jnp.zeros((8 * 128, 128), F32)
        side = jnp.zeros((8 * 8, 128), F32)
        for k in range(total // 256):
            cols = slice(k * 256, (k + 1) * 256)
            lon = lon_w[:, cols].reshape(8, 16, 256)
            parts = []
            side_parts = []
            side_lon = side_w[:, cols]
            for i in range(8):
                one = jnp.broadcast_to(lat8[i : i + 1, cols], (16, 256)).astype(BF16)
                parts.append((lon * one[None]).reshape(128, 256))
                one8 = jnp.broadcast_to(
                    lat8[i : i + 1, cols].astype(BF16).astype(F32), (8, 256)
                )
                side_parts.append(side_lon * one8)
            rows = rows_ref[cols, :]
            acc = acc + mm(jnp.concatenate(parts, axis=0), rows)
            side = side + mm(jnp.concatenate(side_parts, axis=0).astype(BF16), rows)
        canvas_ref[pl.ds(start, 8), 0:128, :] = acc.astype(BF16).reshape(8, 128, 128)
        canvas_ref[pl.ds(start, 8), 128:136, :] = side.reshape(8, 8, 128).astype(BF16)
        return carry

    lax.fori_loop(0, 9, eight_lines, 0)


def scatter(edge, incoming):
    vmem = pl.BlockSpec(memory_space=pltpu.VMEM)
    total = TILES * SLOTS
    return pl.pallas_call(
        scatter_kernel,
        out_shape=jax.ShapeDtypeStruct((72, 136, 128), BF16),
        in_specs=[pl.BlockSpec(memory_space=pltpu.SMEM), vmem],
        out_specs=vmem,
        scratch_shapes=[
            pltpu.VMEM((total, 128), BF16),
            pltpu.VMEM((72, total), F32),
            pltpu.VMEM((128, total), BF16),
            pltpu.VMEM((8, total), F32),
        ],
        compiler_params=pltpu.CompilerParams(vmem_limit_bytes=40 << 20),
        cost_estimate=pl.CostEstimate(
            flops=5_200_000_000, bytes_accessed=3_500_000, transcendentals=500_000
        ),
        name="scatter",
    )(edge, incoming)


def padded_2(cells, sides, width, closed):
    for axis, dim in sides:
        count = lax.axis_size(axis)
        ends = count if closed else count - 1
        head = lax.slice_in_dim(cells, 0, width, axis=dim)
        tail = lax.slice_in_dim(cells, cells.shape[dim] - width, cells.shape[dim], axis=dim)
        cells = jnp.concatenate(
            [
                lax.ppermute(tail, axis, [(i, (i + 1) % count) for i in range(ends)]),
                cells,
                lax.ppermute(head, axis, [((i + 1) % count, i) for i in range(ends)]),
            ],
            axis=dim,
        )
    return cells


def clear_rim(padded):
    lat_index = lax.axis_index("lat")
    lat_count = lax.axis_size("lat")
    row_line = jnp.arange(padded.shape[0], dtype=jnp.int32)
    masked = (row_line == 0) & (lat_index == 0) | (row_line == padded.shape[0] - 1) & (
        lat_index == lat_count - 1
    )
    return jnp.where(masked[:, None, None], jnp.zeros_like(padded), padded)


def total_sum(parts):
    padded = jnp.pad(parts.astype(BF16), ((0, TILES * 16 - parts.shape[0]), (0, 0)))
    got = lax.all_to_all(padded.reshape(TILES, 16, 128), AXES, 0, 0, tiled=True)
    mine = jnp.sum(got.astype(F32), axis=0).astype(BF16)
    every = jnp.broadcast_to(mine[None], (TILES, 16, 128))
    every = lax.all_to_all(every, AXES, 0, 0, tiled=True)
    return every.reshape(TILES * 16, 128)[: parts.shape[0]].astype(F32)


def shards(grad_rows, owner, lat_offset, lon_offset, position, live_count, features, conv_weight):
    channels = grad_rows.shape[1]
    tile_lat = features.shape[0]
    tile_lon = features.shape[1]
    input_padded = clear_rim(padded_2(features, (("lat", 0), ("lon", 1)), 1, True))
    count = grad_rows.shape[0]
    outgoing = pack(
        live_count,
        owner.reshape(1, count),
        lat_offset.reshape(1, count),
        lon_offset.reshape(1, count),
        position.T,
        grad_rows,
    )
    incoming = lax.all_to_all(outgoing, AXES, 0, 0, tiled=True)
    lat_index = lax.axis_index("lat")
    edge = jnp.stack(
        [
            jnp.where(lat_index == 0, 4, 0),
            jnp.where(lat_index == lax.axis_size("lat") - 1, 68, 72),
        ]
    ).astype(jnp.int32)
    canvas = scatter(edge, incoming).astype(F32)
    canvas = jnp.concatenate([canvas[:, 128:132], canvas[:, :128], canvas[:, 132:]], axis=1)
    edge_rows = jnp.concatenate([canvas[:5], canvas[-5:]], axis=0)
    edge_rows = padded_2(edge_rows.astype(jnp.bfloat16), (("lat", 0),), 5, False).astype(
        edge_rows.dtype
    )
    inner = canvas[4:-4]
    inner = inner.at[:4].add(edge_rows[1:5]).at[-4:].add(edge_rows[15:19])
    rim_top = edge_rows[0] + canvas[3]
    rim_bottom = canvas[-4] + edge_rows[19]
    tall = jnp.concatenate([rim_top[None], inner, rim_bottom[None]], axis=0)
    side_cols = jnp.concatenate([tall[:, :5], tall[:, -5:]], axis=1)
    side_cols = padded_2(side_cols.astype(jnp.bfloat16), (("lon", 1),), 5, True).astype(
        side_cols.dtype
    )
    middle = tall[:, 4:-4]
    middle = middle.at[:, :4].add(side_cols[:, 1:5]).at[:, -4:].add(side_cols[:, 15:19])
    rim_left = side_cols[:, 0] + tall[:, 3]
    rim_right = tall[:, -4] + side_cols[:, 19]
    whole = jnp.concatenate([rim_left[:, None], middle, rim_right[:, None]], axis=1)
    grid_padded = clear_rim(whole.astype(jnp.bfloat16))
    grid_grad = grid_padded[1:-1, 1:-1]
    flat_grad = grid_grad.reshape(-1, channels)
    input_grad = jnp.zeros((tile_lat * tile_lon, channels), jnp.float32)
    weight_parts = []
    for a in range(3):
        for b in range(3):
            shifted = grid_padded[2 - a : 2 - a + tile_lat, 2 - b : 2 - b + tile_lon].reshape(
                -1, channels
            )
            input_grad = input_grad + lax.dot_general(
                shifted,
                conv_weight[a, b],
                (((1,), (1,)), ((), ())),
                preferred_element_type=jnp.float32,
            )
            window = input_padded[a : a + tile_lat, b : b + tile_lon].reshape(-1, channels)
            weight_parts.append(
                lax.dot_general(
                    window, flat_grad, (((0,), (0,)), ((), ())), preferred_element_type=jnp.float32
                )
            )
    weight_grad = total_sum(jnp.concatenate(weight_parts, axis=0))
    return (
        input_grad.reshape(tile_lat, tile_lon, channels).astype(jnp.bfloat16),
        weight_grad.reshape(3, 3, channels, channels),
    )


def solution(mesh):
    placed = (
        P(("lat", "lon"), None),
        P(("lat", "lon"), None),
        P(("lat", "lon")),
        P(("lat", "lon")),
        P(("lat", "lon"), None),
        P(("lat", "lon")),
        P("lat", "lon", None),
        P(),
    )
    return jax.shard_map(
        shards, mesh=mesh, in_specs=placed, out_specs=(P("lat", "lon", None), P()), check_vma=False
    )
```

```python
import functools

import jax
import jax.numpy as jnp
from jax import lax
from jax.experimental import pallas as pl
from jax.experimental.pallas import tpu as pltpu
from jax.sharding import PartitionSpec as P

AXES = ("lat", "lon")
BF16 = jnp.bfloat16
F32 = jnp.float32
SLOTS = 16
CHUNK = 24
TILES = 128
GAUSS = 2.0 * 1.5 * 1.5


def nt(lhs, rhs):
    return lax.dot_general(lhs, rhs, (((1,), (1,)), ((), ())), preferred_element_type=F32)


def mm(lhs, rhs):
    return jnp.dot(lhs, rhs, preferred_element_type=F32)


def pack_kernel(live_ref, own_ref, lat_ref, lon_ref, pos_ref, rows_ref, out_ref):
    count = own_ref.shape[1]
    lane = lax.broadcasted_iota(jnp.int32, (1, count), 1)
    own = jnp.where(lane < live_ref[0], own_ref[...], TILES)
    tile_line = lax.broadcasted_iota(jnp.int32, (TILES, count), 0)
    named = jnp.where(own == tile_line, 1.0, 0.0)
    named_b = named.astype(BF16)
    block = 256
    upper = jnp.where(
        lax.broadcasted_iota(jnp.int32, (block, block), 0)
        < lax.broadcasted_iota(jnp.int32, (block, block), 1),
        1.0,
        0.0,
    ).astype(BF16)
    ones = jnp.ones((block, block), BF16)
    before = jnp.zeros((TILES, block), F32)
    ranks = []
    for b in range(count // block):
        part = named_b[:, b * block : (b + 1) * block]
        earlier = mm(part, upper) + before
        ranks.append(
            jnp.sum(earlier * named[:, b * block : (b + 1) * block], axis=0, keepdims=True)
        )
        before = before + mm(part, ones)
    rank = jnp.concatenate(ranks, axis=1).astype(jnp.int32)
    slot = own * SLOTS + rank
    rows = rows_ref[...]
    step = 1024
    for q in range(TILES * SLOTS // step):
        line = lax.broadcasted_iota(jnp.int32, (step, count), 0) + q * step
        picked = jnp.where(slot == line, 1.0, 0.0).astype(BF16)
        moved = mm(picked, rows).astype(BF16)
        out_ref[q * step // SLOTS : (q + 1) * step // SLOTS, 0:SLOTS, :] = moved.reshape(
            step // SLOTS, SLOTS, 128
        )
    at_rank = lax.broadcasted_iota(jnp.int32, (SLOTS, count), 0) == rank
    pos = pos_ref[...].astype(F32)
    fields = (
        lat_ref[...].astype(F32),
        lon_ref[...].astype(F32),
        pos[0:1, :],
        pos[1:2, :],
    )
    spots = [jnp.where(at_rank, f, 0.0) for f in fields]
    spots.append(jnp.zeros((128 - SLOTS * len(fields), count), F32))
    cells = nt(named_b, jnp.concatenate(spots, axis=0).astype(BF16)).astype(BF16)
    out_ref[:, SLOTS:CHUNK, :] = jnp.broadcast_to(
        cells.astype(F32)[:, None, :], (TILES, CHUNK - SLOTS, 128)
    ).astype(BF16)


def pack(live, own, lat, lon, pos, rows):
    vmem = pl.BlockSpec(memory_space=pltpu.VMEM)
    return pl.pallas_call(
        pack_kernel,
        out_shape=jax.ShapeDtypeStruct((TILES, CHUNK, 128), BF16),
        in_specs=[pl.BlockSpec(memory_space=pltpu.SMEM)] + [vmem] * 5,
        out_specs=vmem,
        cost_estimate=pl.CostEstimate(flops=700_000_000, bytes_accessed=1_500_000, transcendentals=0),
        name="pack",
    )(live, own, lat, lon, pos, rows)


def tap_weights(cell, frac, offset):
    tap = offset - cell + 3.0
    dist = tap - 3.0 - frac
    weight = jnp.exp(-(dist * dist) / GAUSS)
    return jnp.where((tap >= 0.0) & (tap <= 7.0), weight, 0.0)


def prep_kernel(feat_ref, above_ref, below_ref, left_ref, right_ref, out_ref, side_ref):
    eye = jnp.where(
        lax.broadcasted_iota(jnp.int32, (128, 128), 0)
        == lax.broadcasted_iota(jnp.int32, (128, 128), 1),
        1.0,
        0.0,
    ).astype(BF16)
    spot = lax.broadcasted_iota(jnp.int32, (144, 384), 0)
    want = lax.broadcasted_iota(jnp.int32, (144, 384), 1)
    want = want % 128 + want // 128 - 1
    want = jnp.where(want < 0, 135, jnp.where(want == 128, 136, want))
    shift = jnp.where(spot == want, 1.0, 0.0).astype(BF16)

    def lines(take, start, count):
        turned = []
        for i in range(count):
            ext = jnp.concatenate(
                [take(i), jnp.concatenate([left_ref[start + i], right_ref[start + i]], axis=0)],
                axis=0,
            )
            turned.append(nt(eye, ext).astype(BF16))
        moved = mm(jnp.concatenate(turned, axis=0), shift).astype(BF16)
        out_ref[pl.ds(start, count)] = moved.reshape(count, 128, 384)

    lines(lambda i: above_ref[i], 0, 5)

    def body(step, carry):
        lines(lambda i: feat_ref[step * 8 + i], step * 8 + 5, 8)
        return carry

    lax.fori_loop(0, 8, body, 0)
    lines(lambda i: below_ref[i], 69, 5)
    left = left_ref[...].astype(F32)
    right = right_ref[...].astype(F32)
    first = jnp.concatenate(
        [above_ref[:, 0:8, :], feat_ref[:, 0:8, :], below_ref[:, 0:8, :]], axis=0
    ).astype(F32)
    last = jnp.concatenate(
        [above_ref[:, 120:128, :], feat_ref[:, 120:128, :], below_ref[:, 120:128, :]], axis=0
    ).astype(F32)
    groups = (
        (left[:, 3:7], last[:, 7:8], right[:, 0:3]),
        (left[:, 4:8], right[:, 0:4]),
        (left[:, 5:8], first[:, 0:1], right[:, 1:5]),
    )
    for b in range(3):
        eight = jnp.concatenate(groups[b], axis=1).reshape(592, 128)
        eight = jnp.concatenate([eight, jnp.zeros((48, 128), F32)], axis=0)
        side_ref[b * 128 : (b + 1) * 128, :] = eight.T.astype(BF16)


def prep(features, above, below, left, right):
    vmem = pl.BlockSpec(memory_space=pltpu.VMEM)
    return pl.pallas_call(
        prep_kernel,
        out_shape=(
            jax.ShapeDtypeStruct((74, 128, 384), BF16),
            jax.ShapeDtypeStruct((384, 640), BF16),
        ),
        in_specs=[vmem] * 5,
        out_specs=(vmem, vmem),
        compiler_params=pltpu.CompilerParams(vmem_limit_bytes=24 << 20),
        cost_estimate=pl.CostEstimate(
            flops=2_500_000_000, bytes_accessed=10_000_000, transcendentals=0
        ),
        name="prep",
    )(features, above, below, left, right)


def scatter_kernel(
    edge_ref,
    in_ref,
    feat_ref,
    feat_side_ref,
    canvas_ref,
    up_ref,
    down_ref,
    sum_ref,
    rows_ref,
    lat_w,
    lon_w,
    side_w,
    three,
    three_side,
    acc_ref,
):
    total = TILES * SLOTS
    rows_ref[...] = in_ref[:, 0:SLOTS, :].reshape(total, 128)
    tail = in_ref[:, SLOTS:CHUNK, :].reshape(TILES * (CHUNK - SLOTS), 128)
    first = jnp.where(
        lax.broadcasted_iota(jnp.int32, (TILES, tail.shape[0]), 1)
        == (CHUNK - SLOTS) * lax.broadcasted_iota(jnp.int32, (TILES, tail.shape[0]), 0),
        1.0,
        0.0,
    ).astype(BF16)
    cells = mm(first, tail)
    cells_t = cells.T.astype(BF16)[: 4 * SLOTS]
    slot_lane = lax.broadcasted_iota(jnp.int32, (TILES, total), 1)
    spread = jnp.where(
        (slot_lane // SLOTS) == lax.broadcasted_iota(jnp.int32, (TILES, total), 0), 1.0, 0.0
    ).astype(BF16)
    wide = mm(cells_t, spread)
    own_slot = (
        lax.broadcasted_iota(jnp.int32, (SLOTS, total), 1) % SLOTS
        == lax.broadcasted_iota(jnp.int32, (SLOTS, total), 0)
    )
    cell_lat, cell_lon, frac_lat, frac_lon = [
        jnp.sum(
            jnp.where(own_slot, wide[f * SLOTS : (f + 1) * SLOTS], 0.0), axis=0, keepdims=True
        )
        for f in range(4)
    ]
    line = lax.broadcasted_iota(jnp.int32, (72, total), 0)
    kept = (line >= edge_ref[0]) & (line < edge_ref[1])
    lat_w[...] = jnp.where(
        kept, tap_weights(cell_lat, frac_lat, line.astype(F32) - 4.0), 0.0
    )
    column = lax.broadcasted_iota(jnp.int32, (128, total), 0).astype(F32)
    lon_w[...] = tap_weights(cell_lon, frac_lon, column).astype(BF16)
    line8 = lax.broadcasted_iota(jnp.int32, (8, total), 0)
    column = jnp.where(line8 < 4, line8 - 4, line8 + 124).astype(F32)
    side_w[...] = tap_weights(cell_lon, frac_lon, column).astype(BF16).astype(F32)
    blank = jnp.zeros((2, 128, 128), BF16)
    three[0:2, :, 256:384] = blank
    three[72:74, :, 0:128] = blank
    three[0:1, :, 128:256] = blank[:1]
    three[73:74, :, 128:256] = blank[:1]
    three_side[...] = jnp.zeros_like(three_side)
    acc_ref[...] = jnp.zeros_like(acc_ref)

    def weight_part(start, count):
        parts = []
        for b in range(3):
            parts.append(
                jnp.concatenate(
                    [feat_ref[start + i, :, b * 128 : (b + 1) * 128] for i in range(count)],
                    axis=1,
                )
            )
        acc_ref[...] += mm(
            jnp.concatenate(parts, axis=0),
            three[pl.ds(start, count)].reshape(count * 128, 384),
        )

    def eight_lines(step, carry):
        start = pl.multiple_of(step * 8, 8)
        lat8 = lat_w[pl.ds(start, 8), :]
        acc = jnp.zeros((8 * 128, 128), F32)
        side = jnp.zeros((8 * 8, 128), F32)
        for k in range(total // 256):
            cols = slice(k * 256, (k + 1) * 256)
            lon = lon_w[:, cols].reshape(8, 16, 256)
            parts = []
            side_parts = []
            side_lon = side_w[:, cols]
            for i in range(8):
                one = jnp.broadcast_to(lat8[i : i + 1, cols], (16, 256)).astype(BF16)
                parts.append((lon * one[None]).reshape(128, 256))
                one8 = jnp.broadcast_to(
                    lat8[i : i + 1, cols].astype(BF16).astype(F32), (8, 256)
                )
                side_parts.append(side_lon * one8)
            rows = rows_ref[cols, :]
            acc = acc + mm(jnp.concatenate(parts, axis=0), rows)
            side = side + mm(jnp.concatenate(side_parts, axis=0).astype(BF16), rows)
        main = acc.astype(BF16).reshape(8, 128, 128)
        canvas_ref[pl.ds(start, 8), 0:128, :] = main
        for a in range(3):
            three[pl.ds(start + a, 8), :, a * 128 : (a + 1) * 128] = main
        side = side.reshape(8, 8, 128)
        canvas_ref[pl.ds(start, 8), 128:136, :] = side.astype(BF16)
        for a in range(3):
            three_side[pl.ds(start + a, 8), :, a * 128 : (a + 1) * 128] = side
        weight_part(start, 8)
        return carry

    lax.fori_loop(0, 9, eight_lines, 0)
    weight_part(72, 2)
    acc = acc_ref[...] + mm(
        feat_side_ref[...], three_side[...].reshape(640, 384).astype(BF16)
    )
    for a in range(3):
        for b in range(3):
            at = (a * 3 + b) * 128
            sum_ref[at : at + 128, :] = acc[
                b * 128 : (b + 1) * 128, a * 128 : (a + 1) * 128
            ].astype(BF16)
    sum_ref[1152:, :] = jnp.zeros((2048 - 1152, 128), BF16)
    up_ref[...] = canvas_ref[1:5]
    down_ref[...] = canvas_ref[67:72]


def scatter(edge, incoming, feat, feat_side):
    vmem = pl.BlockSpec(memory_space=pltpu.VMEM)
    total = TILES * SLOTS
    return pl.pallas_call(
        scatter_kernel,
        out_shape=(
            jax.ShapeDtypeStruct((72, 136, 128), BF16),
            jax.ShapeDtypeStruct((4, 136, 128), BF16),
            jax.ShapeDtypeStruct((5, 136, 128), BF16),
            jax.ShapeDtypeStruct((2048, 128), BF16),
        ),
        in_specs=[pl.BlockSpec(memory_space=pltpu.SMEM), vmem, vmem, vmem],
        out_specs=(vmem,) * 4,
        scratch_shapes=[
            pltpu.VMEM((total, 128), BF16),
            pltpu.VMEM((72, total), F32),
            pltpu.VMEM((128, total), BF16),
            pltpu.VMEM((8, total), F32),
            pltpu.VMEM((74, 128, 384), BF16),
            pltpu.VMEM((80, 8, 384), F32),
            pltpu.VMEM((384, 384), F32),
        ],
        compiler_params=pltpu.CompilerParams(vmem_limit_bytes=44 << 20),
        cost_estimate=pl.CostEstimate(
            flops=8_200_000_000, bytes_accessed=12_000_000, transcendentals=500_000
        ),
        name="scatter",
    )(edge, incoming, feat, feat_side)


def sides_kernel(canvas_ref, above_ref, below_ref, right_ref, left_ref):
    def tall(cols):
        block = canvas_ref[3:69, cols, :].astype(F32)
        return jnp.concatenate(
            [
                block[0:5] + above_ref[:, cols, :].astype(F32),
                block[5:62],
                block[62:66] + below_ref[:, cols, :].astype(F32),
            ],
            axis=0,
        )

    side = tall(slice(128, 136))
    last = tall(slice(120, 128))
    head = tall(slice(0, 8))
    blank = jnp.zeros((66, 4, 128), F32)
    right_ref[...] = jnp.concatenate([last[:, 7:8], side[:, 4:8], blank[:, :3]], axis=1).astype(
        BF16
    )
    left_ref[...] = jnp.concatenate([side[:, 1:4], head[:, 0:1], blank], axis=1).astype(BF16)


def sides(canvas, above, below):
    vmem = pl.BlockSpec(memory_space=pltpu.VMEM)
    shape = jax.ShapeDtypeStruct((66, 8, 128), BF16)
    return pl.pallas_call(
        sides_kernel,
        out_shape=(shape, shape),
        in_specs=[vmem] * 3,
        out_specs=(vmem, vmem),
        cost_estimate=pl.CostEstimate(flops=1_000_000, bytes_accessed=1_000_000, transcendentals=0),
        name="sides",
    )(canvas, above, below)


def conv_kernel(canvas_ref, above_ref, below_ref, left_ref, right_ref, weight_ref, out_ref, grid):
    @pl.when(pl.program_id(0) == 0)
    def _():
        grid[5:62, 0:128, :] = canvas_ref[8:65, 0:128, :]
        grid[0:5, 0:128, :] = (
            canvas_ref[3:8, 0:128, :].astype(F32) + above_ref[:, 0:128, :].astype(F32)
        ).astype(BF16)
        grid[62:66, 0:128, :] = (
            canvas_ref[65:69, 0:128, :].astype(F32) + below_ref[:, 0:128, :].astype(F32)
        ).astype(BF16)
        left = left_ref[...].astype(F32)
        right = right_ref[...].astype(F32)
        blank = jnp.zeros((66, 14, 128), F32)
        grid[:, 0:16, :] = (
            grid[:, 0:16, :].astype(F32)
            + jnp.concatenate([left[:, 1:5], blank[:, :12]], axis=1)
        ).astype(BF16)
        grid[:, 112:128, :] = (
            grid[:, 112:128, :].astype(F32)
            + jnp.concatenate([blank[:, :13], right[:, 0:3]], axis=1)
        ).astype(BF16)
        side = canvas_ref[3:69, 128:136, :].astype(F32)
        side = jnp.concatenate(
            [
                side[0:5] + above_ref[:, 128:136, :].astype(F32),
                side[5:62],
                side[62:66] + below_ref[:, 128:136, :].astype(F32),
            ],
            axis=0,
        )
        grid[:, 128:144, :] = jnp.concatenate(
            [side[:, 4:5] + right[:, 3:4], blank, side[:, 3:4] + left[:, 0:1]], axis=1
        ).astype(BF16)

    start = pl.program_id(0) * 8
    taps = jnp.concatenate(
        [grid[pl.ds(start + 2 - a, 8)].reshape(8 * 144, 128) for a in range(3)], axis=1
    )
    weight = jnp.concatenate([weight_ref[a].reshape(384, 128) for a in range(3)], axis=1)
    every = nt(taps, weight).reshape(8, 144, 384)
    for i in range(8):
        one = every[i]
        got = (
            one[:, 128:256]
            + pltpu.roll(one[:, 0:128], 143, 0)
            + pltpu.roll(one[:, 256:384], 1, 0)
        )
        out_ref[i] = got[0:128].astype(BF16)


def conv(canvas, above, below, left, right, weight):
    def whole(x):
        return pl.BlockSpec(
            x.shape, lambda i: (0,) * x.ndim, pipeline_mode=pl.Buffered(1)
        )

    args = (canvas, above, below, left, right, weight)
    return pl.pallas_call(
        conv_kernel,
        grid=(8,),
        out_shape=jax.ShapeDtypeStruct((64, 128, 128), BF16),
        in_specs=[whole(x) for x in args],
        out_specs=pl.BlockSpec((8, 128, 128), lambda i: (i, 0, 0)),
        scratch_shapes=[pltpu.VMEM((66, 144, 128), BF16)],
        compiler_params=pltpu.CompilerParams(vmem_limit_bytes=24 << 20),
        cost_estimate=pl.CostEstimate(
            flops=2_700_000_000, bytes_accessed=4_500_000, transcendentals=0
        ),
        name="conv",
    )(*args)


def gather_kernel(in_ref, out_ref):
    mine = jnp.sum(in_ref[...].astype(F32), axis=0)
    out_ref[...] = jnp.broadcast_to(mine.astype(BF16)[None], out_ref.shape)


def share(got):
    vmem = pl.BlockSpec(memory_space=pltpu.VMEM)
    return pl.pallas_call(
        gather_kernel,
        out_shape=jax.ShapeDtypeStruct(got.shape, BF16),
        in_specs=[vmem],
        out_specs=vmem,
        cost_estimate=pl.CostEstimate(flops=300_000, bytes_accessed=1_000_000, transcendentals=0),
        name="share",
    )(got)


def both_ways(forth, back, axis, closed):
    count = lax.axis_size(axis)
    ends = count if closed else count - 1
    return (
        lax.ppermute(forth, axis, [(i, (i + 1) % count) for i in range(ends)]),
        lax.ppermute(back, axis, [((i + 1) % count, i) for i in range(ends)]),
    )


def shards(grad_rows, owner, lat_offset, lon_offset, position, live_count, features, conv_weight):
    count = grad_rows.shape[0]
    lat_index = lax.axis_index("lat")
    edge = jnp.stack(
        [
            jnp.where(lat_index == 0, 4, 0),
            jnp.where(lat_index == lax.axis_size("lat") - 1, 68, 72),
        ]
    ).astype(jnp.int32)
    outgoing = pack(
        live_count,
        owner.reshape(1, count),
        lat_offset.reshape(1, count),
        lon_offset.reshape(1, count),
        position.T,
        grad_rows,
    )
    incoming = lax.all_to_all(outgoing, AXES, 0, 0, tiled=True)
    above, below = both_ways(features[59:64], features[0:5], "lat", False)
    ends = [
        jnp.concatenate([x[:, c : c + 8] for x in (above, features, below)], axis=0)
        for c in (120, 0)
    ]
    left, right = both_ways(ends[0], ends[1], "lon", True)
    feat, feat_side = prep(features, above, below, left, right)
    canvas, up, down, part = scatter(edge, incoming, feat, feat_side)
    got = lax.all_to_all(part.reshape(TILES, 16, 128), AXES, 0, 0, tiled=True)
    grid_above, grid_below = both_ways(down, up, "lat", False)
    send_right, send_left = sides(canvas, grid_above, grid_below)
    from_left, from_right = both_ways(send_right, send_left, "lon", True)
    every = lax.all_to_all(share(got), AXES, 0, 0, tiled=True)
    input_grad = conv(canvas, grid_above, grid_below, from_left, from_right, conv_weight)
    weight_grad = every.reshape(TILES * 16, 128)[:1152].astype(F32)
    return input_grad, weight_grad.reshape(3, 3, 128, 128)


def solution(mesh):
    placed = (
        P(("lat", "lon"), None),
        P(("lat", "lon"), None),
        P(("lat", "lon")),
        P(("lat", "lon")),
        P(("lat", "lon"), None),
        P(("lat", "lon")),
        P("lat", "lon", None),
        P(),
    )
    return jax.shard_map(
        shards, mesh=mesh, in_specs=placed, out_specs=(P("lat", "lon", None), P()), check_vma=False
    )
```

```python
import functools

import jax
import jax.numpy as jnp
from jax import lax
from jax.experimental import pallas as pl
from jax.experimental.pallas import tpu as pltpu
from jax.sharding import PartitionSpec as P

AXES = ("lat", "lon")
BF16 = jnp.bfloat16
F32 = jnp.float32
SLOTS = 16
CHUNK = 24
TILES = 128
MOST_VMEM = 62_600_000
GAUSS = 2.0 * 1.5 * 1.5


def nt(lhs, rhs):
    return lax.dot_general(lhs, rhs, (((1,), (1,)), ((), ())), preferred_element_type=F32)


def mm(lhs, rhs):
    return jnp.dot(lhs, rhs, preferred_element_type=F32)


def pack_kernel(live_ref, own_ref, lat_ref, lon_ref, pos_ref, rows_ref, out_ref):
    count = own_ref.shape[1]
    lane = lax.broadcasted_iota(jnp.int32, (1, count), 1)
    own = jnp.where(lane < live_ref[0], own_ref[...], TILES)
    tile_line = lax.broadcasted_iota(jnp.int32, (TILES, count), 0)
    named = jnp.where(own == tile_line, 1.0, 0.0)
    named_b = named.astype(BF16)
    block = 256
    upper = jnp.where(
        lax.broadcasted_iota(jnp.int32, (block, block), 0)
        < lax.broadcasted_iota(jnp.int32, (block, block), 1),
        1.0,
        0.0,
    ).astype(BF16)
    ones = jnp.ones((block, block), BF16)
    before = jnp.zeros((TILES, block), F32)
    ranks = []
    for b in range(count // block):
        part = named_b[:, b * block : (b + 1) * block]
        earlier = mm(part, upper) + before
        ranks.append(
            jnp.sum(earlier * named[:, b * block : (b + 1) * block], axis=0, keepdims=True)
        )
        before = before + mm(part, ones)
    rank = jnp.concatenate(ranks, axis=1).astype(jnp.int32)
    slot = own * SLOTS + rank
    rows = rows_ref[...]
    step = 1024
    for q in range(TILES * SLOTS // step):
        line = lax.broadcasted_iota(jnp.int32, (step, count), 0) + q * step
        picked = jnp.where(slot == line, 1.0, 0.0).astype(BF16)
        moved = mm(picked, rows).astype(BF16)
        out_ref[q * step // SLOTS : (q + 1) * step // SLOTS, 0:SLOTS, :] = moved.reshape(
            step // SLOTS, SLOTS, 128
        )
    at_rank = lax.broadcasted_iota(jnp.int32, (SLOTS, count), 0) == rank
    pos = pos_ref[...].astype(F32)
    fields = (
        lat_ref[...].astype(F32),
        lon_ref[...].astype(F32),
        pos[0:1, :],
        pos[1:2, :],
    )
    spots = [jnp.where(at_rank, f, 0.0) for f in fields]
    spots.append(jnp.zeros((128 - SLOTS * len(fields), count), F32))
    cells = nt(named_b, jnp.concatenate(spots, axis=0).astype(BF16)).astype(BF16)
    out_ref[:, SLOTS:CHUNK, :] = jnp.broadcast_to(
        cells.astype(F32)[:, None, :], (TILES, CHUNK - SLOTS, 128)
    ).astype(BF16)


def pack(live, own, lat, lon, pos, rows):
    vmem = pl.BlockSpec(memory_space=pltpu.VMEM)
    return pl.pallas_call(
        pack_kernel,
        out_shape=jax.ShapeDtypeStruct((TILES, CHUNK, 128), BF16),
        in_specs=[pl.BlockSpec(memory_space=pltpu.SMEM)] + [vmem] * 5,
        out_specs=vmem,
        cost_estimate=pl.CostEstimate(flops=700_000_000, bytes_accessed=1_500_000, transcendentals=0),
        name="pack",
    )(live, own, lat, lon, pos, rows)


def tap_weights(cell, frac, offset):
    tap = offset - cell + 3.0
    dist = tap - 3.0 - frac
    weight = jnp.exp(-(dist * dist) / GAUSS)
    return jnp.where((tap >= 0.0) & (tap <= 7.0), weight, 0.0)


def column_shift():
    spot = lax.broadcasted_iota(jnp.int32, (128, 384), 0)
    want = lax.broadcasted_iota(jnp.int32, (128, 384), 1)
    want = want % 128 + want // 128 - 1
    return jnp.where(spot == want, 1.0, 0.0).astype(BF16)


def identity():
    return jnp.where(
        lax.broadcasted_iota(jnp.int32, (128, 128), 0)
        == lax.broadcasted_iota(jnp.int32, (128, 128), 1),
        1.0,
        0.0,
    ).astype(BF16)


def turn_lines(lines, eye, shift):
    turned = jnp.concatenate([nt(eye, x).astype(BF16) for x in lines], axis=0)
    moved = mm(turned, shift).astype(BF16)
    return [moved[:, b * 128 : (b + 1) * 128].reshape(len(lines), 128, 128) for b in range(3)]


def prep_kernel(feat_ref, out_ref):
    moved = turn_lines([feat_ref[i] for i in range(8)], identity(), column_shift())
    for b in range(3):
        out_ref[b] = moved[b]


def prep(features):
    return pl.pallas_call(
        prep_kernel,
        grid=(8,),
        out_shape=jax.ShapeDtypeStruct((3, 64, 128, 128), BF16),
        in_specs=[pl.BlockSpec((8, 128, 128), lambda i: (i, 0, 0))],
        out_specs=pl.BlockSpec((3, 8, 128, 128), lambda i: (0, i, 0, 0)),
        cost_estimate=pl.CostEstimate(
            flops=2_200_000_000, bytes_accessed=8_000_000, transcendentals=0
        ),
        name="prep",
    )(features)


def prep_edge_kernel(head_ref, last_ref, above_ref, below_ref, left_ref, right_ref, out_ref, side_ref):
    eye = identity()
    shift = column_shift()
    moved = turn_lines(
        [above_ref[i] for i in range(5)] + [below_ref[i] for i in range(5)], eye, shift
    )
    for b in range(3):
        out_ref[b] = moved[b]
    left = left_ref[...].astype(F32)
    right = right_ref[...].astype(F32)
    first = head_ref[...].astype(F32)
    last = last_ref[...].astype(F32)
    none = jnp.zeros((74, 8, 128), F32)
    groups = (
        (left[:, 3:7], last[:, 7:8], right[:, 0:3], left[:, 7:8], none[:, :7]),
        (left[:, 4:8], right[:, 0:4], none),
        (left[:, 5:8], first[:, 0:1], right[:, 1:5], none[:, :1], right[:, 0:1], none[:, :6]),
    )
    for b in range(3):
        cells = jnp.concatenate(groups[b], axis=1).reshape(1184, 128)
        cells = jnp.concatenate([cells, jnp.zeros((96, 128), F32)], axis=0).astype(BF16)
        side_ref[b * 128 : (b + 1) * 128, :] = nt(eye, cells).astype(BF16)


def prep_edge(head, last, above, below, left, right):
    vmem = pl.BlockSpec(memory_space=pltpu.VMEM)
    return pl.pallas_call(
        prep_edge_kernel,
        out_shape=(
            jax.ShapeDtypeStruct((3, 10, 128, 128), BF16),
            jax.ShapeDtypeStruct((384, 1280), BF16),
        ),
        in_specs=[vmem] * 6,
        out_specs=(vmem, vmem),
        cost_estimate=pl.CostEstimate(
            flops=500_000_000, bytes_accessed=3_000_000, transcendentals=0
        ),
        name="prep_edge",
    )(head, last, above, below, left, right)


def scatter_kernel(
    edge_ref,
    in_ref,
    feat_hbm,
    feat_edge_hbm,
    feat_side_hbm,
    canvas_hbm,
    rim_hbm,
    up_hbm,
    down_hbm,
    sum_hbm,
    rows_ref,
    lat_w,
    lon_w,
    side_w,
    three,
    three_side,
    acc_ref,
    feat_ref,
    feat_edge_ref,
    feat_side_ref,
    canvas_ref,
    rim_ref,
    sum_ref,
    load_sem,
    store_sem,
):
    loads = [
        pltpu.make_async_copy(feat_hbm, feat_ref, load_sem.at[0]),
        pltpu.make_async_copy(feat_edge_hbm, feat_edge_ref, load_sem.at[1]),
        pltpu.make_async_copy(feat_side_hbm, feat_side_ref, load_sem.at[2]),
    ]
    for copy in loads:
        copy.start()
    total = TILES * SLOTS
    rows_ref[...] = in_ref[:, 0:SLOTS, :].reshape(total, 128)
    tail = in_ref[:, SLOTS:CHUNK, :].reshape(TILES * (CHUNK - SLOTS), 128)
    first = jnp.where(
        lax.broadcasted_iota(jnp.int32, (TILES, tail.shape[0]), 1)
        == (CHUNK - SLOTS) * lax.broadcasted_iota(jnp.int32, (TILES, tail.shape[0]), 0),
        1.0,
        0.0,
    ).astype(BF16)
    cells = mm(first, tail)
    cells_t = cells.T.astype(BF16)[: 4 * SLOTS]
    slot_lane = lax.broadcasted_iota(jnp.int32, (TILES, total), 1)
    spread = jnp.where(
        (slot_lane // SLOTS) == lax.broadcasted_iota(jnp.int32, (TILES, total), 0), 1.0, 0.0
    ).astype(BF16)
    wide = mm(cells_t, spread)
    own_slot = (
        lax.broadcasted_iota(jnp.int32, (SLOTS, total), 1) % SLOTS
        == lax.broadcasted_iota(jnp.int32, (SLOTS, total), 0)
    )
    cell_lat, cell_lon, frac_lat, frac_lon = [
        jnp.sum(
            jnp.where(own_slot, wide[f * SLOTS : (f + 1) * SLOTS], 0.0), axis=0, keepdims=True
        )
        for f in range(4)
    ]
    line = lax.broadcasted_iota(jnp.int32, (72, total), 0)
    kept = (line >= edge_ref[0]) & (line < edge_ref[1])
    lat_w[...] = jnp.where(
        kept, tap_weights(cell_lat, frac_lat, line.astype(F32) - 4.0), 0.0
    )
    column = lax.broadcasted_iota(jnp.int32, (128, total), 0).astype(F32)
    lon_w[...] = tap_weights(cell_lon, frac_lon, column).astype(BF16)
    line8 = lax.broadcasted_iota(jnp.int32, (8, total), 0)
    column = jnp.where(line8 < 4, line8 - 4, line8 + 124).astype(F32)
    side_w[...] = tap_weights(cell_lon, frac_lon, column).astype(BF16).astype(F32)
    blank = jnp.zeros((2, 128, 128), BF16)
    three[0:2, :, 256:384] = blank
    three[72:74, :, 0:128] = blank
    three[0:1, :, 128:256] = blank[:1]
    three[73:74, :, 128:256] = blank[:1]
    three_side[...] = jnp.zeros_like(three_side)
    acc_ref[...] = jnp.zeros_like(acc_ref)

    def weight_part(take, at):
        lhs = jnp.concatenate([jnp.concatenate(take(b), axis=1) for b in range(3)], axis=0)
        rhs = jnp.concatenate(
            [three[x:y].reshape((y - x) * 128, 384) for x, y in at], axis=0
        )
        acc_ref[...] += mm(lhs, rhs)

    def eight_lines(step, carry):
        start = pl.multiple_of(step * 8, 8)
        lat8 = lat_w[pl.ds(start, 8), :]
        acc = jnp.zeros((8 * 128, 128), F32)
        side = jnp.zeros((8 * 8, 128), F32)
        for k in range(total // 256):
            cols = slice(k * 256, (k + 1) * 256)
            lon = lon_w[:, cols].reshape(8, 16, 256)
            parts = []
            side_parts = []
            side_lon = side_w[:, cols]
            for i in range(8):
                one = jnp.broadcast_to(lat8[i : i + 1, cols], (16, 256)).astype(BF16)
                parts.append((lon * one[None]).reshape(128, 256))
                one8 = jnp.broadcast_to(
                    lat8[i : i + 1, cols].astype(BF16).astype(F32), (8, 256)
                )
                side_parts.append(side_lon * one8)
            rows = rows_ref[cols, :]
            acc = acc + mm(jnp.concatenate(parts, axis=0), rows)
            side = side + mm(jnp.concatenate(side_parts, axis=0).astype(BF16), rows)
        main = acc.astype(BF16).reshape(8, 128, 128)
        canvas_ref[pl.ds(start, 8), 0:128, :] = main
        for a in range(3):
            three[pl.ds(start + a, 8), :, a * 128 : (a + 1) * 128] = main
        side = side.reshape(8, 8, 128)
        canvas_ref[pl.ds(start, 8), 128:136, :] = side.astype(BF16)
        ends = acc.reshape(8, 128, 128)
        side = jnp.concatenate(
            [side, ends[:, 0:1], ends[:, 127:128], jnp.zeros((8, 6, 128), F32)], axis=1
        )
        for a in range(3):
            three_side[pl.ds(start + a, 8), :, a * 128 : (a + 1) * 128] = side
        rim_ref[pl.ds(start, 8), 0:8, :] = ends[:, 0:8].astype(BF16)
        rim_ref[pl.ds(start, 8), 8:16, :] = ends[:, 120:128].astype(BF16)
        rim_ref[pl.ds(start, 8), 16:24, :] = side[:, 0:8].astype(BF16)
        return carry

    lax.fori_loop(0, 9, eight_lines, 0)
    stores = [
        pltpu.make_async_copy(canvas_ref, canvas_hbm, store_sem.at[0]),
        pltpu.make_async_copy(rim_ref, rim_hbm, store_sem.at[1]),
        pltpu.make_async_copy(canvas_ref.at[1:5], up_hbm, store_sem.at[2]),
        pltpu.make_async_copy(canvas_ref.at[67:72], down_hbm, store_sem.at[3]),
    ]
    for copy in stores:
        copy.start()
    for copy in loads:
        copy.wait()
    for part in range(2):
        weight_part(
            lambda b: [feat_ref[b, part * 32 + i] for i in range(32)],
            ((5 + part * 32, 37 + part * 32),),
        )
    weight_part(lambda b: [feat_edge_ref[b, i] for i in range(10)], ((0, 5), (69, 74)))
    acc = acc_ref[...] + mm(
        feat_side_ref[...], three_side[...].reshape(1280, 384).astype(BF16)
    )
    for a in range(3):
        for b in range(3):
            at = (a * 3 + b) * 128
            sum_ref[at : at + 128, :] = acc[
                b * 128 : (b + 1) * 128, a * 128 : (a + 1) * 128
            ].astype(BF16)
    sum_ref[1152:, :] = jnp.zeros((2048 - 1152, 128), BF16)
    last = pltpu.make_async_copy(sum_ref, sum_hbm, store_sem.at[4])
    last.start()
    for copy in stores:
        copy.wait()
    last.wait()


def scatter(edge, incoming, feat, feat_edge, feat_side):
    vmem = pl.BlockSpec(memory_space=pltpu.VMEM)
    hbm = pl.BlockSpec(memory_space=pltpu.HBM)
    total = TILES * SLOTS
    return pl.pallas_call(
        scatter_kernel,
        out_shape=(
            jax.ShapeDtypeStruct((72, 136, 128), BF16),
            jax.ShapeDtypeStruct((72, 24, 128), BF16),
            jax.ShapeDtypeStruct((4, 136, 128), BF16),
            jax.ShapeDtypeStruct((5, 136, 128), BF16),
            jax.ShapeDtypeStruct((2048, 128), BF16),
        ),
        in_specs=[pl.BlockSpec(memory_space=pltpu.SMEM), vmem] + [hbm] * 3,
        out_specs=(hbm,) * 5,
        scratch_shapes=[
            pltpu.VMEM((total, 128), BF16),
            pltpu.VMEM((72, total), F32),
            pltpu.VMEM((128, total), BF16),
            pltpu.VMEM((8, total), F32),
            pltpu.VMEM((74, 128, 384), BF16),
            pltpu.VMEM((80, 16, 384), F32),
            pltpu.VMEM((384, 384), F32),
            pltpu.VMEM((3, 64, 128, 128), BF16),
            pltpu.VMEM((3, 10, 128, 128), BF16),
            pltpu.VMEM((384, 1280), BF16),
            pltpu.VMEM((72, 136, 128), BF16),
            pltpu.VMEM((72, 24, 128), BF16),
            pltpu.VMEM((2048, 128), BF16),
            pltpu.SemaphoreType.DMA((3,)),
            pltpu.SemaphoreType.DMA((5,)),
        ],
        compiler_params=pltpu.CompilerParams(vmem_limit_bytes=MOST_VMEM),
        cost_estimate=pl.CostEstimate(
            flops=8_200_000_000, bytes_accessed=12_000_000, transcendentals=500_000
        ),
        name="scatter",
    )(edge, incoming, feat, feat_edge, feat_side)


def sides_kernel(rim_ref, above_ref, below_ref, right_ref, left_ref):
    def tall(at, cols):
        block = rim_ref[3:69, at : at + 8, :].astype(F32)
        return jnp.concatenate(
            [
                block[0:5] + above_ref[:, cols : cols + 8, :].astype(F32),
                block[5:62],
                block[62:66] + below_ref[:, cols : cols + 8, :].astype(F32),
            ],
            axis=0,
        )

    head = tall(0, 0)
    last = tall(8, 120)
    side = tall(16, 128)
    blank = jnp.zeros((66, 4, 128), F32)
    right_ref[...] = jnp.concatenate([last[:, 7:8], side[:, 4:8], blank[:, :3]], axis=1).astype(
        BF16
    )
    left_ref[...] = jnp.concatenate([side[:, 1:4], head[:, 0:1], blank], axis=1).astype(BF16)


def sides(rim, above, below):
    vmem = pl.BlockSpec(memory_space=pltpu.VMEM)
    shape = jax.ShapeDtypeStruct((66, 8, 128), BF16)
    return pl.pallas_call(
        sides_kernel,
        out_shape=(shape, shape),
        in_specs=[vmem] * 3,
        out_specs=(vmem, vmem),
        cost_estimate=pl.CostEstimate(flops=1_000_000, bytes_accessed=1_000_000, transcendentals=0),
        compiler_params=pltpu.CompilerParams(vmem_limit_bytes=4 << 20),
        name="sides",
    )(rim, above, below)


def conv_kernel(canvas_ref, above_ref, below_ref, left_ref, right_ref, weight_ref, out_ref, grid):
    @pl.when(pl.program_id(0) == 0)
    def _():
        grid[5:62, 0:128, :] = canvas_ref[8:65, 0:128, :]
        grid[0:5, 0:128, :] = (
            canvas_ref[3:8, 0:128, :].astype(F32) + above_ref[:, 0:128, :].astype(F32)
        ).astype(BF16)
        grid[62:66, 0:128, :] = (
            canvas_ref[65:69, 0:128, :].astype(F32) + below_ref[:, 0:128, :].astype(F32)
        ).astype(BF16)
        left = left_ref[...].astype(F32)
        right = right_ref[...].astype(F32)
        blank = jnp.zeros((66, 14, 128), F32)
        grid[:, 0:16, :] = (
            grid[:, 0:16, :].astype(F32)
            + jnp.concatenate([left[:, 1:5], blank[:, :12]], axis=1)
        ).astype(BF16)
        grid[:, 112:128, :] = (
            grid[:, 112:128, :].astype(F32)
            + jnp.concatenate([blank[:, :13], right[:, 0:3]], axis=1)
        ).astype(BF16)
        side = canvas_ref[3:69, 128:136, :].astype(F32)
        side = jnp.concatenate(
            [
                side[0:5] + above_ref[:, 128:136, :].astype(F32),
                side[5:62],
                side[62:66] + below_ref[:, 128:136, :].astype(F32),
            ],
            axis=0,
        )
        grid[:, 128:144, :] = jnp.concatenate(
            [side[:, 4:5] + right[:, 3:4], blank, side[:, 3:4] + left[:, 0:1]], axis=1
        ).astype(BF16)

    start = pl.program_id(0) * 8
    taps = jnp.concatenate(
        [grid[pl.ds(start + 2 - a, 8)].reshape(8 * 144, 128) for a in range(3)], axis=1
    )
    weight = jnp.concatenate([weight_ref[a].reshape(384, 128) for a in range(3)], axis=1)
    every = nt(taps, weight).reshape(8, 144, 384)
    for i in range(8):
        one = every[i]
        got = (
            one[:, 128:256]
            + pltpu.roll(one[:, 0:128], 143, 0)
            + pltpu.roll(one[:, 256:384], 1, 0)
        )
        out_ref[i] = got[0:128].astype(BF16)


def conv(canvas, above, below, left, right, weight):
    def whole(x):
        return pl.BlockSpec(
            x.shape, lambda i: (0,) * x.ndim, pipeline_mode=pl.Buffered(1)
        )

    args = (canvas, above, below, left, right, weight)
    return pl.pallas_call(
        conv_kernel,
        grid=(8,),
        out_shape=jax.ShapeDtypeStruct((64, 128, 128), BF16),
        in_specs=[whole(x) for x in args],
        out_specs=pl.BlockSpec((8, 128, 128), lambda i: (i, 0, 0)),
        scratch_shapes=[pltpu.VMEM((66, 144, 128), BF16)],
        compiler_params=pltpu.CompilerParams(vmem_limit_bytes=MOST_VMEM),
        cost_estimate=pl.CostEstimate(
            flops=2_700_000_000, bytes_accessed=4_500_000, transcendentals=0
        ),
        name="conv",
    )(*args)


def gather_kernel(in_ref, out_ref):
    mine = jnp.sum(in_ref[...].astype(F32), axis=0)
    out_ref[...] = jnp.broadcast_to(mine.astype(BF16)[None], out_ref.shape)


def share(got):
    vmem = pl.BlockSpec(memory_space=pltpu.VMEM)
    return pl.pallas_call(
        gather_kernel,
        out_shape=jax.ShapeDtypeStruct(got.shape, BF16),
        in_specs=[vmem],
        out_specs=vmem,
        cost_estimate=pl.CostEstimate(flops=300_000, bytes_accessed=1_000_000, transcendentals=0),
        compiler_params=pltpu.CompilerParams(vmem_limit_bytes=3 << 20),
        name="share",
    )(got)


def finish_kernel(in_ref, out_ref):
    out_ref[...] = in_ref[...].reshape(384, 128).astype(F32)


def finish(every):
    return pl.pallas_call(
        finish_kernel,
        grid=(3,),
        out_shape=jax.ShapeDtypeStruct((1152, 128), F32),
        in_specs=[pl.BlockSpec((24, 16, 128), lambda i: (i, 0, 0))],
        out_specs=pl.BlockSpec((384, 128), lambda i: (i, 0)),
        compiler_params=pltpu.CompilerParams(vmem_limit_bytes=2 << 20),
        cost_estimate=pl.CostEstimate(flops=0, bytes_accessed=900_000, transcendentals=0),
        name="finish",
    )(every)


def both_ways(forth, back, axis, closed):
    count = lax.axis_size(axis)
    ends = count if closed else count - 1
    return (
        lax.ppermute(forth, axis, [(i, (i + 1) % count) for i in range(ends)]),
        lax.ppermute(back, axis, [((i + 1) % count, i) for i in range(ends)]),
    )


def shards(grad_rows, owner, lat_offset, lon_offset, position, live_count, features, conv_weight):
    count = grad_rows.shape[0]
    lat_index = lax.axis_index("lat")
    edge = jnp.stack(
        [
            jnp.where(lat_index == 0, 4, 0),
            jnp.where(lat_index == lax.axis_size("lat") - 1, 68, 72),
        ]
    ).astype(jnp.int32)
    outgoing = pack(
        live_count,
        owner.reshape(1, count),
        lat_offset.reshape(1, count),
        lon_offset.reshape(1, count),
        position.T,
        grad_rows,
    )
    incoming = lax.all_to_all(outgoing, AXES, 0, 0, tiled=True)
    above, below = both_ways(features[59:64], features[0:5], "lat", False)
    last, head = [
        jnp.concatenate([x[:, c : c + 8] for x in (above, features, below)], axis=0)
        for c in (120, 0)
    ]
    left, right = both_ways(last, head, "lon", True)
    feat = prep(features)
    feat_edge, feat_side = prep_edge(head, last, above, below, left, right)
    canvas, rim, up, down, part = scatter(edge, incoming, feat, feat_edge, feat_side)
    got = lax.all_to_all(part.reshape(TILES, 16, 128), AXES, 0, 0, tiled=True)
    grid_above, grid_below = both_ways(down, up, "lat", False)
    send_right, send_left = sides(rim, grid_above, grid_below)
    got, send_right, send_left = lax.optimization_barrier((got, send_right, send_left))
    from_left, from_right = both_ways(send_right, send_left, "lon", True)
    every = lax.all_to_all(share(got), AXES, 0, 0, tiled=True)
    input_grad = conv(canvas, grid_above, grid_below, from_left, from_right, conv_weight)
    weight_grad = finish(every)
    return input_grad, weight_grad.reshape(3, 3, 128, 128)


def solution(mesh):
    placed = (
        P(("lat", "lon"), None),
        P(("lat", "lon"), None),
        P(("lat", "lon")),
        P(("lat", "lon")),
        P(("lat", "lon"), None),
        P(("lat", "lon")),
        P("lat", "lon", None),
        P(),
    )
    return jax.shard_map(
        shards, mesh=mesh, in_specs=placed, out_specs=(P("lat", "lon", None), P()), check_vma=False
    )
```

```python
import functools

import jax
import jax.numpy as jnp
from jax import lax
from jax.experimental import pallas as pl
from jax.experimental.pallas import tpu as pltpu
from jax.sharding import PartitionSpec as P

AXES = ("lat", "lon")
BF16 = jnp.bfloat16
F32 = jnp.float32
SLOTS = 16
CHUNK = 24
TILES = 128
MOST_VMEM = 62_600_000
GAUSS = 2.0 * 1.5 * 1.5


def nt(lhs, rhs):
    return lax.dot_general(lhs, rhs, (((1,), (1,)), ((), ())), preferred_element_type=F32)


def mm(lhs, rhs):
    return jnp.dot(lhs, rhs, preferred_element_type=F32)


def pack_kernel(live_ref, own_ref, lat_ref, lon_ref, pos_ref, rows_ref, out_ref):
    count = own_ref.shape[1]
    lane = lax.broadcasted_iota(jnp.int32, (1, count), 1)
    own = jnp.where(lane < live_ref[0], own_ref[...], TILES)
    tile_line = lax.broadcasted_iota(jnp.int32, (TILES, count), 0)
    named = jnp.where(own == tile_line, 1.0, 0.0)
    named_b = named.astype(BF16)
    block = 256
    upper = jnp.where(
        lax.broadcasted_iota(jnp.int32, (block, block), 0)
        < lax.broadcasted_iota(jnp.int32, (block, block), 1),
        1.0,
        0.0,
    ).astype(BF16)
    ones = jnp.ones((block, block), BF16)
    before = jnp.zeros((TILES, block), F32)
    ranks = []
    for b in range(count // block):
        part = named_b[:, b * block : (b + 1) * block]
        earlier = mm(part, upper) + before
        ranks.append(
            jnp.sum(earlier * named[:, b * block : (b + 1) * block], axis=0, keepdims=True)
        )
        before = before + mm(part, ones)
    rank = jnp.concatenate(ranks, axis=1).astype(jnp.int32)
    slot = own * SLOTS + rank
    rows = rows_ref[...]
    step = 1024
    for q in range(TILES * SLOTS // step):
        line = lax.broadcasted_iota(jnp.int32, (step, count), 0) + q * step
        picked = jnp.where(slot == line, 1.0, 0.0).astype(BF16)
        moved = mm(picked, rows).astype(BF16)
        out_ref[q * step // SLOTS : (q + 1) * step // SLOTS, 0:SLOTS, :] = moved.reshape(
            step // SLOTS, SLOTS, 128
        )
    at_rank = lax.broadcasted_iota(jnp.int32, (SLOTS, count), 0) == rank
    pos = pos_ref[...].astype(F32)
    fields = (
        lat_ref[...].astype(F32),
        lon_ref[...].astype(F32),
        pos[0:1, :],
        pos[1:2, :],
    )
    spots = [jnp.where(at_rank, f, 0.0) for f in fields]
    spots.append(jnp.zeros((128 - SLOTS * len(fields), count), F32))
    cells = nt(named_b, jnp.concatenate(spots, axis=0).astype(BF16)).astype(BF16)
    out_ref[:, SLOTS:CHUNK, :] = jnp.broadcast_to(
        cells.astype(F32)[:, None, :], (TILES, CHUNK - SLOTS, 128)
    ).astype(BF16)


def pack(live, own, lat, lon, pos, rows):
    vmem = pl.BlockSpec(memory_space=pltpu.VMEM)
    return pl.pallas_call(
        pack_kernel,
        out_shape=jax.ShapeDtypeStruct((TILES, CHUNK, 128), BF16),
        in_specs=[pl.BlockSpec(memory_space=pltpu.SMEM)] + [vmem] * 5,
        out_specs=vmem,
        cost_estimate=pl.CostEstimate(flops=700_000_000, bytes_accessed=1_500_000, transcendentals=0),
        name="pack",
    )(live, own, lat, lon, pos, rows)


def tap_weights(cell, frac, offset):
    tap = offset - cell + 3.0
    dist = tap - 3.0 - frac
    weight = jnp.exp(-(dist * dist) / GAUSS)
    return jnp.where((tap >= 0.0) & (tap <= 7.0), weight, 0.0)


def column_shift():
    spot = lax.broadcasted_iota(jnp.int32, (128, 384), 0)
    want = lax.broadcasted_iota(jnp.int32, (128, 384), 1)
    want = want % 128 + want // 128 - 1
    return jnp.where(spot == want, 1.0, 0.0).astype(BF16)


def identity():
    return jnp.where(
        lax.broadcasted_iota(jnp.int32, (128, 128), 0)
        == lax.broadcasted_iota(jnp.int32, (128, 128), 1),
        1.0,
        0.0,
    ).astype(BF16)


def turn_lines(lines, eye, shift):
    turned = jnp.concatenate([nt(eye, x).astype(BF16) for x in lines], axis=0)
    moved = mm(turned, shift).astype(BF16)
    return [moved[:, b * 128 : (b + 1) * 128].reshape(len(lines), 128, 128) for b in range(3)]


def prep_kernel(feat_ref, out_ref, eye_ref, shift_ref):
    @pl.when(pl.program_id(0) == 0)
    def _():
        eye_ref[...] = identity()
        shift_ref[...] = column_shift()

    moved = turn_lines([feat_ref[i] for i in range(8)], eye_ref[...], shift_ref[...])
    for b in range(3):
        out_ref[b] = moved[b]


def prep(features):
    return pl.pallas_call(
        prep_kernel,
        grid=(8,),
        out_shape=jax.ShapeDtypeStruct((3, 64, 128, 128), BF16),
        in_specs=[pl.BlockSpec((8, 128, 128), lambda i: (i, 0, 0))],
        out_specs=pl.BlockSpec((3, 8, 128, 128), lambda i: (0, i, 0, 0)),
        scratch_shapes=[pltpu.VMEM((128, 128), BF16), pltpu.VMEM((128, 384), BF16)],
        cost_estimate=pl.CostEstimate(
            flops=2_200_000_000, bytes_accessed=8_000_000, transcendentals=0
        ),
        name="prep",
    )(features)


def prep_edge_kernel(head_ref, last_ref, above_ref, below_ref, left_ref, right_ref, out_ref, side_ref):
    eye = identity()
    shift = column_shift()
    moved = turn_lines(
        [above_ref[i] for i in range(5)] + [below_ref[i] for i in range(5)], eye, shift
    )
    for b in range(3):
        out_ref[b] = moved[b]
    left = left_ref[...].astype(F32)
    right = right_ref[...].astype(F32)
    first = head_ref[...].astype(F32)
    last = last_ref[...].astype(F32)
    none = jnp.zeros((74, 8, 128), F32)
    groups = (
        (left[:, 3:7], last[:, 7:8], right[:, 0:3], left[:, 7:8], none[:, :7]),
        (left[:, 4:8], right[:, 0:4], none),
        (left[:, 5:8], first[:, 0:1], right[:, 1:5], none[:, :1], right[:, 0:1], none[:, :6]),
    )
    for b in range(3):
        cells = jnp.concatenate(groups[b], axis=1).reshape(1184, 128)
        cells = jnp.concatenate([cells, jnp.zeros((96, 128), F32)], axis=0).astype(BF16)
        side_ref[b * 128 : (b + 1) * 128, :] = nt(eye, cells).astype(BF16)


def prep_edge(head, last, above, below, left, right):
    vmem = pl.BlockSpec(memory_space=pltpu.VMEM)
    return pl.pallas_call(
        prep_edge_kernel,
        out_shape=(
            jax.ShapeDtypeStruct((3, 10, 128, 128), BF16),
            jax.ShapeDtypeStruct((384, 1280), BF16),
        ),
        in_specs=[vmem] * 6,
        out_specs=(vmem, vmem),
        cost_estimate=pl.CostEstimate(
            flops=500_000_000, bytes_accessed=3_000_000, transcendentals=0
        ),
        name="prep_edge",
    )(head, last, above, below, left, right)


def scatter_kernel(
    edge_ref,
    in_ref,
    feat_hbm,
    feat_edge_hbm,
    feat_side_hbm,
    canvas_hbm,
    rim_hbm,
    up_hbm,
    down_hbm,
    sum_hbm,
    rows_ref,
    lat_w,
    lon_w,
    side_w,
    three,
    three_side,
    acc_ref,
    feat_ref,
    feat_edge_ref,
    feat_side_ref,
    canvas_ref,
    rim_ref,
    sum_ref,
    load_sem,
    store_sem,
):
    loads = [
        pltpu.make_async_copy(feat_hbm, feat_ref, load_sem.at[0]),
        pltpu.make_async_copy(feat_edge_hbm, feat_edge_ref, load_sem.at[1]),
        pltpu.make_async_copy(feat_side_hbm, feat_side_ref, load_sem.at[2]),
    ]
    for copy in loads:
        copy.start()
    total = TILES * SLOTS
    rows_ref[...] = in_ref[:, 0:SLOTS, :].reshape(total, 128)
    tail = in_ref[:, SLOTS:CHUNK, :].reshape(TILES * (CHUNK - SLOTS), 128)
    first = jnp.where(
        lax.broadcasted_iota(jnp.int32, (TILES, tail.shape[0]), 1)
        == (CHUNK - SLOTS) * lax.broadcasted_iota(jnp.int32, (TILES, tail.shape[0]), 0),
        1.0,
        0.0,
    ).astype(BF16)
    cells = mm(first, tail)
    cells_t = cells.T.astype(BF16)[: 4 * SLOTS]
    slot_lane = lax.broadcasted_iota(jnp.int32, (TILES, total), 1)
    spread = jnp.where(
        (slot_lane // SLOTS) == lax.broadcasted_iota(jnp.int32, (TILES, total), 0), 1.0, 0.0
    ).astype(BF16)
    wide = mm(cells_t, spread)
    own_slot = (
        lax.broadcasted_iota(jnp.int32, (SLOTS, total), 1) % SLOTS
        == lax.broadcasted_iota(jnp.int32, (SLOTS, total), 0)
    )
    cell_lat, cell_lon, frac_lat, frac_lon = [
        jnp.sum(
            jnp.where(own_slot, wide[f * SLOTS : (f + 1) * SLOTS], 0.0), axis=0, keepdims=True
        )
        for f in range(4)
    ]
    line = lax.broadcasted_iota(jnp.int32, (72, total), 0)
    kept = (line >= edge_ref[0]) & (line < edge_ref[1])
    lat_w[...] = jnp.where(
        kept, tap_weights(cell_lat, frac_lat, line.astype(F32) - 4.0), 0.0
    )
    column = lax.broadcasted_iota(jnp.int32, (128, total), 0).astype(F32)
    lon_w[...] = tap_weights(cell_lon, frac_lon, column).astype(BF16)
    line8 = lax.broadcasted_iota(jnp.int32, (8, total), 0)
    column = jnp.where(line8 < 4, line8 - 4, line8 + 124).astype(F32)
    side_w[...] = tap_weights(cell_lon, frac_lon, column).astype(BF16).astype(F32)
    blank = jnp.zeros((2, 128, 128), BF16)
    three[0:2, :, 256:384] = blank
    three[72:74, :, 0:128] = blank
    three[0:1, :, 128:256] = blank[:1]
    three[73:74, :, 128:256] = blank[:1]
    three_side[...] = jnp.zeros_like(three_side)
    acc_ref[...] = jnp.zeros_like(acc_ref)

    def weight_part(take, at):
        lhs = jnp.concatenate([jnp.concatenate(take(b), axis=1) for b in range(3)], axis=0)
        rhs = jnp.concatenate(
            [three[x:y].reshape((y - x) * 128, 384) for x, y in at], axis=0
        )
        acc_ref[...] += mm(lhs, rhs)

    def eight_lines(step, carry):
        start = pl.multiple_of(step * 8, 8)
        lat8 = lat_w[pl.ds(start, 8), :]
        acc = jnp.zeros((8 * 128, 128), F32)
        side = jnp.zeros((8 * 8, 128), F32)
        for k in range(total // 256):
            cols = slice(k * 256, (k + 1) * 256)
            lon = lon_w[:, cols].reshape(8, 16, 256)
            parts = []
            side_parts = []
            side_lon = side_w[:, cols]
            for i in range(8):
                one = jnp.broadcast_to(lat8[i : i + 1, cols], (16, 256)).astype(BF16)
                parts.append((lon * one[None]).reshape(128, 256))
                one8 = jnp.broadcast_to(
                    lat8[i : i + 1, cols].astype(BF16).astype(F32), (8, 256)
                )
                side_parts.append(side_lon * one8)
            rows = rows_ref[cols, :]
            acc = acc + mm(jnp.concatenate(parts, axis=0), rows)
            side = side + mm(jnp.concatenate(side_parts, axis=0).astype(BF16), rows)
        main = acc.astype(BF16).reshape(8, 128, 128)
        canvas_ref[pl.ds(start, 8), 0:128, :] = main
        for a in range(3):
            three[pl.ds(start + a, 8), :, a * 128 : (a + 1) * 128] = main
        side = side.reshape(8, 8, 128)
        canvas_ref[pl.ds(start, 8), 128:136, :] = side.astype(BF16)
        ends = acc.reshape(8, 128, 128)
        side = jnp.concatenate(
            [side, ends[:, 0:1], ends[:, 127:128], jnp.zeros((8, 6, 128), F32)], axis=1
        )
        for a in range(3):
            three_side[pl.ds(start + a, 8), :, a * 128 : (a + 1) * 128] = side
        rim_ref[pl.ds(start, 8), 0:8, :] = ends[:, 0:8].astype(BF16)
        rim_ref[pl.ds(start, 8), 8:16, :] = ends[:, 120:128].astype(BF16)
        rim_ref[pl.ds(start, 8), 16:24, :] = side[:, 0:8].astype(BF16)
        return carry

    lax.fori_loop(0, 9, eight_lines, 0)
    stores = [
        pltpu.make_async_copy(canvas_ref, canvas_hbm, store_sem.at[0]),
        pltpu.make_async_copy(rim_ref, rim_hbm, store_sem.at[1]),
        pltpu.make_async_copy(canvas_ref.at[1:5], up_hbm, store_sem.at[2]),
        pltpu.make_async_copy(canvas_ref.at[67:72], down_hbm, store_sem.at[3]),
    ]
    for copy in stores:
        copy.start()
    for copy in loads:
        copy.wait()
    for part in range(2):
        weight_part(
            lambda b: [feat_ref[b, part * 32 + i] for i in range(32)],
            ((5 + part * 32, 37 + part * 32),),
        )
    weight_part(lambda b: [feat_edge_ref[b, i] for i in range(10)], ((0, 5), (69, 74)))
    acc = acc_ref[...] + mm(
        feat_side_ref[...], three_side[...].reshape(1280, 384).astype(BF16)
    )
    for a in range(3):
        for b in range(3):
            at = (a * 3 + b) * 128
            sum_ref[at : at + 128, :] = acc[
                b * 128 : (b + 1) * 128, a * 128 : (a + 1) * 128
            ].astype(BF16)
    sum_ref[1152:, :] = jnp.zeros((2048 - 1152, 128), BF16)
    last = pltpu.make_async_copy(sum_ref, sum_hbm, store_sem.at[4])
    last.start()
    for copy in stores:
        copy.wait()
    last.wait()


def scatter(edge, incoming, feat, feat_edge, feat_side):
    vmem = pl.BlockSpec(memory_space=pltpu.VMEM)
    hbm = pl.BlockSpec(memory_space=pltpu.HBM)
    total = TILES * SLOTS
    return pl.pallas_call(
        scatter_kernel,
        out_shape=(
            jax.ShapeDtypeStruct((72, 136, 128), BF16),
            jax.ShapeDtypeStruct((72, 24, 128), BF16),
            jax.ShapeDtypeStruct((4, 136, 128), BF16),
            jax.ShapeDtypeStruct((5, 136, 128), BF16),
            jax.ShapeDtypeStruct((2048, 128), BF16),
        ),
        in_specs=[pl.BlockSpec(memory_space=pltpu.SMEM), vmem] + [hbm] * 3,
        out_specs=(hbm,) * 5,
        scratch_shapes=[
            pltpu.VMEM((total, 128), BF16),
            pltpu.VMEM((72, total), F32),
            pltpu.VMEM((128, total), BF16),
            pltpu.VMEM((8, total), F32),
            pltpu.VMEM((74, 128, 384), BF16),
            pltpu.VMEM((80, 16, 384), F32),
            pltpu.VMEM((384, 384), F32),
            pltpu.VMEM((3, 64, 128, 128), BF16),
            pltpu.VMEM((3, 10, 128, 128), BF16),
            pltpu.VMEM((384, 1280), BF16),
            pltpu.VMEM((72, 136, 128), BF16),
            pltpu.VMEM((72, 24, 128), BF16),
            pltpu.VMEM((2048, 128), BF16),
            pltpu.SemaphoreType.DMA((3,)),
            pltpu.SemaphoreType.DMA((5,)),
        ],
        compiler_params=pltpu.CompilerParams(vmem_limit_bytes=MOST_VMEM),
        cost_estimate=pl.CostEstimate(
            flops=8_200_000_000, bytes_accessed=12_000_000, transcendentals=500_000
        ),
        name="scatter",
    )(edge, incoming, feat, feat_edge, feat_side)


def sides_kernel(rim_ref, above_ref, below_ref, right_ref, left_ref):
    def tall(at, cols):
        block = rim_ref[3:69, at : at + 8, :].astype(F32)
        return jnp.concatenate(
            [
                block[0:5] + above_ref[:, cols : cols + 8, :].astype(F32),
                block[5:62],
                block[62:66] + below_ref[:, cols : cols + 8, :].astype(F32),
            ],
            axis=0,
        )

    head = tall(0, 0)
    last = tall(8, 120)
    side = tall(16, 128)
    blank = jnp.zeros((66, 4, 128), F32)
    right_ref[...] = jnp.concatenate([last[:, 7:8], side[:, 4:8], blank[:, :3]], axis=1).astype(
        BF16
    )
    left_ref[...] = jnp.concatenate([side[:, 1:4], head[:, 0:1], blank], axis=1).astype(BF16)


def sides(rim, above, below):
    vmem = pl.BlockSpec(memory_space=pltpu.VMEM)
    shape = jax.ShapeDtypeStruct((66, 8, 128), BF16)
    return pl.pallas_call(
        sides_kernel,
        out_shape=(shape, shape),
        in_specs=[vmem] * 3,
        out_specs=(vmem, vmem),
        cost_estimate=pl.CostEstimate(flops=1_000_000, bytes_accessed=1_000_000, transcendentals=0),
        compiler_params=pltpu.CompilerParams(vmem_limit_bytes=4 << 20),
        name="sides",
    )(rim, above, below)


def conv_kernel(canvas_ref, above_ref, below_ref, left_ref, right_ref, weight_ref, out_ref, grid):
    @pl.when(pl.program_id(0) == 0)
    def _():
        grid[5:62, 0:128, :] = canvas_ref[8:65, 0:128, :]
        grid[0:5, 0:128, :] = (
            canvas_ref[3:8, 0:128, :].astype(F32) + above_ref[:, 0:128, :].astype(F32)
        ).astype(BF16)
        grid[62:66, 0:128, :] = (
            canvas_ref[65:69, 0:128, :].astype(F32) + below_ref[:, 0:128, :].astype(F32)
        ).astype(BF16)
        left = left_ref[...].astype(F32)
        right = right_ref[...].astype(F32)
        blank = jnp.zeros((66, 14, 128), F32)
        grid[:, 0:16, :] = (
            grid[:, 0:16, :].astype(F32)
            + jnp.concatenate([left[:, 1:5], blank[:, :12]], axis=1)
        ).astype(BF16)
        grid[:, 112:128, :] = (
            grid[:, 112:128, :].astype(F32)
            + jnp.concatenate([blank[:, :13], right[:, 0:3]], axis=1)
        ).astype(BF16)
        side = canvas_ref[3:69, 128:136, :].astype(F32)
        side = jnp.concatenate(
            [
                side[0:5] + above_ref[:, 128:136, :].astype(F32),
                side[5:62],
                side[62:66] + below_ref[:, 128:136, :].astype(F32),
            ],
            axis=0,
        )
        grid[:, 128:144, :] = jnp.concatenate(
            [side[:, 4:5] + right[:, 3:4], blank, side[:, 3:4] + left[:, 0:1]], axis=1
        ).astype(BF16)

    start = pl.program_id(0) * 8
    taps = jnp.concatenate(
        [grid[pl.ds(start + 2 - a, 8)].reshape(8 * 144, 128) for a in range(3)], axis=1
    )
    weight = jnp.concatenate([weight_ref[a].reshape(384, 128) for a in range(3)], axis=1)
    every = nt(taps, weight).reshape(8, 144, 384)
    for i in range(8):
        one = every[i]
        got = (
            one[:, 128:256]
            + pltpu.roll(one[:, 0:128], 143, 0)
            + pltpu.roll(one[:, 256:384], 1, 0)
        )
        out_ref[i] = got[0:128].astype(BF16)


def conv(canvas, above, below, left, right, weight):
    def whole(x):
        return pl.BlockSpec(
            x.shape, lambda i: (0,) * x.ndim, pipeline_mode=pl.Buffered(1)
        )

    args = (canvas, above, below, left, right, weight)
    return pl.pallas_call(
        conv_kernel,
        grid=(8,),
        out_shape=jax.ShapeDtypeStruct((64, 128, 128), BF16),
        in_specs=[whole(x) for x in args],
        out_specs=pl.BlockSpec((8, 128, 128), lambda i: (i, 0, 0)),
        scratch_shapes=[pltpu.VMEM((66, 144, 128), BF16)],
        compiler_params=pltpu.CompilerParams(vmem_limit_bytes=MOST_VMEM),
        cost_estimate=pl.CostEstimate(
            flops=2_700_000_000, bytes_accessed=4_500_000, transcendentals=0
        ),
        name="conv",
    )(*args)


def gather_kernel(in_ref, out_ref):
    mine = jnp.sum(in_ref[...].astype(F32), axis=0)
    out_ref[...] = jnp.broadcast_to(mine.astype(BF16)[None], out_ref.shape)


def share(got):
    vmem = pl.BlockSpec(memory_space=pltpu.VMEM)
    return pl.pallas_call(
        gather_kernel,
        out_shape=jax.ShapeDtypeStruct(got.shape, BF16),
        in_specs=[vmem],
        out_specs=vmem,
        cost_estimate=pl.CostEstimate(flops=300_000, bytes_accessed=1_000_000, transcendentals=0),
        compiler_params=pltpu.CompilerParams(vmem_limit_bytes=3 << 20),
        name="share",
    )(got)


def finish_kernel(in_ref, out_ref):
    out_ref[...] = in_ref[...].reshape(384, 128).astype(F32)


def finish(every):
    return pl.pallas_call(
        finish_kernel,
        grid=(3,),
        out_shape=jax.ShapeDtypeStruct((1152, 128), F32),
        in_specs=[pl.BlockSpec((24, 16, 128), lambda i: (i, 0, 0))],
        out_specs=pl.BlockSpec((384, 128), lambda i: (i, 0)),
        compiler_params=pltpu.CompilerParams(vmem_limit_bytes=2 << 20),
        cost_estimate=pl.CostEstimate(flops=0, bytes_accessed=900_000, transcendentals=0),
        name="finish",
    )(every)


def both_ways(forth, back, axis, closed):
    count = lax.axis_size(axis)
    ends = count if closed else count - 1
    return (
        lax.ppermute(forth, axis, [(i, (i + 1) % count) for i in range(ends)]),
        lax.ppermute(back, axis, [((i + 1) % count, i) for i in range(ends)]),
    )


def shards(grad_rows, owner, lat_offset, lon_offset, position, live_count, features, conv_weight):
    count = grad_rows.shape[0]
    lat_index = lax.axis_index("lat")
    edge = jnp.stack(
        [
            jnp.where(lat_index == 0, 4, 0),
            jnp.where(lat_index == lax.axis_size("lat") - 1, 68, 72),
        ]
    ).astype(jnp.int32)
    outgoing = pack(
        live_count,
        owner.reshape(1, count),
        lat_offset.reshape(1, count),
        lon_offset.reshape(1, count),
        position.T,
        grad_rows,
    )
    incoming = lax.all_to_all(outgoing, AXES, 0, 0, tiled=True)
    above, below = both_ways(features[59:64], features[0:5], "lat", False)
    last, head = [
        jnp.concatenate([x[:, c : c + 8] for x in (above, features, below)], axis=0)
        for c in (120, 0)
    ]
    left, right = both_ways(last, head, "lon", True)
    feat = prep(features)
    feat_edge, feat_side = prep_edge(head, last, above, below, left, right)
    canvas, rim, up, down, part = scatter(edge, incoming, feat, feat_edge, feat_side)
    grid_above, grid_below = both_ways(down, up, "lat", False)
    part, grid_above, grid_below = lax.optimization_barrier((part, grid_above, grid_below))
    got = lax.all_to_all(part.reshape(TILES, 16, 128), AXES, 0, 0, tiled=True)
    send_right, send_left = sides(rim, grid_above, grid_below)
    from_left, from_right = both_ways(send_right, send_left, "lon", True)
    got, from_left, from_right = lax.optimization_barrier((got, from_left, from_right))
    every = lax.all_to_all(share(got), AXES, 0, 0, tiled=True)
    input_grad = conv(canvas, grid_above, grid_below, from_left, from_right, conv_weight)
    weight_grad = finish(every)
    return input_grad, weight_grad.reshape(3, 3, 128, 128)


def solution(mesh):
    placed = (
        P(("lat", "lon"), None),
        P(("lat", "lon"), None),
        P(("lat", "lon")),
        P(("lat", "lon")),
        P(("lat", "lon"), None),
        P(("lat", "lon")),
        P("lat", "lon", None),
        P(),
    )
    return jax.shard_map(
        shards, mesh=mesh, in_specs=placed, out_specs=(P("lat", "lon", None), P()), check_vma=False
    )
```

```python
import functools

import jax
import jax.numpy as jnp
import numpy as np
from jax import lax
from jax.experimental import pallas as pl
from jax.experimental.pallas import tpu as pltpu
from jax.sharding import PartitionSpec as P

AXES = ("lat", "lon")
BF16 = jnp.bfloat16
F32 = jnp.float32
SLOTS = 16
CHUNK = 24
TILES = 128
MOST_VMEM = 62_600_000
GAUSS = 2.0 * 1.5 * 1.5


def nt(lhs, rhs):
    return lax.dot_general(lhs, rhs, (((1,), (1,)), ((), ())), preferred_element_type=F32)


def mm(lhs, rhs):
    return jnp.dot(lhs, rhs, preferred_element_type=F32)


def pack_kernel(live_ref, own_ref, lat_ref, lon_ref, pos_ref, rows_ref, out_ref):
    count = own_ref.shape[1]
    lane = lax.broadcasted_iota(jnp.int32, (1, count), 1)
    own = jnp.where(lane < live_ref[0], own_ref[...], TILES)
    tile_line = lax.broadcasted_iota(jnp.int32, (TILES, count), 0)
    named = jnp.where(own == tile_line, 1.0, 0.0)
    named_b = named.astype(BF16)
    block = 256
    upper = jnp.where(
        lax.broadcasted_iota(jnp.int32, (block, block), 0)
        < lax.broadcasted_iota(jnp.int32, (block, block), 1),
        1.0,
        0.0,
    ).astype(BF16)
    ones = jnp.ones((block, block), BF16)
    before = jnp.zeros((TILES, block), F32)
    ranks = []
    for b in range(count // block):
        part = named_b[:, b * block : (b + 1) * block]
        earlier = mm(part, upper) + before
        ranks.append(
            jnp.sum(earlier * named[:, b * block : (b + 1) * block], axis=0, keepdims=True)
        )
        before = before + mm(part, ones)
    rank = jnp.concatenate(ranks, axis=1).astype(jnp.int32)
    slot = own * SLOTS + rank
    rows = rows_ref[...]
    step = 1024
    for q in range(TILES * SLOTS // step):
        line = lax.broadcasted_iota(jnp.int32, (step, count), 0) + q * step
        picked = jnp.where(slot == line, 1.0, 0.0).astype(BF16)
        moved = mm(picked, rows).astype(BF16)
        out_ref[q * step // SLOTS : (q + 1) * step // SLOTS, 0:SLOTS, :] = moved.reshape(
            step // SLOTS, SLOTS, 128
        )
    at_rank = lax.broadcasted_iota(jnp.int32, (SLOTS, count), 0) == rank
    pos = pos_ref[...].astype(F32)
    fields = (
        lat_ref[...].astype(F32),
        lon_ref[...].astype(F32),
        pos[0:1, :],
        pos[1:2, :],
    )
    spots = [jnp.where(at_rank, f, 0.0) for f in fields]
    spots.append(jnp.zeros((128 - SLOTS * len(fields), count), F32))
    cells = nt(named_b, jnp.concatenate(spots, axis=0).astype(BF16)).astype(BF16)
    out_ref[:, SLOTS:CHUNK, :] = jnp.broadcast_to(
        cells.astype(F32)[:, None, :], (TILES, CHUNK - SLOTS, 128)
    ).astype(BF16)


def pack(live, own, lat, lon, pos, rows):
    vmem = pl.BlockSpec(memory_space=pltpu.VMEM)
    return pl.pallas_call(
        pack_kernel,
        out_shape=jax.ShapeDtypeStruct((TILES, CHUNK, 128), BF16),
        in_specs=[pl.BlockSpec(memory_space=pltpu.SMEM)] + [vmem] * 5,
        out_specs=vmem,
        cost_estimate=pl.CostEstimate(flops=700_000_000, bytes_accessed=1_500_000, transcendentals=0),
        name="pack",
    )(live, own, lat, lon, pos, rows)


def tap_weights(cell, frac, offset):
    tap = offset - cell + 3.0
    dist = tap - 3.0 - frac
    weight = jnp.exp(-(dist * dist) / GAUSS)
    return jnp.where((tap >= 0.0) & (tap <= 7.0), weight, 0.0)


def picks():
    eye = np.eye(128, dtype=np.float32)
    shift = np.concatenate([np.eye(128, k=1), np.eye(128, k=-1)], axis=1)
    wanted = (
        {0: 3, 1: 4, 2: 5, 3: 6, 4: 31, 5: 8, 6: 9, 7: 10, 8: 7},
        {0: 4, 1: 5, 2: 6, 3: 7, 4: 8, 5: 9, 6: 10, 7: 11},
        {0: 5, 1: 6, 2: 7, 3: 16, 4: 9, 5: 10, 6: 11, 7: 12, 9: 8},
    )
    side = np.zeros((8, 32, 3, 8, 16), np.float32)
    for b in range(3):
        for target, source in wanted[b].items():
            for line in range(8):
                side[line, source, b, line, target] = 1.0
    return [jnp.asarray(x, BF16) for x in (eye, shift, side.reshape(256, 384))]


def prep_kernel(eye_ref, shift_ref, feat_ref, out_ref):
    eye = eye_ref[...]
    turned = jnp.concatenate([nt(eye, feat_ref[i]).astype(BF16) for i in range(8)], axis=0)
    moved = mm(turned, shift_ref[...]).astype(BF16)
    out_ref[0] = moved[:, 0:128].reshape(8, 128, 128)
    out_ref[1] = turned.reshape(8, 128, 128)
    out_ref[2] = moved[:, 128:256].reshape(8, 128, 128)


def prep(eye, shift, features):
    return pl.pallas_call(
        prep_kernel,
        grid=(8,),
        out_shape=jax.ShapeDtypeStruct((3, 64, 128, 128), BF16),
        in_specs=[
            pl.BlockSpec((128, 128), lambda i: (0, 0)),
            pl.BlockSpec((128, 256), lambda i: (0, 0)),
            pl.BlockSpec((8, 128, 128), lambda i: (i, 0, 0)),
        ],
        out_specs=pl.BlockSpec((3, 8, 128, 128), lambda i: (0, i, 0, 0)),
        cost_estimate=pl.CostEstimate(
            flops=2_200_000_000, bytes_accessed=8_000_000, transcendentals=0
        ),
        name="prep",
    )(eye, shift, features)


def prep_side_kernel(eye_ref, pick_ref, left_ref, right_ref, head_ref, last_ref, side_ref, cells):
    for at, ref in enumerate((left_ref, right_ref, head_ref, last_ref)):
        cells[:, at * 8 : at * 8 + 8, :] = ref[...]
    turned = nt(eye_ref[...], cells[...].reshape(2048, 128)).astype(BF16)
    for g in range(8):
        moved = mm(turned[:, g * 256 : (g + 1) * 256], pick_ref[...]).astype(BF16)
        for b in range(3):
            side_ref[b * 128 : (b + 1) * 128, g * 128 : (g + 1) * 128] = moved[
                :, b * 128 : (b + 1) * 128
            ]


def prep_side(eye, pick, left, right, head, last):
    vmem = pl.BlockSpec(memory_space=pltpu.VMEM)
    return pl.pallas_call(
        prep_side_kernel,
        out_shape=jax.ShapeDtypeStruct((384, 1024), BF16),
        in_specs=[vmem] * 6,
        out_specs=vmem,
        scratch_shapes=[pltpu.VMEM((64, 32, 128), BF16)],
        cost_estimate=pl.CostEstimate(
            flops=300_000_000, bytes_accessed=1_500_000, transcendentals=0
        ),
        name="prep_side",
    )(eye, pick, left, right, head, last)


def scatter_kernel(
    edge_ref,
    in_ref,
    canvas_hbm,
    side_hbm,
    rim_hbm,
    up_hbm,
    down_hbm,
    rows_ref,
    lat_w,
    lon_w,
    side_w,
    canvas_ref,
    side_ref,
    rim_ref,
    block_sem,
    store_sem,
):
    def block_store(step):
        lines = pl.ds(pl.multiple_of(step * 8, 8), 8)
        return pltpu.make_async_copy(
            canvas_ref.at[lines], canvas_hbm.at[lines], block_sem.at[step]
        )

    total = TILES * SLOTS
    rows_ref[...] = in_ref[:, 0:SLOTS, :].reshape(total, 128)
    tail = in_ref[:, SLOTS:CHUNK, :].reshape(TILES * (CHUNK - SLOTS), 128)
    first = jnp.where(
        lax.broadcasted_iota(jnp.int32, (TILES, tail.shape[0]), 1)
        == (CHUNK - SLOTS) * lax.broadcasted_iota(jnp.int32, (TILES, tail.shape[0]), 0),
        1.0,
        0.0,
    ).astype(BF16)
    cells = mm(first, tail)
    cells_t = cells.T.astype(BF16)[: 4 * SLOTS]
    slot_lane = lax.broadcasted_iota(jnp.int32, (TILES, total), 1)
    spread = jnp.where(
        (slot_lane // SLOTS) == lax.broadcasted_iota(jnp.int32, (TILES, total), 0), 1.0, 0.0
    ).astype(BF16)
    wide = mm(cells_t, spread)
    own_slot = (
        lax.broadcasted_iota(jnp.int32, (SLOTS, total), 1) % SLOTS
        == lax.broadcasted_iota(jnp.int32, (SLOTS, total), 0)
    )
    cell_lat, cell_lon, frac_lat, frac_lon = [
        jnp.sum(
            jnp.where(own_slot, wide[f * SLOTS : (f + 1) * SLOTS], 0.0), axis=0, keepdims=True
        )
        for f in range(4)
    ]
    line = lax.broadcasted_iota(jnp.int32, (72, total), 0)
    kept = (line >= edge_ref[0]) & (line < edge_ref[1])
    lat_w[...] = jnp.where(
        kept, tap_weights(cell_lat, frac_lat, line.astype(F32) - 4.0), 0.0
    )
    column = lax.broadcasted_iota(jnp.int32, (128, total), 0).astype(F32)
    lon_w[...] = tap_weights(cell_lon, frac_lon, column).astype(BF16)
    line8 = lax.broadcasted_iota(jnp.int32, (8, total), 0)
    column = jnp.where(line8 < 4, line8 - 4, line8 + 124).astype(F32)
    side_w[...] = tap_weights(cell_lon, frac_lon, column).astype(BF16).astype(F32)
    def eight_lines(step, carry):
        start = pl.multiple_of(step * 8, 8)
        lat8 = lat_w[pl.ds(start, 8), :]
        acc = jnp.zeros((8 * 128, 128), F32)
        side = jnp.zeros((8 * 8, 128), F32)
        for k in range(total // 256):
            cols = slice(k * 256, (k + 1) * 256)
            lon = lon_w[:, cols].reshape(8, 16, 256)
            parts = []
            side_parts = []
            side_lon = side_w[:, cols]
            for i in range(8):
                one = jnp.broadcast_to(lat8[i : i + 1, cols], (16, 256)).astype(BF16)
                parts.append((lon * one[None]).reshape(128, 256))
                one8 = jnp.broadcast_to(
                    lat8[i : i + 1, cols].astype(BF16).astype(F32), (8, 256)
                )
                side_parts.append(side_lon * one8)
            rows = rows_ref[cols, :]
            acc = acc + mm(jnp.concatenate(parts, axis=0), rows)
            side = side + mm(jnp.concatenate(side_parts, axis=0).astype(BF16), rows)
        ends = acc.reshape(8, 128, 128)
        side = side.reshape(8, 8, 128)
        lines = pl.ds(start, 8)
        canvas_ref[lines, 0:128, :] = ends.astype(BF16)
        canvas_ref[lines, 128:136, :] = side.astype(BF16)
        block_store(step).start()
        side_ref[lines] = jnp.concatenate(
            [side, ends[:, 0:1], ends[:, 127:128], jnp.zeros((8, 6, 128), F32)], axis=1
        ).astype(BF16)
        rim_ref[lines, 0:8, :] = ends[:, 0:8].astype(BF16)
        rim_ref[lines, 8:16, :] = ends[:, 120:128].astype(BF16)
        rim_ref[lines, 16:24, :] = side.astype(BF16)
        return carry

    lax.fori_loop(0, 9, eight_lines, 0)
    stores = [
        pltpu.make_async_copy(canvas_ref.at[1:5], up_hbm, store_sem.at[0]),
        pltpu.make_async_copy(canvas_ref.at[67:72], down_hbm, store_sem.at[1]),
        pltpu.make_async_copy(side_ref, side_hbm, store_sem.at[2]),
        pltpu.make_async_copy(rim_ref, rim_hbm, store_sem.at[3]),
    ]
    for copy in stores:
        copy.start()
    for step in range(9):
        block_store(step).wait()
    for copy in stores:
        copy.wait()


def scatter(edge, incoming):
    vmem = pl.BlockSpec(memory_space=pltpu.VMEM)
    hbm = pl.BlockSpec(memory_space=pltpu.HBM)
    total = TILES * SLOTS
    return pl.pallas_call(
        scatter_kernel,
        out_shape=(
            jax.ShapeDtypeStruct((72, 136, 128), BF16),
            jax.ShapeDtypeStruct((72, 16, 128), BF16),
            jax.ShapeDtypeStruct((72, 24, 128), BF16),
            jax.ShapeDtypeStruct((4, 136, 128), BF16),
            jax.ShapeDtypeStruct((5, 136, 128), BF16),
        ),
        in_specs=[pl.BlockSpec(memory_space=pltpu.SMEM), vmem],
        out_specs=(hbm,) * 5,
        scratch_shapes=[
            pltpu.VMEM((total, 128), BF16),
            pltpu.VMEM((72, total), F32),
            pltpu.VMEM((128, total), BF16),
            pltpu.VMEM((8, total), F32),
            pltpu.VMEM((72, 136, 128), BF16),
            pltpu.VMEM((72, 16, 128), BF16),
            pltpu.VMEM((72, 24, 128), BF16),
            pltpu.SemaphoreType.DMA((9,)),
            pltpu.SemaphoreType.DMA((4,)),
        ],
        compiler_params=pltpu.CompilerParams(vmem_limit_bytes=62_000_000),
        cost_estimate=pl.CostEstimate(
            flops=5_200_000_000, bytes_accessed=4_000_000, transcendentals=500_000
        ),
        name="scatter",
    )(edge, incoming)


def own_grad_kernel(
    canvas_hbm, side_hbm, feat_hbm, feat_side_hbm, acc_ref, canvas, side, feat, feat_side, sem
):
    step = 16
    loads = [
        pltpu.make_async_copy(canvas_hbm.at[3:69], canvas, sem.at[4]),
        *[
            pltpu.make_async_copy(
                feat_hbm.at[:, k * step : (k + 1) * step],
                feat.at[:, k * step : (k + 1) * step],
                sem.at[k],
            )
            for k in range(4)
        ],
        pltpu.make_async_copy(side_hbm.at[3:69], side, sem.at[5]),
        pltpu.make_async_copy(feat_side_hbm, feat_side, sem.at[6]),
    ]
    for copy in loads:
        copy.start()
    loads[0].wait()
    total = jnp.zeros((384, 384), F32)
    for k in range(4):
        loads[1 + k].wait()
        lines = range(k * step, (k + 1) * step)
        lhs = jnp.concatenate(
            [jnp.concatenate([feat[b, i] for i in lines], axis=1) for b in range(3)], axis=0
        )
        rhs = jnp.concatenate(
            [
                canvas[k * step + 2 - a : (k + 1) * step + 2 - a, 0:128, :].reshape(
                    step * 128, 128
                )
                for a in range(3)
            ],
            axis=1,
        )
        total = total + mm(lhs, rhs)
    loads[5].wait()
    loads[6].wait()
    rhs = jnp.concatenate(
        [side[2 - a : 66 - a].reshape(1024, 128) for a in range(3)], axis=1
    )
    acc_ref[...] = total + mm(feat_side[...], rhs)


def own_grad(canvas, side, feat, feat_side):
    hbm = pl.BlockSpec(memory_space=pltpu.HBM)
    return pl.pallas_call(
        own_grad_kernel,
        out_shape=jax.ShapeDtypeStruct((384, 384), F32),
        in_specs=[hbm] * 4,
        out_specs=pl.BlockSpec(memory_space=pltpu.VMEM),
        scratch_shapes=[
            pltpu.VMEM((66, 136, 128), BF16),
            pltpu.VMEM((66, 16, 128), BF16),
            pltpu.VMEM((3, 64, 128, 128), BF16),
            pltpu.VMEM((384, 1024), BF16),
            pltpu.SemaphoreType.DMA((7,)),
        ],
        cost_estimate=pl.CostEstimate(
            flops=2_800_000_000, bytes_accessed=10_000_000, transcendentals=0
        ),
        compiler_params=pltpu.CompilerParams(vmem_limit_bytes=62_000_000),
        name="own_grad",
    )(canvas, side, feat, feat_side)


def halo_grad_kernel(
    acc_ref, above_ref, below_ref, feat_hbm, feat_side_ref, sum_hbm, feat, sums, sem
):
    top = pltpu.make_async_copy(feat_hbm.at[:, 0:5], feat.at[:, 0:5], sem.at[0])
    bottom = pltpu.make_async_copy(feat_hbm.at[:, 60:64], feat.at[:, 5:9], sem.at[1])
    top.start()
    bottom.start()
    sums[1152:, :] = jnp.zeros((2048 - 1152, 128), BF16)

    def beside(ref, count):
        eight = ref[:, 128:136, :].astype(F32)
        first = ref[:, 0:8, :].astype(F32)
        last = ref[:, 120:128, :].astype(F32)
        return jnp.concatenate(
            [eight, first[:, 0:1], last[:, 7:8], jnp.zeros((count, 6, 128), F32)], axis=1
        ).astype(BF16)

    def lines(count, width):
        return jnp.zeros((count, width, 128), BF16)

    above = jnp.concatenate([above_ref[:, 0:128, :], lines(2, 128)], axis=0)
    below = jnp.concatenate([lines(2, 128), below_ref[:, 0:128, :]], axis=0)
    rhs = jnp.concatenate(
        [
            jnp.concatenate([above[2 - a : 7 - a], below[2 - a : 6 - a]], axis=0).reshape(
                9 * 128, 128
            )
            for a in range(3)
        ],
        axis=1,
    )
    above = jnp.concatenate([beside(above_ref, 5), lines(5, 16)], axis=0)
    below = jnp.concatenate([lines(6, 16), beside(below_ref, 4)], axis=0)
    rhs_side = jnp.concatenate(
        [
            jnp.concatenate([above[2 - a : 10 - a], below[2 - a : 10 - a]], axis=0).reshape(
                256, 128
            )
            for a in range(3)
        ],
        axis=1,
    )
    lhs_side = jnp.concatenate([feat_side_ref[:, 0:128], feat_side_ref[:, 896:1024]], axis=1)
    total = acc_ref[...] + mm(lhs_side, rhs_side)
    top.wait()
    bottom.wait()
    lhs = jnp.concatenate(
        [jnp.concatenate([feat[b, i] for i in range(9)], axis=1) for b in range(3)], axis=0
    )
    total = total + mm(lhs, rhs)
    for a in range(3):
        for b in range(3):
            at = (a * 3 + b) * 128
            sums[at : at + 128, :] = total[
                b * 128 : (b + 1) * 128, a * 128 : (a + 1) * 128
            ].astype(BF16)
    store = pltpu.make_async_copy(sums, sum_hbm, sem.at[2])
    store.start()
    store.wait()


def halo_grad(acc, above, below, feat, feat_side):
    vmem = pl.BlockSpec(memory_space=pltpu.VMEM)
    hbm = pl.BlockSpec(memory_space=pltpu.HBM)
    return pl.pallas_call(
        halo_grad_kernel,
        out_shape=jax.ShapeDtypeStruct((2048, 128), BF16),
        in_specs=[vmem, vmem, vmem, hbm, vmem],
        out_specs=hbm,
        scratch_shapes=[
            pltpu.VMEM((3, 9, 128, 128), BF16),
            pltpu.VMEM((2048, 128), BF16),
            pltpu.SemaphoreType.DMA((3,)),
        ],
        cost_estimate=pl.CostEstimate(
            flops=420_000_000, bytes_accessed=3_500_000, transcendentals=0
        ),
        compiler_params=pltpu.CompilerParams(vmem_limit_bytes=58_000_000),
        name="halo_grad",
    )(acc, above, below, feat, feat_side)


def sides_kernel(rim_ref, above_ref, below_ref, right_ref, left_ref):
    def tall(at, cols):
        block = rim_ref[3:69, at : at + 8, :].astype(F32)
        return jnp.concatenate(
            [
                block[0:5] + above_ref[:, cols : cols + 8, :].astype(F32),
                block[5:62],
                block[62:66] + below_ref[:, cols : cols + 8, :].astype(F32),
            ],
            axis=0,
        )

    head = tall(0, 0)
    last = tall(8, 120)
    side = tall(16, 128)
    blank = jnp.zeros((66, 4, 128), F32)
    right_ref[...] = jnp.concatenate([last[:, 7:8], side[:, 4:8], blank[:, :3]], axis=1).astype(
        BF16
    )
    left_ref[...] = jnp.concatenate([side[:, 1:4], head[:, 0:1], blank], axis=1).astype(BF16)


def sides(rim, above, below):
    vmem = pl.BlockSpec(memory_space=pltpu.VMEM)
    shape = jax.ShapeDtypeStruct((66, 8, 128), BF16)
    return pl.pallas_call(
        sides_kernel,
        out_shape=(shape, shape),
        in_specs=[vmem] * 3,
        out_specs=(vmem, vmem),
        cost_estimate=pl.CostEstimate(flops=1_000_000, bytes_accessed=1_000_000, transcendentals=0),
        compiler_params=pltpu.CompilerParams(vmem_limit_bytes=4 << 20),
        name="sides",
    )(rim, above, below)


def conv_kernel(canvas_ref, above_ref, below_ref, left_ref, right_ref, weight_ref, out_ref, grid):
    @pl.when(pl.program_id(0) == 0)
    def _():
        grid[5:62, 0:128, :] = canvas_ref[8:65, 0:128, :]
        grid[0:5, 0:128, :] = (
            canvas_ref[3:8, 0:128, :].astype(F32) + above_ref[:, 0:128, :].astype(F32)
        ).astype(BF16)
        grid[62:66, 0:128, :] = (
            canvas_ref[65:69, 0:128, :].astype(F32) + below_ref[:, 0:128, :].astype(F32)
        ).astype(BF16)
        left = left_ref[...].astype(F32)
        right = right_ref[...].astype(F32)
        blank = jnp.zeros((66, 14, 128), F32)
        grid[:, 0:16, :] = (
            grid[:, 0:16, :].astype(F32)
            + jnp.concatenate([left[:, 1:5], blank[:, :12]], axis=1)
        ).astype(BF16)
        grid[:, 112:128, :] = (
            grid[:, 112:128, :].astype(F32)
            + jnp.concatenate([blank[:, :13], right[:, 0:3]], axis=1)
        ).astype(BF16)
        side = canvas_ref[3:69, 128:136, :].astype(F32)
        side = jnp.concatenate(
            [
                side[0:5] + above_ref[:, 128:136, :].astype(F32),
                side[5:62],
                side[62:66] + below_ref[:, 128:136, :].astype(F32),
            ],
            axis=0,
        )
        grid[:, 128:144, :] = jnp.concatenate(
            [side[:, 4:5] + right[:, 3:4], blank, side[:, 3:4] + left[:, 0:1]], axis=1
        ).astype(BF16)

    start = pl.program_id(0) * 8
    taps = jnp.concatenate(
        [grid[pl.ds(start + 2 - a, 8)].reshape(8 * 144, 128) for a in range(3)], axis=1
    )
    weight = jnp.concatenate([weight_ref[a].reshape(384, 128) for a in range(3)], axis=1)
    every = nt(taps, weight).reshape(8, 144, 384)
    for i in range(8):
        one = every[i]
        got = (
            one[:, 128:256]
            + pltpu.roll(one[:, 0:128], 143, 0)
            + pltpu.roll(one[:, 256:384], 1, 0)
        )
        out_ref[i] = got[0:128].astype(BF16)


def conv(canvas, above, below, left, right, weight):
    def whole(x):
        return pl.BlockSpec(
            x.shape, lambda i: (0,) * x.ndim, pipeline_mode=pl.Buffered(1)
        )

    args = (canvas, above, below, left, right, weight)
    return pl.pallas_call(
        conv_kernel,
        grid=(8,),
        out_shape=jax.ShapeDtypeStruct((64, 128, 128), BF16),
        in_specs=[whole(x) for x in args],
        out_specs=pl.BlockSpec((8, 128, 128), lambda i: (i, 0, 0)),
        scratch_shapes=[pltpu.VMEM((66, 144, 128), BF16)],
        compiler_params=pltpu.CompilerParams(vmem_limit_bytes=MOST_VMEM),
        cost_estimate=pl.CostEstimate(
            flops=2_700_000_000, bytes_accessed=4_500_000, transcendentals=0
        ),
        name="conv",
    )(*args)


def gather_kernel(in_ref, out_ref):
    mine = jnp.sum(in_ref[...].astype(F32), axis=0)
    out_ref[...] = jnp.broadcast_to(mine.astype(BF16)[None], out_ref.shape)


def share(got):
    vmem = pl.BlockSpec(memory_space=pltpu.VMEM)
    return pl.pallas_call(
        gather_kernel,
        out_shape=jax.ShapeDtypeStruct(got.shape, BF16),
        in_specs=[vmem],
        out_specs=vmem,
        cost_estimate=pl.CostEstimate(flops=300_000, bytes_accessed=1_000_000, transcendentals=0),
        compiler_params=pltpu.CompilerParams(vmem_limit_bytes=3 << 20),
        name="share",
    )(got)


def finish_kernel(in_ref, out_ref):
    out_ref[...] = in_ref[...].reshape(384, 128).astype(F32)


def finish(every):
    return pl.pallas_call(
        finish_kernel,
        grid=(3,),
        out_shape=jax.ShapeDtypeStruct((1152, 128), F32),
        in_specs=[pl.BlockSpec((24, 16, 128), lambda i: (i, 0, 0))],
        out_specs=pl.BlockSpec((384, 128), lambda i: (i, 0)),
        compiler_params=pltpu.CompilerParams(vmem_limit_bytes=2 << 20),
        cost_estimate=pl.CostEstimate(flops=0, bytes_accessed=900_000, transcendentals=0),
        name="finish",
    )(every)


def both_ways(forth, back, axis, closed):
    count = lax.axis_size(axis)
    ends = count if closed else count - 1
    return (
        lax.ppermute(forth, axis, [(i, (i + 1) % count) for i in range(ends)]),
        lax.ppermute(back, axis, [((i + 1) % count, i) for i in range(ends)]),
    )


def shards(grad_rows, owner, lat_offset, lon_offset, position, live_count, features, conv_weight):
    count = grad_rows.shape[0]
    lat_index = lax.axis_index("lat")
    edge = jnp.stack(
        [
            jnp.where(lat_index == 0, 4, 0),
            jnp.where(lat_index == lax.axis_size("lat") - 1, 68, 72),
        ]
    ).astype(jnp.int32)
    outgoing = pack(
        live_count,
        owner.reshape(1, count),
        lat_offset.reshape(1, count),
        lon_offset.reshape(1, count),
        position.T,
        grad_rows,
    )
    incoming = lax.all_to_all(outgoing, AXES, 0, 0, tiled=True)
    eye, shift, pick = picks()
    last, head = features[:, 120:128], features[:, 0:8]
    left, right = both_ways(last, head, "lon", True)
    feat = prep(eye, shift, features)
    feat_side = prep_side(eye, pick, left, right, head, last)
    canvas, side, rim, up, down = scatter(edge, incoming)
    grid_above, grid_below = both_ways(down, up, "lat", False)
    acc = own_grad(canvas, side, feat, feat_side)
    part = halo_grad(acc, grid_above, grid_below, feat, feat_side)
    got = lax.all_to_all(part.reshape(TILES, 16, 128), AXES, 0, 0, tiled=True)
    send_right, send_left = sides(rim, grid_above, grid_below)
    from_left, from_right = both_ways(send_right, send_left, "lon", True)
    got, from_left, from_right = lax.optimization_barrier((got, from_left, from_right))
    every = lax.all_to_all(share(got), AXES, 0, 0, tiled=True)
    input_grad = conv(canvas, grid_above, grid_below, from_left, from_right, conv_weight)
    weight_grad = finish(every)
    return input_grad, weight_grad.reshape(3, 3, 128, 128)


def solution(mesh):
    placed = (
        P(("lat", "lon"), None),
        P(("lat", "lon"), None),
        P(("lat", "lon")),
        P(("lat", "lon")),
        P(("lat", "lon"), None),
        P(("lat", "lon")),
        P("lat", "lon", None),
        P(),
    )
    return jax.shard_map(
        shards, mesh=mesh, in_specs=placed, out_specs=(P("lat", "lon", None), P()), check_vma=False
    )
```

```python
import functools

import jax
import jax.numpy as jnp
import numpy as np
from jax import lax
from jax.experimental import pallas as pl
from jax.experimental.pallas import tpu as pltpu
from jax.sharding import PartitionSpec as P

AXES = ("lat", "lon")
BF16 = jnp.bfloat16
F32 = jnp.float32
SLOTS = 16
CHUNK = 24
TILES = 128
GAUSS = 2.0 * 1.5 * 1.5


def nt(lhs, rhs):
    return lax.dot_general(lhs, rhs, (((1,), (1,)), ((), ())), preferred_element_type=F32)


def mm(lhs, rhs):
    return jnp.dot(lhs, rhs, preferred_element_type=F32)


def pack_kernel(live_ref, own_ref, lat_ref, lon_ref, pos_ref, rows_ref, out_ref):
    count = own_ref.shape[1]
    lane = lax.broadcasted_iota(jnp.int32, (1, count), 1)
    own = jnp.where(lane < live_ref[0], own_ref[...], TILES)
    tile_line = lax.broadcasted_iota(jnp.int32, (TILES, count), 0)
    named = jnp.where(own == tile_line, 1.0, 0.0)
    named_b = named.astype(BF16)
    block = 256
    upper = jnp.where(
        lax.broadcasted_iota(jnp.int32, (block, block), 0)
        < lax.broadcasted_iota(jnp.int32, (block, block), 1),
        1.0,
        0.0,
    ).astype(BF16)
    ones = jnp.ones((block, block), BF16)
    before = jnp.zeros((TILES, block), F32)
    ranks = []
    for b in range(count // block):
        part = named_b[:, b * block : (b + 1) * block]
        earlier = mm(part, upper) + before
        ranks.append(
            jnp.sum(earlier * named[:, b * block : (b + 1) * block], axis=0, keepdims=True)
        )
        before = before + mm(part, ones)
    rank = jnp.concatenate(ranks, axis=1).astype(jnp.int32)
    slot = own * SLOTS + rank
    rows = rows_ref[...]
    step = 1024
    for q in range(TILES * SLOTS // step):
        line = lax.broadcasted_iota(jnp.int32, (step, count), 0) + q * step
        picked = jnp.where(slot == line, 1.0, 0.0).astype(BF16)
        moved = mm(picked, rows).astype(BF16)
        out_ref[q * step // SLOTS : (q + 1) * step // SLOTS, 0:SLOTS, :] = moved.reshape(
            step // SLOTS, SLOTS, 128
        )
    at_rank = lax.broadcasted_iota(jnp.int32, (SLOTS, count), 0) == rank
    pos = pos_ref[...].astype(F32)
    fields = (
        lat_ref[...].astype(F32),
        lon_ref[...].astype(F32),
        pos[0:1, :],
        pos[1:2, :],
    )
    spots = [jnp.where(at_rank, f, 0.0) for f in fields]
    spots.append(jnp.zeros((128 - SLOTS * len(fields), count), F32))
    cells = nt(named_b, jnp.concatenate(spots, axis=0).astype(BF16)).astype(BF16)
    out_ref[:, SLOTS:CHUNK, :] = jnp.broadcast_to(
        cells.astype(F32)[:, None, :], (TILES, CHUNK - SLOTS, 128)
    ).astype(BF16)


def pack(live, own, lat, lon, pos, rows):
    vmem = pl.BlockSpec(memory_space=pltpu.VMEM)
    return pl.pallas_call(
        pack_kernel,
        out_shape=jax.ShapeDtypeStruct((TILES, CHUNK, 128), BF16),
        in_specs=[pl.BlockSpec(memory_space=pltpu.SMEM)] + [vmem] * 5,
        out_specs=vmem,
        cost_estimate=pl.CostEstimate(flops=700_000_000, bytes_accessed=1_500_000, transcendentals=0),
        name="pack",
    )(live, own, lat, lon, pos, rows)


def tap_weights(cell, frac, offset):
    tap = offset - cell + 3.0
    dist = tap - 3.0 - frac
    weight = jnp.exp(-(dist * dist) / GAUSS)
    return jnp.where((tap >= 0.0) & (tap <= 7.0), weight, 0.0)


def picks():
    eye = np.eye(128, dtype=np.float32)
    shift = np.concatenate([np.eye(128, k=1), np.eye(128, k=-1)], axis=1)
    wanted = (
        {0: 3, 1: 4, 2: 5, 3: 6, 4: 31, 5: 8, 6: 9, 7: 10, 8: 7},
        {0: 4, 1: 5, 2: 6, 3: 7, 4: 8, 5: 9, 6: 10, 7: 11},
        {0: 5, 1: 6, 2: 7, 3: 16, 4: 9, 5: 10, 6: 11, 7: 12, 9: 8},
    )
    side = np.zeros((8, 32, 3, 8, 16), np.float32)
    for b in range(3):
        for target, source in wanted[b].items():
            for line in range(8):
                side[line, source, b, line, target] = 1.0
    return [jnp.asarray(x, BF16) for x in (eye, shift, side.reshape(256, 384))]


def prep_kernel(shift_ref, feat_ref, out_ref):
    count = feat_ref.shape[0]
    turned = jnp.concatenate([feat_ref[i].T for i in range(count)], axis=0)
    moved = mm(turned, shift_ref[...]).astype(BF16)
    out_ref[:, 0] = moved[:, 0:128].reshape(count, 128, 128)
    out_ref[:, 1] = turned.reshape(count, 128, 128)
    out_ref[:, 2] = moved[:, 128:256].reshape(count, 128, 128)


def prep(shift, features):
    return pl.pallas_call(
        prep_kernel,
        grid=(4,),
        out_shape=jax.ShapeDtypeStruct((64, 3, 128, 128), BF16),
        in_specs=[
            pl.BlockSpec((128, 256), lambda i: (0, 0)),
            pl.BlockSpec((16, 128, 128), lambda i: (i, 0, 0)),
        ],
        out_specs=pl.BlockSpec((16, 3, 128, 128), lambda i: (i, 0, 0, 0)),
        cost_estimate=pl.CostEstimate(
            flops=2_200_000_000, bytes_accessed=8_000_000, transcendentals=0
        ),
        compiler_params=pltpu.CompilerParams(vmem_limit_bytes=12 << 20),
        name="prep",
    )(shift, features)


def prep_side_kernel(eye_ref, pick_ref, left_ref, right_ref, head_ref, last_ref, side_ref, cells):
    for at, ref in enumerate((left_ref, right_ref, head_ref, last_ref)):
        cells[:, at * 8 : at * 8 + 8, :] = ref[...]
    turned = nt(eye_ref[...], cells[...].reshape(2048, 128)).astype(BF16)
    for g in range(8):
        moved = mm(turned[:, g * 256 : (g + 1) * 256], pick_ref[...]).astype(BF16)
        for b in range(3):
            side_ref[b * 128 : (b + 1) * 128, g * 128 : (g + 1) * 128] = moved[
                :, b * 128 : (b + 1) * 128
            ]


def prep_side(eye, pick, left, right, head, last):
    vmem = pl.BlockSpec(memory_space=pltpu.VMEM)
    return pl.pallas_call(
        prep_side_kernel,
        out_shape=jax.ShapeDtypeStruct((384, 1024), BF16),
        in_specs=[vmem] * 6,
        out_specs=vmem,
        scratch_shapes=[pltpu.VMEM((64, 32, 128), BF16)],
        cost_estimate=pl.CostEstimate(
            flops=300_000_000, bytes_accessed=1_500_000, transcendentals=0
        ),
        compiler_params=pltpu.CompilerParams(vmem_limit_bytes=6 << 20),
        name="prep_side",
    )(eye, pick, left, right, head, last)


def scatter_kernel(
    in_ref,
    canvas_hbm,
    side_hbm,
    rim_hbm,
    up_hbm,
    down_hbm,
    rows_ref,
    lat_w,
    lon_w,
    side_w,
    canvas_ref,
    side_ref,
    rim_ref,
    block_sem,
    store_sem,
):
    def block_store(step):
        lines = pl.ds(pl.multiple_of(step * 8, 8), 8)
        return pltpu.make_async_copy(
            canvas_ref.at[lines], canvas_hbm.at[lines], block_sem.at[step]
        )

    total = TILES * SLOTS
    rows_ref[...] = in_ref[:, 0:SLOTS, :].reshape(total, 128)
    tail = in_ref[:, SLOTS:CHUNK, :].reshape(TILES * (CHUNK - SLOTS), 128)
    first = jnp.where(
        lax.broadcasted_iota(jnp.int32, (TILES, tail.shape[0]), 1)
        == (CHUNK - SLOTS) * lax.broadcasted_iota(jnp.int32, (TILES, tail.shape[0]), 0),
        1.0,
        0.0,
    ).astype(BF16)
    cells = mm(first, tail)
    cells_t = cells.T.astype(BF16)[: 4 * SLOTS]
    slot_lane = lax.broadcasted_iota(jnp.int32, (TILES, total), 1)
    spread = jnp.where(
        (slot_lane // SLOTS) == lax.broadcasted_iota(jnp.int32, (TILES, total), 0), 1.0, 0.0
    ).astype(BF16)
    wide = mm(cells_t, spread)
    own_slot = (
        lax.broadcasted_iota(jnp.int32, (SLOTS, total), 1) % SLOTS
        == lax.broadcasted_iota(jnp.int32, (SLOTS, total), 0)
    )
    cell_lat, cell_lon, frac_lat, frac_lon = [
        jnp.sum(
            jnp.where(own_slot, wide[f * SLOTS : (f + 1) * SLOTS], 0.0), axis=0, keepdims=True
        )
        for f in range(4)
    ]
    line = lax.broadcasted_iota(jnp.int32, (72, total), 0)
    lat_index = lax.axis_index("lat")
    first_line = jnp.where(lat_index == 0, 4, 0)
    end_line = jnp.where(lat_index == lax.axis_size("lat") - 1, 68, 72)
    kept = (line >= first_line) & (line < end_line)
    lat_w[...] = jnp.where(
        kept, tap_weights(cell_lat, frac_lat, line.astype(F32) - 4.0), 0.0
    )
    column = lax.broadcasted_iota(jnp.int32, (128, total), 0).astype(F32)
    lon_w[...] = tap_weights(cell_lon, frac_lon, column).astype(BF16)
    line8 = lax.broadcasted_iota(jnp.int32, (8, total), 0)
    column = jnp.where(line8 < 4, line8 - 4, line8 + 124).astype(F32)
    side_w[...] = tap_weights(cell_lon, frac_lon, column).astype(BF16).astype(F32)
    def eight_lines(step, carry):
        start = pl.multiple_of(step * 8, 8)
        lat8 = lat_w[pl.ds(start, 8), :]
        acc = jnp.zeros((8 * 128, 128), F32)
        side = jnp.zeros((8 * 8, 128), F32)
        for k in range(total // 256):
            cols = slice(k * 256, (k + 1) * 256)
            lon = lon_w[:, cols].reshape(8, 16, 256)
            parts = []
            side_parts = []
            side_lon = side_w[:, cols]
            for i in range(8):
                one = jnp.broadcast_to(lat8[i : i + 1, cols], (16, 256)).astype(BF16)
                parts.append((lon * one[None]).reshape(128, 256))
                one8 = jnp.broadcast_to(
                    lat8[i : i + 1, cols].astype(BF16).astype(F32), (8, 256)
                )
                side_parts.append(side_lon * one8)
            rows = rows_ref[cols, :]
            acc = acc + mm(jnp.concatenate(parts, axis=0), rows)
            side = side + mm(jnp.concatenate(side_parts, axis=0).astype(BF16), rows)
        ends = acc.reshape(8, 128, 128)
        side = side.reshape(8, 8, 128)
        lines = pl.ds(start, 8)
        canvas_ref[lines, 0:128, :] = ends.astype(BF16)
        canvas_ref[lines, 128:136, :] = side.astype(BF16)
        block_store(step).start()
        side_ref[lines] = jnp.concatenate(
            [side, ends[:, 0:1], ends[:, 127:128], jnp.zeros((8, 6, 128), F32)], axis=1
        ).astype(BF16)
        rim_ref[lines, 0:8, :] = ends[:, 0:8].astype(BF16)
        rim_ref[lines, 8:16, :] = ends[:, 120:128].astype(BF16)
        rim_ref[lines, 16:24, :] = side.astype(BF16)
        return carry

    lax.fori_loop(0, 9, eight_lines, 0)
    stores = [
        pltpu.make_async_copy(canvas_ref.at[1:5], up_hbm, store_sem.at[0]),
        pltpu.make_async_copy(canvas_ref.at[67:72], down_hbm, store_sem.at[1]),
        pltpu.make_async_copy(side_ref, side_hbm, store_sem.at[2]),
        pltpu.make_async_copy(rim_ref, rim_hbm, store_sem.at[3]),
    ]
    for copy in stores:
        copy.start()
    for step in range(9):
        block_store(step).wait()
    for copy in stores:
        copy.wait()


def scatter(incoming):
    vmem = pl.BlockSpec(memory_space=pltpu.VMEM)
    hbm = pl.BlockSpec(memory_space=pltpu.HBM)
    total = TILES * SLOTS
    return pl.pallas_call(
        scatter_kernel,
        out_shape=(
            jax.ShapeDtypeStruct((72, 136, 128), BF16),
            jax.ShapeDtypeStruct((72, 16, 128), BF16),
            jax.ShapeDtypeStruct((72, 24, 128), BF16),
            jax.ShapeDtypeStruct((4, 136, 128), BF16),
            jax.ShapeDtypeStruct((5, 136, 128), BF16),
        ),
        in_specs=[vmem],
        out_specs=(hbm,) * 5,
        scratch_shapes=[
            pltpu.VMEM((total, 128), BF16),
            pltpu.VMEM((72, total), F32),
            pltpu.VMEM((128, total), BF16),
            pltpu.VMEM((8, total), F32),
            pltpu.VMEM((72, 136, 128), BF16),
            pltpu.VMEM((72, 16, 128), BF16),
            pltpu.VMEM((72, 24, 128), BF16),
            pltpu.SemaphoreType.DMA((9,)),
            pltpu.SemaphoreType.DMA((4,)),
        ],
        compiler_params=pltpu.CompilerParams(vmem_limit_bytes=24 << 20),
        cost_estimate=pl.CostEstimate(
            flops=5_200_000_000, bytes_accessed=4_000_000, transcendentals=500_000
        ),
        name="scatter",
    )(incoming)


def own_grad_kernel(
    canvas_hbm, side_hbm, feat_hbm, feat_side_hbm, acc_ref, canvas, side, feat, feat_side, sem
):
    step = 16
    ends = (0, 18, 34, 50, 66)
    parts = [
        (
            pltpu.make_async_copy(
                canvas_hbm.at[3 + ends[k] : 3 + ends[k + 1]],
                canvas.at[ends[k] : ends[k + 1]],
                sem.at[2 * k],
            ),
            pltpu.make_async_copy(
                feat_hbm.at[k * step : (k + 1) * step],
                feat.at[k * step : (k + 1) * step],
                sem.at[2 * k + 1],
            ),
        )
        for k in range(4)
    ]
    rest = [
        pltpu.make_async_copy(side_hbm.at[3:69], side, sem.at[8]),
        pltpu.make_async_copy(feat_side_hbm, feat_side, sem.at[9]),
    ]
    for pair in parts:
        for copy in pair:
            copy.start()
    for copy in rest:
        copy.start()
    total = jnp.zeros((384, 384), F32)
    for k in range(4):
        for copy in parts[k]:
            copy.wait()
        lines = range(k * step, (k + 1) * step)
        lhs = jnp.concatenate(
            [jnp.concatenate([feat[i, b] for i in lines], axis=1) for b in range(3)], axis=0
        )
        rhs = jnp.concatenate(
            [
                canvas[k * step + 2 - a : (k + 1) * step + 2 - a, 0:128, :].reshape(
                    step * 128, 128
                )
                for a in range(3)
            ],
            axis=1,
        )
        total = total + mm(lhs, rhs)
    for copy in rest:
        copy.wait()
    rhs = jnp.concatenate(
        [side[2 - a : 66 - a].reshape(1024, 128) for a in range(3)], axis=1
    )
    acc_ref[...] = total + mm(feat_side[...], rhs)


def own_grad(canvas, side, feat, feat_side):
    hbm = pl.BlockSpec(memory_space=pltpu.HBM)
    return pl.pallas_call(
        own_grad_kernel,
        out_shape=jax.ShapeDtypeStruct((384, 384), F32),
        in_specs=[hbm] * 4,
        out_specs=pl.BlockSpec(memory_space=pltpu.VMEM),
        scratch_shapes=[
            pltpu.VMEM((66, 136, 128), BF16),
            pltpu.VMEM((66, 16, 128), BF16),
            pltpu.VMEM((64, 3, 128, 128), BF16),
            pltpu.VMEM((384, 1024), BF16),
            pltpu.SemaphoreType.DMA((10,)),
        ],
        cost_estimate=pl.CostEstimate(
            flops=2_800_000_000, bytes_accessed=10_000_000, transcendentals=0
        ),
        compiler_params=pltpu.CompilerParams(vmem_limit_bytes=20 << 20),
        name="own_grad",
    )(canvas, side, feat, feat_side)


def halo_grad_kernel(
    acc_ref, above_ref, below_ref, feat_hbm, feat_side_ref, sum_hbm, feat, sums, sem
):
    top = pltpu.make_async_copy(feat_hbm.at[0:5], feat.at[0:5], sem.at[0])
    bottom = pltpu.make_async_copy(feat_hbm.at[60:64], feat.at[5:9], sem.at[1])
    top.start()
    bottom.start()
    sums[1152:, :] = jnp.zeros((2048 - 1152, 128), BF16)

    def beside(ref, count):
        eight = ref[:, 128:136, :].astype(F32)
        first = ref[:, 0:8, :].astype(F32)
        last = ref[:, 120:128, :].astype(F32)
        return jnp.concatenate(
            [eight, first[:, 0:1], last[:, 7:8], jnp.zeros((count, 6, 128), F32)], axis=1
        ).astype(BF16)

    def lines(count, width):
        return jnp.zeros((count, width, 128), BF16)

    above = jnp.concatenate([above_ref[:, 0:128, :], lines(2, 128)], axis=0)
    below = jnp.concatenate([lines(2, 128), below_ref[:, 0:128, :]], axis=0)
    rhs = jnp.concatenate(
        [
            jnp.concatenate([above[2 - a : 7 - a], below[2 - a : 6 - a]], axis=0).reshape(
                9 * 128, 128
            )
            for a in range(3)
        ],
        axis=1,
    )
    above = jnp.concatenate([beside(above_ref, 5), lines(5, 16)], axis=0)
    below = jnp.concatenate([lines(6, 16), beside(below_ref, 4)], axis=0)
    rhs_side = jnp.concatenate(
        [
            jnp.concatenate([above[2 - a : 10 - a], below[2 - a : 10 - a]], axis=0).reshape(
                256, 128
            )
            for a in range(3)
        ],
        axis=1,
    )
    lhs_side = jnp.concatenate([feat_side_ref[:, 0:128], feat_side_ref[:, 896:1024]], axis=1)
    total = acc_ref[...] + mm(lhs_side, rhs_side)
    top.wait()
    bottom.wait()
    lhs = jnp.concatenate(
        [jnp.concatenate([feat[i, b] for i in range(9)], axis=1) for b in range(3)], axis=0
    )
    total = total + mm(lhs, rhs)
    for a in range(3):
        for b in range(3):
            at = (a * 3 + b) * 128
            sums[at : at + 128, :] = total[
                b * 128 : (b + 1) * 128, a * 128 : (a + 1) * 128
            ].astype(BF16)
    store = pltpu.make_async_copy(sums, sum_hbm, sem.at[2])
    store.start()
    store.wait()


def halo_grad(acc, above, below, feat, feat_side):
    vmem = pl.BlockSpec(memory_space=pltpu.VMEM)
    hbm = pl.BlockSpec(memory_space=pltpu.HBM)
    return pl.pallas_call(
        halo_grad_kernel,
        out_shape=jax.ShapeDtypeStruct((2048, 128), BF16),
        in_specs=[vmem, vmem, vmem, hbm, vmem],
        out_specs=hbm,
        scratch_shapes=[
            pltpu.VMEM((9, 3, 128, 128), BF16),
            pltpu.VMEM((2048, 128), BF16),
            pltpu.SemaphoreType.DMA((3,)),
        ],
        cost_estimate=pl.CostEstimate(
            flops=420_000_000, bytes_accessed=3_500_000, transcendentals=0
        ),
        compiler_params=pltpu.CompilerParams(vmem_limit_bytes=12 << 20),
        name="halo_grad",
    )(acc, above, below, feat, feat_side)


def sides_kernel(rim_ref, above_ref, below_ref, right_ref, left_ref):
    def tall(at, cols):
        block = rim_ref[3:69, at : at + 8, :].astype(F32)
        return jnp.concatenate(
            [
                block[0:5] + above_ref[:, cols : cols + 8, :].astype(F32),
                block[5:62],
                block[62:66] + below_ref[:, cols : cols + 8, :].astype(F32),
            ],
            axis=0,
        )

    head = tall(0, 0)
    last = tall(8, 120)
    side = tall(16, 128)
    blank = jnp.zeros((66, 4, 128), F32)
    right_ref[...] = jnp.concatenate([last[:, 7:8], side[:, 4:8], blank[:, :3]], axis=1).astype(
        BF16
    )
    left_ref[...] = jnp.concatenate([side[:, 1:4], head[:, 0:1], blank], axis=1).astype(BF16)


def sides(rim, above, below):
    vmem = pl.BlockSpec(memory_space=pltpu.VMEM)
    shape = jax.ShapeDtypeStruct((66, 8, 128), BF16)
    return pl.pallas_call(
        sides_kernel,
        out_shape=(shape, shape),
        in_specs=[vmem] * 3,
        out_specs=(vmem, vmem),
        cost_estimate=pl.CostEstimate(flops=1_000_000, bytes_accessed=1_000_000, transcendentals=0),
        compiler_params=pltpu.CompilerParams(vmem_limit_bytes=4 << 20),
        name="sides",
    )(rim, above, below)


def conv_kernel(canvas_ref, above_ref, below_ref, left_ref, right_ref, weight_ref, out_ref, grid):
    @pl.when(pl.program_id(0) == 0)
    def _():
        grid[5:62, 0:128, :] = canvas_ref[8:65, 0:128, :]
        grid[0:5, 0:128, :] = (
            canvas_ref[3:8, 0:128, :].astype(F32) + above_ref[:, 0:128, :].astype(F32)
        ).astype(BF16)
        grid[62:66, 0:128, :] = (
            canvas_ref[65:69, 0:128, :].astype(F32) + below_ref[:, 0:128, :].astype(F32)
        ).astype(BF16)
        left = left_ref[...].astype(F32)
        right = right_ref[...].astype(F32)
        blank = jnp.zeros((66, 14, 128), F32)
        grid[:, 0:16, :] = (
            grid[:, 0:16, :].astype(F32)
            + jnp.concatenate([left[:, 1:5], blank[:, :12]], axis=1)
        ).astype(BF16)
        grid[:, 112:128, :] = (
            grid[:, 112:128, :].astype(F32)
            + jnp.concatenate([blank[:, :13], right[:, 0:3]], axis=1)
        ).astype(BF16)
        side = canvas_ref[3:69, 128:136, :].astype(F32)
        side = jnp.concatenate(
            [
                side[0:5] + above_ref[:, 128:136, :].astype(F32),
                side[5:62],
                side[62:66] + below_ref[:, 128:136, :].astype(F32),
            ],
            axis=0,
        )
        grid[:, 128:144, :] = jnp.concatenate(
            [side[:, 4:5] + right[:, 3:4], blank, side[:, 3:4] + left[:, 0:1]], axis=1
        ).astype(BF16)

    start = pl.program_id(0) * 8
    taps = jnp.concatenate(
        [grid[pl.ds(start + 2 - a, 8)].reshape(8 * 144, 128) for a in range(3)], axis=1
    )
    weight = jnp.concatenate([weight_ref[a].reshape(384, 128) for a in range(3)], axis=1)
    every = nt(taps, weight).reshape(8, 144, 384)
    for i in range(8):
        one = every[i]
        got = (
            one[:, 128:256]
            + pltpu.roll(one[:, 0:128], 143, 0)
            + pltpu.roll(one[:, 256:384], 1, 0)
        )
        out_ref[i] = got[0:128].astype(BF16)


def conv(canvas, above, below, left, right, weight):
    def whole(x):
        return pl.BlockSpec(
            x.shape, lambda i: (0,) * x.ndim, pipeline_mode=pl.Buffered(1)
        )

    args = (canvas, above, below, left, right, weight)
    return pl.pallas_call(
        conv_kernel,
        grid=(8,),
        out_shape=jax.ShapeDtypeStruct((64, 128, 128), BF16),
        in_specs=[whole(x) for x in args],
        out_specs=pl.BlockSpec((8, 128, 128), lambda i: (i, 0, 0)),
        scratch_shapes=[pltpu.VMEM((66, 144, 128), BF16)],
        compiler_params=pltpu.CompilerParams(vmem_limit_bytes=16 << 20),
        cost_estimate=pl.CostEstimate(
            flops=2_700_000_000, bytes_accessed=4_500_000, transcendentals=0
        ),
        name="conv",
    )(*args)


def gather_kernel(in_ref, out_ref):
    mine = jnp.sum(in_ref[...].astype(F32), axis=0)
    out_ref[...] = jnp.broadcast_to(mine.astype(BF16)[None], out_ref.shape)


def share(got):
    vmem = pl.BlockSpec(memory_space=pltpu.VMEM)
    return pl.pallas_call(
        gather_kernel,
        out_shape=jax.ShapeDtypeStruct(got.shape, BF16),
        in_specs=[vmem],
        out_specs=vmem,
        cost_estimate=pl.CostEstimate(flops=300_000, bytes_accessed=1_000_000, transcendentals=0),
        compiler_params=pltpu.CompilerParams(vmem_limit_bytes=3 << 20),
        name="share",
    )(got)


def finish_kernel(in_ref, out_ref):
    out_ref[...] = in_ref[...].reshape(384, 128).astype(F32)


def finish(every):
    return pl.pallas_call(
        finish_kernel,
        grid=(3,),
        out_shape=jax.ShapeDtypeStruct((1152, 128), F32),
        in_specs=[pl.BlockSpec((24, 16, 128), lambda i: (i, 0, 0))],
        out_specs=pl.BlockSpec((384, 128), lambda i: (i, 0)),
        compiler_params=pltpu.CompilerParams(vmem_limit_bytes=2 << 20),
        cost_estimate=pl.CostEstimate(flops=0, bytes_accessed=900_000, transcendentals=0),
        name="finish",
    )(every)


def both_ways(forth, back, axis, closed):
    count = lax.axis_size(axis)
    ends = count if closed else count - 1
    return (
        lax.ppermute(forth, axis, [(i, (i + 1) % count) for i in range(ends)]),
        lax.ppermute(back, axis, [((i + 1) % count, i) for i in range(ends)]),
    )


def shards(grad_rows, owner, lat_offset, lon_offset, position, live_count, features, conv_weight):
    count = grad_rows.shape[0]
    outgoing = pack(
        live_count,
        owner.reshape(1, count),
        lat_offset.reshape(1, count),
        lon_offset.reshape(1, count),
        position.T,
        grad_rows,
    )
    incoming = lax.all_to_all(outgoing, AXES, 0, 0, tiled=True)
    eye, shift, pick = picks()
    last, head = features[:, 120:128], features[:, 0:8]
    left, right = both_ways(last, head, "lon", True)
    feat = prep(shift, features)
    feat_side = prep_side(eye, pick, left, right, head, last)
    canvas, side, rim, up, down = scatter(incoming)
    grid_above, grid_below = both_ways(down, up, "lat", False)
    acc = own_grad(canvas, side, feat, feat_side)
    part = halo_grad(acc, grid_above, grid_below, feat, feat_side)
    got = lax.all_to_all(part.reshape(TILES, 16, 128), AXES, 0, 0, tiled=True)
    send_right, send_left = sides(rim, grid_above, grid_below)
    from_left, from_right = both_ways(send_right, send_left, "lon", True)
    got, from_left, from_right = lax.optimization_barrier((got, from_left, from_right))
    every = lax.all_to_all(share(got), AXES, 0, 0, tiled=True)
    input_grad = conv(canvas, grid_above, grid_below, from_left, from_right, conv_weight)
    weight_grad = finish(every)
    return input_grad, weight_grad.reshape(3, 3, 128, 128)


def solution(mesh):
    placed = (
        P(("lat", "lon"), None),
        P(("lat", "lon"), None),
        P(("lat", "lon")),
        P(("lat", "lon")),
        P(("lat", "lon"), None),
        P(("lat", "lon")),
        P("lat", "lon", None),
        P(),
    )
    return jax.shard_map(
        shards, mesh=mesh, in_specs=placed, out_specs=(P("lat", "lon", None), P()), check_vma=False
    )
```

```python
import functools

import jax
import jax.numpy as jnp
import numpy as np
from jax import lax
from jax.experimental import pallas as pl
from jax.experimental.pallas import tpu as pltpu
from jax.sharding import PartitionSpec as P

AXES = ("lat", "lon")
BF16 = jnp.bfloat16
F32 = jnp.float32
SLOTS = 16
CHUNK = 18
SHARE = 10
TILES = 128
GAUSS = 2.0 * 1.5 * 1.5


def nt(lhs, rhs):
    return lax.dot_general(lhs, rhs, (((1,), (1,)), ((), ())), preferred_element_type=F32)


def mm(lhs, rhs):
    return jnp.dot(lhs, rhs, preferred_element_type=F32)


def pack_kernel(live_ref, own_ref, lat_ref, lon_ref, pos_ref, rows_ref, out_ref):
    count = own_ref.shape[1]
    lane = lax.broadcasted_iota(jnp.int32, (1, count), 1)
    own = jnp.where(lane < live_ref[0], own_ref[...], TILES)
    tile_line = lax.broadcasted_iota(jnp.int32, (TILES, count), 0)
    named = jnp.where(own == tile_line, 1.0, 0.0)
    named_b = named.astype(BF16)
    block = 256
    upper = jnp.where(
        lax.broadcasted_iota(jnp.int32, (block, block), 0)
        < lax.broadcasted_iota(jnp.int32, (block, block), 1),
        1.0,
        0.0,
    ).astype(BF16)
    ones = jnp.ones((block, block), BF16)
    before = jnp.zeros((TILES, block), F32)
    ranks = []
    for b in range(count // block):
        part = named_b[:, b * block : (b + 1) * block]
        earlier = mm(part, upper) + before
        ranks.append(
            jnp.sum(earlier * named[:, b * block : (b + 1) * block], axis=0, keepdims=True)
        )
        before = before + mm(part, ones)
    rank = jnp.concatenate(ranks, axis=1).astype(jnp.int32)
    at_rank = lax.broadcasted_iota(jnp.int32, (SLOTS, count), 0) == rank
    pos = pos_ref[...].astype(F32)
    fields = (
        lat_ref[...].astype(F32),
        lon_ref[...].astype(F32),
        pos[0:1, :],
        pos[1:2, :],
    )
    spots = [jnp.where(at_rank, f, 0.0) for f in fields]
    spots.append(jnp.zeros((128 - SLOTS * len(fields), count), F32))
    cells = nt(named_b, jnp.concatenate(spots, axis=0).astype(BF16)).astype(BF16)
    slot = own * CHUNK + rank
    rows = rows_ref[...]
    step = 64 * CHUNK
    for q in range(TILES // 64):
        line = lax.broadcasted_iota(jnp.int32, (step, count), 0) + q * step
        picked = jnp.where(slot == line, 1.0, 0.0).astype(BF16)
        line = lax.broadcasted_iota(jnp.int32, (step, TILES), 0) + q * step
        tile = lax.broadcasted_iota(jnp.int32, (step, TILES), 1)
        cell_row = jnp.where(line == tile * CHUNK + SLOTS, 1.0, 0.0).astype(BF16)
        out_ref[q * step : (q + 1) * step, :] = (mm(picked, rows) + mm(cell_row, cells)).astype(
            BF16
        )


def pack(live, own, lat, lon, pos, rows):
    vmem = pl.BlockSpec(memory_space=pltpu.VMEM)
    return pl.pallas_call(
        pack_kernel,
        out_shape=jax.ShapeDtypeStruct((TILES * CHUNK, 128), BF16),
        in_specs=[pl.BlockSpec(memory_space=pltpu.SMEM)] + [vmem] * 5,
        out_specs=vmem,
        cost_estimate=pl.CostEstimate(flops=700_000_000, bytes_accessed=1_500_000, transcendentals=0),
        name="pack",
    )(live, own, lat, lon, pos, rows)


def tap_weights(cell, frac, offset):
    tap = offset - cell + 3.0
    dist = tap - 3.0 - frac
    weight = jnp.exp(-(dist * dist) / GAUSS)
    return jnp.where((tap >= 0.0) & (tap <= 7.0), weight, 0.0)


def picks():
    eye = np.eye(128, dtype=np.float32)
    shift = np.concatenate([np.eye(128, k=1), np.eye(128, k=-1)], axis=1)
    wanted = (
        {0: 3, 1: 4, 2: 5, 3: 6, 4: 31, 5: 8, 6: 9, 7: 10, 8: 7},
        {0: 4, 1: 5, 2: 6, 3: 7, 4: 8, 5: 9, 6: 10, 7: 11},
        {0: 5, 1: 6, 2: 7, 3: 16, 4: 9, 5: 10, 6: 11, 7: 12, 9: 8},
    )
    side = np.zeros((8, 32, 3, 8, 16), np.float32)
    for b in range(3):
        for target, source in wanted[b].items():
            for line in range(8):
                side[line, source, b, line, target] = 1.0
    return [jnp.asarray(x, BF16) for x in (eye, shift, side.reshape(256, 384))]


def prep_kernel(shift_ref, feat_ref, out_ref):
    count = feat_ref.shape[0]
    turned = jnp.concatenate([feat_ref[i].T for i in range(count)], axis=0)
    moved = mm(turned, shift_ref[...]).astype(BF16)
    out_ref[:, 0] = moved[:, 0:128].reshape(count, 128, 128)
    out_ref[:, 1] = turned.reshape(count, 128, 128)
    out_ref[:, 2] = moved[:, 128:256].reshape(count, 128, 128)


def prep(shift, features):
    return pl.pallas_call(
        prep_kernel,
        grid=(4,),
        out_shape=jax.ShapeDtypeStruct((64, 3, 128, 128), BF16),
        in_specs=[
            pl.BlockSpec((128, 256), lambda i: (0, 0)),
            pl.BlockSpec((16, 128, 128), lambda i: (i, 0, 0)),
        ],
        out_specs=pl.BlockSpec((16, 3, 128, 128), lambda i: (i, 0, 0, 0)),
        cost_estimate=pl.CostEstimate(
            flops=2_200_000_000, bytes_accessed=8_000_000, transcendentals=0
        ),
        compiler_params=pltpu.CompilerParams(vmem_limit_bytes=12 << 20),
        name="prep",
    )(shift, features)


def prep_side_kernel(eye_ref, pick_ref, left_ref, right_ref, head_ref, last_ref, side_ref, cells):
    for at, ref in enumerate((left_ref, right_ref, head_ref, last_ref)):
        cells[:, at * 8 : at * 8 + 8, :] = ref[...]
    turned = nt(eye_ref[...], cells[...].reshape(2048, 128)).astype(BF16)
    for g in range(8):
        moved = mm(turned[:, g * 256 : (g + 1) * 256], pick_ref[...]).astype(BF16)
        for b in range(3):
            side_ref[b * 128 : (b + 1) * 128, g * 128 : (g + 1) * 128] = moved[
                :, b * 128 : (b + 1) * 128
            ]


def prep_side(eye, pick, left, right, head, last):
    vmem = pl.BlockSpec(memory_space=pltpu.VMEM)
    return pl.pallas_call(
        prep_side_kernel,
        out_shape=jax.ShapeDtypeStruct((384, 1024), BF16),
        in_specs=[vmem] * 6,
        out_specs=vmem,
        scratch_shapes=[pltpu.VMEM((64, 32, 128), BF16)],
        cost_estimate=pl.CostEstimate(
            flops=300_000_000, bytes_accessed=1_500_000, transcendentals=0
        ),
        compiler_params=pltpu.CompilerParams(vmem_limit_bytes=6 << 20),
        name="prep_side",
    )(eye, pick, left, right, head, last)


def scatter_kernel(
    in_ref,
    canvas_hbm,
    side_hbm,
    rim_hbm,
    up_hbm,
    down_hbm,
    rows_ref,
    lat_w,
    lon_w,
    side_w,
    canvas_ref,
    side_ref,
    rim_ref,
    block_sem,
    store_sem,
):
    def block_store(step):
        lines = pl.ds(pl.multiple_of(step * 8, 8), 8)
        return pltpu.make_async_copy(
            canvas_ref.at[lines], canvas_hbm.at[lines], block_sem.at[step]
        )

    total = TILES * SLOTS
    for source in range(TILES):
        rows_ref[source * SLOTS : (source + 1) * SLOTS, :] = in_ref[
            source * CHUNK : source * CHUNK + SLOTS, :
        ]
    first = jnp.where(
        lax.broadcasted_iota(jnp.int32, (TILES, TILES * CHUNK), 1)
        == CHUNK * lax.broadcasted_iota(jnp.int32, (TILES, TILES * CHUNK), 0) + SLOTS,
        1.0,
        0.0,
    ).astype(BF16)
    cells = mm(first, in_ref[...])
    cells_t = cells.T.astype(BF16)[: 4 * SLOTS]
    slot_lane = lax.broadcasted_iota(jnp.int32, (TILES, total), 1)
    spread = jnp.where(
        lax.shift_right_logical(slot_lane, 4) == lax.broadcasted_iota(jnp.int32, (TILES, total), 0), 1.0, 0.0
    ).astype(BF16)
    wide = mm(cells_t, spread)
    own_slot = (
        (lax.broadcasted_iota(jnp.int32, (SLOTS, total), 1) & (SLOTS - 1))
        == lax.broadcasted_iota(jnp.int32, (SLOTS, total), 0)
    )
    cell_lat, cell_lon, frac_lat, frac_lon = [
        jnp.sum(
            jnp.where(own_slot, wide[f * SLOTS : (f + 1) * SLOTS], 0.0), axis=0, keepdims=True
        )
        for f in range(4)
    ]
    line = lax.broadcasted_iota(jnp.int32, (72, total), 0)
    lat_index = lax.axis_index("lat")
    first_line = jnp.where(lat_index == 0, 4, 0)
    end_line = jnp.where(lat_index == lax.axis_size("lat") - 1, 68, 72)
    kept = (line >= first_line) & (line < end_line)
    lat_w[...] = jnp.where(
        kept, tap_weights(cell_lat, frac_lat, line.astype(F32) - 4.0), 0.0
    )
    column = lax.broadcasted_iota(jnp.int32, (128, total), 0).astype(F32)
    lon_w[...] = tap_weights(cell_lon, frac_lon, column).astype(BF16)
    line8 = lax.broadcasted_iota(jnp.int32, (8, total), 0)
    column = jnp.where(line8 < 4, line8 - 4, line8 + 124).astype(F32)
    side_w[...] = tap_weights(cell_lon, frac_lon, column).astype(BF16).astype(F32)
    def eight_lines(step, carry):
        start = pl.multiple_of(step * 8, 8)
        lat8 = lat_w[pl.ds(start, 8), :]
        acc = jnp.zeros((8 * 128, 128), F32)
        side = jnp.zeros((8 * 8, 128), F32)
        for k in range(total // 256):
            cols = slice(k * 256, (k + 1) * 256)
            lon = lon_w[:, cols].reshape(8, 16, 256)
            parts = []
            side_parts = []
            side_lon = side_w[:, cols]
            for i in range(8):
                one = jnp.broadcast_to(lat8[i : i + 1, cols], (16, 256)).astype(BF16)
                parts.append((lon * one[None]).reshape(128, 256))
                one8 = jnp.broadcast_to(
                    lat8[i : i + 1, cols].astype(BF16).astype(F32), (8, 256)
                )
                side_parts.append(side_lon * one8)
            rows = rows_ref[cols, :]
            acc = acc + mm(jnp.concatenate(parts, axis=0), rows)
            side = side + mm(jnp.concatenate(side_parts, axis=0).astype(BF16), rows)
        ends = acc.reshape(8, 128, 128)
        side = side.reshape(8, 8, 128)
        lines = pl.ds(start, 8)
        canvas_ref[lines, 0:128, :] = ends.astype(BF16)
        canvas_ref[lines, 128:136, :] = side.astype(BF16)
        block_store(step).start()
        side_ref[lines] = jnp.concatenate(
            [side, ends[:, 0:1], ends[:, 127:128], jnp.zeros((8, 6, 128), F32)], axis=1
        ).astype(BF16)
        rim_ref[lines, 0:8, :] = ends[:, 0:8].astype(BF16)
        rim_ref[lines, 8:16, :] = ends[:, 120:128].astype(BF16)
        rim_ref[lines, 16:24, :] = side.astype(BF16)
        return carry

    lax.fori_loop(0, 9, eight_lines, 0)
    stores = [
        pltpu.make_async_copy(canvas_ref.at[1:5], up_hbm, store_sem.at[0]),
        pltpu.make_async_copy(canvas_ref.at[67:72], down_hbm, store_sem.at[1]),
        pltpu.make_async_copy(side_ref, side_hbm, store_sem.at[2]),
        pltpu.make_async_copy(rim_ref, rim_hbm, store_sem.at[3]),
    ]
    for copy in stores:
        copy.start()
    for step in range(9):
        block_store(step).wait()
    for copy in stores:
        copy.wait()


def scatter(incoming):
    vmem = pl.BlockSpec(memory_space=pltpu.VMEM)
    hbm = pl.BlockSpec(memory_space=pltpu.HBM)
    total = TILES * SLOTS
    return pl.pallas_call(
        scatter_kernel,
        out_shape=(
            jax.ShapeDtypeStruct((72, 136, 128), BF16),
            jax.ShapeDtypeStruct((72, 16, 128), BF16),
            jax.ShapeDtypeStruct((72, 24, 128), BF16),
            jax.ShapeDtypeStruct((4, 136, 128), BF16),
            jax.ShapeDtypeStruct((5, 136, 128), BF16),
        ),
        in_specs=[vmem],
        out_specs=(hbm,) * 5,
        scratch_shapes=[
            pltpu.VMEM((total, 128), BF16),
            pltpu.VMEM((72, total), F32),
            pltpu.VMEM((128, total), BF16),
            pltpu.VMEM((8, total), F32),
            pltpu.VMEM((72, 136, 128), BF16),
            pltpu.VMEM((72, 16, 128), BF16),
            pltpu.VMEM((72, 24, 128), BF16),
            pltpu.SemaphoreType.DMA((9,)),
            pltpu.SemaphoreType.DMA((4,)),
        ],
        compiler_params=pltpu.CompilerParams(vmem_limit_bytes=24 << 20),
        cost_estimate=pl.CostEstimate(
            flops=5_200_000_000, bytes_accessed=4_000_000, transcendentals=500_000
        ),
        name="scatter",
    )(incoming)


def own_grad_kernel(
    canvas_hbm, side_hbm, feat_hbm, feat_side_hbm, acc_ref, canvas, side, feat, feat_side, sem
):
    step = 16
    ends = (0, 18, 34, 50, 66)
    parts = [
        (
            pltpu.make_async_copy(
                canvas_hbm.at[3 + ends[k] : 3 + ends[k + 1]],
                canvas.at[ends[k] : ends[k + 1]],
                sem.at[2 * k],
            ),
            pltpu.make_async_copy(
                feat_hbm.at[k * step : (k + 1) * step],
                feat.at[k * step : (k + 1) * step],
                sem.at[2 * k + 1],
            ),
        )
        for k in range(4)
    ]
    rest = [
        pltpu.make_async_copy(side_hbm.at[3:69], side, sem.at[8]),
        pltpu.make_async_copy(feat_side_hbm, feat_side, sem.at[9]),
    ]
    for pair in parts:
        for copy in pair:
            copy.start()
    for copy in rest:
        copy.start()
    total = jnp.zeros((384, 384), F32)
    for k in range(4):
        for copy in parts[k]:
            copy.wait()
        lines = range(k * step, (k + 1) * step)
        lhs = jnp.concatenate(
            [jnp.concatenate([feat[i, b] for i in lines], axis=1) for b in range(3)], axis=0
        )
        rhs = jnp.concatenate(
            [
                canvas[k * step + 2 - a : (k + 1) * step + 2 - a, 0:128, :].reshape(
                    step * 128, 128
                )
                for a in range(3)
            ],
            axis=1,
        )
        total = total + mm(lhs, rhs)
    for copy in rest:
        copy.wait()
    rhs = jnp.concatenate(
        [side[2 - a : 66 - a].reshape(1024, 128) for a in range(3)], axis=1
    )
    acc_ref[...] = total + mm(feat_side[...], rhs)


def own_grad(canvas, side, feat, feat_side):
    hbm = pl.BlockSpec(memory_space=pltpu.HBM)
    return pl.pallas_call(
        own_grad_kernel,
        out_shape=jax.ShapeDtypeStruct((384, 384), F32),
        in_specs=[hbm] * 4,
        out_specs=pl.BlockSpec(memory_space=pltpu.VMEM),
        scratch_shapes=[
            pltpu.VMEM((66, 136, 128), BF16),
            pltpu.VMEM((66, 16, 128), BF16),
            pltpu.VMEM((64, 3, 128, 128), BF16),
            pltpu.VMEM((384, 1024), BF16),
            pltpu.SemaphoreType.DMA((10,)),
        ],
        cost_estimate=pl.CostEstimate(
            flops=2_800_000_000, bytes_accessed=10_000_000, transcendentals=0
        ),
        compiler_params=pltpu.CompilerParams(vmem_limit_bytes=20 << 20),
        name="own_grad",
    )(canvas, side, feat, feat_side)


def halo_grad_kernel(
    acc_ref, above_ref, below_ref, feat_hbm, feat_side_ref, sum_hbm, feat, sums, sem
):
    top = pltpu.make_async_copy(feat_hbm.at[0:5], feat.at[0:5], sem.at[0])
    bottom = pltpu.make_async_copy(feat_hbm.at[60:64], feat.at[5:9], sem.at[1])
    top.start()
    bottom.start()
    sums[1152:, :] = jnp.zeros((TILES * SHARE - 1152, 128), BF16)

    def beside(ref, count):
        eight = ref[:, 128:136, :].astype(F32)
        first = ref[:, 0:8, :].astype(F32)
        last = ref[:, 120:128, :].astype(F32)
        return jnp.concatenate(
            [eight, first[:, 0:1], last[:, 7:8], jnp.zeros((count, 6, 128), F32)], axis=1
        ).astype(BF16)

    def lines(count, width):
        return jnp.zeros((count, width, 128), BF16)

    above = jnp.concatenate([above_ref[:, 0:128, :], lines(2, 128)], axis=0)
    below = jnp.concatenate([lines(2, 128), below_ref[:, 0:128, :]], axis=0)
    rhs = jnp.concatenate(
        [
            jnp.concatenate([above[2 - a : 7 - a], below[2 - a : 6 - a]], axis=0).reshape(
                9 * 128, 128
            )
            for a in range(3)
        ],
        axis=1,
    )
    above = jnp.concatenate([beside(above_ref, 5), lines(5, 16)], axis=0)
    below = jnp.concatenate([lines(6, 16), beside(below_ref, 4)], axis=0)
    rhs_side = jnp.concatenate(
        [
            jnp.concatenate([above[2 - a : 10 - a], below[2 - a : 10 - a]], axis=0).reshape(
                256, 128
            )
            for a in range(3)
        ],
        axis=1,
    )
    lhs_side = jnp.concatenate([feat_side_ref[:, 0:128], feat_side_ref[:, 896:1024]], axis=1)
    total = acc_ref[...] + mm(lhs_side, rhs_side)
    top.wait()
    bottom.wait()
    lhs = jnp.concatenate(
        [jnp.concatenate([feat[i, b] for i in range(9)], axis=1) for b in range(3)], axis=0
    )
    total = total + mm(lhs, rhs)
    for a in range(3):
        for b in range(3):
            at = (a * 3 + b) * 128
            sums[at : at + 128, :] = total[
                b * 128 : (b + 1) * 128, a * 128 : (a + 1) * 128
            ].astype(BF16)
    store = pltpu.make_async_copy(sums, sum_hbm, sem.at[2])
    store.start()
    store.wait()


def halo_grad(acc, above, below, feat, feat_side):
    vmem = pl.BlockSpec(memory_space=pltpu.VMEM)
    hbm = pl.BlockSpec(memory_space=pltpu.HBM)
    return pl.pallas_call(
        halo_grad_kernel,
        out_shape=jax.ShapeDtypeStruct((TILES * SHARE, 128), BF16),
        in_specs=[vmem, vmem, vmem, hbm, vmem],
        out_specs=hbm,
        scratch_shapes=[
            pltpu.VMEM((9, 3, 128, 128), BF16),
            pltpu.VMEM((TILES * SHARE, 128), BF16),
            pltpu.SemaphoreType.DMA((3,)),
        ],
        cost_estimate=pl.CostEstimate(
            flops=420_000_000, bytes_accessed=3_500_000, transcendentals=0
        ),
        compiler_params=pltpu.CompilerParams(vmem_limit_bytes=12 << 20),
        name="halo_grad",
    )(acc, above, below, feat, feat_side)


def sides_kernel(rim_ref, above_ref, below_ref, right_ref, left_ref):
    def tall(at, cols):
        block = rim_ref[3:69, at : at + 8, :].astype(F32)
        return jnp.concatenate(
            [
                block[0:5] + above_ref[:, cols : cols + 8, :].astype(F32),
                block[5:62],
                block[62:66] + below_ref[:, cols : cols + 8, :].astype(F32),
            ],
            axis=0,
        )

    head = tall(0, 0)
    last = tall(8, 120)
    side = tall(16, 128)
    blank = jnp.zeros((66, 4, 128), F32)
    right_ref[...] = jnp.concatenate([last[:, 7:8], side[:, 4:8], blank[:, :3]], axis=1).astype(
        BF16
    )
    left_ref[...] = jnp.concatenate([side[:, 1:4], head[:, 0:1], blank], axis=1).astype(BF16)


def sides(rim, above, below):
    vmem = pl.BlockSpec(memory_space=pltpu.VMEM)
    shape = jax.ShapeDtypeStruct((66, 8, 128), BF16)
    return pl.pallas_call(
        sides_kernel,
        out_shape=(shape, shape),
        in_specs=[vmem] * 3,
        out_specs=(vmem, vmem),
        cost_estimate=pl.CostEstimate(flops=1_000_000, bytes_accessed=1_000_000, transcendentals=0),
        compiler_params=pltpu.CompilerParams(vmem_limit_bytes=4 << 20),
        name="sides",
    )(rim, above, below)


def conv_kernel(canvas_ref, above_ref, below_ref, left_ref, right_ref, weight_ref, out_ref, grid):
    @pl.when(pl.program_id(0) == 0)
    def _():
        grid[5:62, 0:128, :] = canvas_ref[8:65, 0:128, :]
        grid[0:5, 0:128, :] = (
            canvas_ref[3:8, 0:128, :].astype(F32) + above_ref[:, 0:128, :].astype(F32)
        ).astype(BF16)
        grid[62:66, 0:128, :] = (
            canvas_ref[65:69, 0:128, :].astype(F32) + below_ref[:, 0:128, :].astype(F32)
        ).astype(BF16)
        left = left_ref[...].astype(F32)
        right = right_ref[...].astype(F32)
        blank = jnp.zeros((66, 14, 128), F32)
        grid[:, 0:16, :] = (
            grid[:, 0:16, :].astype(F32)
            + jnp.concatenate([left[:, 1:5], blank[:, :12]], axis=1)
        ).astype(BF16)
        grid[:, 112:128, :] = (
            grid[:, 112:128, :].astype(F32)
            + jnp.concatenate([blank[:, :13], right[:, 0:3]], axis=1)
        ).astype(BF16)
        side = canvas_ref[3:69, 128:136, :].astype(F32)
        side = jnp.concatenate(
            [
                side[0:5] + above_ref[:, 128:136, :].astype(F32),
                side[5:62],
                side[62:66] + below_ref[:, 128:136, :].astype(F32),
            ],
            axis=0,
        )
        grid[:, 128:144, :] = jnp.concatenate(
            [side[:, 4:5] + right[:, 3:4], blank, side[:, 3:4] + left[:, 0:1]], axis=1
        ).astype(BF16)

    start = pl.program_id(0) * 8
    taps = jnp.concatenate(
        [grid[pl.ds(start + 2 - a, 8)].reshape(8 * 144, 128) for a in range(3)], axis=1
    )
    weight = jnp.concatenate([weight_ref[a].reshape(384, 128) for a in range(3)], axis=1)
    every = nt(taps, weight).reshape(8, 144, 384)
    for i in range(8):
        one = every[i]
        got = (
            one[:, 128:256]
            + pltpu.roll(one[:, 0:128], 143, 0)
            + pltpu.roll(one[:, 256:384], 1, 0)
        )
        out_ref[i] = got[0:128].astype(BF16)


def conv(canvas, above, below, left, right, weight):
    def whole(x):
        return pl.BlockSpec(
            x.shape, lambda i: (0,) * x.ndim, pipeline_mode=pl.Buffered(1)
        )

    args = (canvas, above, below, left, right, weight)
    return pl.pallas_call(
        conv_kernel,
        grid=(8,),
        out_shape=jax.ShapeDtypeStruct((64, 128, 128), BF16),
        in_specs=[whole(x) for x in args],
        out_specs=pl.BlockSpec((8, 128, 128), lambda i: (i, 0, 0)),
        scratch_shapes=[pltpu.VMEM((66, 144, 128), BF16)],
        compiler_params=pltpu.CompilerParams(vmem_limit_bytes=16 << 20),
        cost_estimate=pl.CostEstimate(
            flops=2_700_000_000, bytes_accessed=4_500_000, transcendentals=0
        ),
        name="conv",
    )(*args)


def share_rows():
    which = np.arange(TILES * SHARE)[:, None] % SHARE == np.arange(16)[None, :]
    return jnp.asarray(which.astype(np.float32), BF16)


def share_kernel(spread_ref, in_ref, out_ref):
    shape = (16, TILES * SHARE)
    row = lax.broadcasted_iota(jnp.int32, shape, 1)
    pick = jnp.where(
        lax.rem(row, SHARE) == lax.broadcasted_iota(jnp.int32, shape, 0), 1.0, 0.0
    ).astype(BF16)
    mine = mm(pick, in_ref[...]).astype(BF16)
    out_ref[...] = mm(spread_ref[...], mine).astype(BF16)


def share(got):
    vmem = pl.BlockSpec(memory_space=pltpu.VMEM)
    return pl.pallas_call(
        share_kernel,
        out_shape=jax.ShapeDtypeStruct(got.shape, BF16),
        in_specs=[vmem] * 2,
        out_specs=vmem,
        compiler_params=pltpu.CompilerParams(vmem_limit_bytes=3 << 20),
        cost_estimate=pl.CostEstimate(flops=10_000_000, bytes_accessed=1_000_000, transcendentals=0),
        name="share",
    )(share_rows(), got)


def finish_kernel(in_ref, out_ref):
    out_ref[...] = in_ref[0:1152, :].astype(F32)


def finish(every):
    vmem = pl.BlockSpec(memory_space=pltpu.VMEM)
    return pl.pallas_call(
        finish_kernel,
        out_shape=jax.ShapeDtypeStruct((1152, 128), F32),
        in_specs=[vmem],
        out_specs=vmem,
        compiler_params=pltpu.CompilerParams(vmem_limit_bytes=2 << 20),
        cost_estimate=pl.CostEstimate(flops=0, bytes_accessed=900_000, transcendentals=0),
        name="finish",
    )(every)


def exchange(rows):
    pairs = rows.reshape(TILES, -1, 2, rows.shape[1])
    return lax.all_to_all(pairs, AXES, 0, 0, tiled=True).reshape(rows.shape)


def both_ways(forth, back, axis, closed):
    count = lax.axis_size(axis)
    ends = count if closed else count - 1
    return (
        lax.ppermute(forth, axis, [(i, (i + 1) % count) for i in range(ends)]),
        lax.ppermute(back, axis, [((i + 1) % count, i) for i in range(ends)]),
    )


def shards(grad_rows, owner, lat_offset, lon_offset, position, live_count, features, conv_weight):
    count = grad_rows.shape[0]
    outgoing = pack(
        live_count,
        owner.reshape(1, count),
        lat_offset.reshape(1, count),
        lon_offset.reshape(1, count),
        position.T,
        grad_rows,
    )
    incoming = exchange(outgoing)
    eye, shift, pick = picks()
    last, head = features[:, 120:128], features[:, 0:8]
    left, right = both_ways(last, head, "lon", True)
    feat = prep(shift, features)
    feat_side = prep_side(eye, pick, left, right, head, last)
    canvas, side, rim, up, down = scatter(incoming)
    grid_above, grid_below = both_ways(down, up, "lat", False)
    acc = own_grad(canvas, side, feat, feat_side)
    part = halo_grad(acc, grid_above, grid_below, feat, feat_side)
    got = exchange(part)
    send_right, send_left = sides(rim, grid_above, grid_below)
    from_left, from_right = both_ways(send_right, send_left, "lon", True)
    got, from_left, from_right = lax.optimization_barrier((got, from_left, from_right))
    every = exchange(share(got))
    input_grad = conv(canvas, grid_above, grid_below, from_left, from_right, conv_weight)
    weight_grad = finish(every)
    return input_grad, weight_grad.reshape(3, 3, 128, 128)


def solution(mesh):
    placed = (
        P(("lat", "lon"), None),
        P(("lat", "lon"), None),
        P(("lat", "lon")),
        P(("lat", "lon")),
        P(("lat", "lon"), None),
        P(("lat", "lon")),
        P("lat", "lon", None),
        P(),
    )
    return jax.shard_map(
        shards, mesh=mesh, in_specs=placed, out_specs=(P("lat", "lon", None), P()), check_vma=False
    )
```

```python
import functools

import jax
import jax.numpy as jnp
import numpy as np
from jax import lax
from jax.experimental import pallas as pl
from jax.experimental.pallas import tpu as pltpu
from jax.sharding import PartitionSpec as P

AXES = ("lat", "lon")
BF16 = jnp.bfloat16
F32 = jnp.float32
SLOTS = 16
CHUNK = 18
SHARE = 10
TILES = 128
GAUSS = 2.0 * 1.5 * 1.5


def nt(lhs, rhs):
    return lax.dot_general(lhs, rhs, (((1,), (1,)), ((), ())), preferred_element_type=F32)


def mm(lhs, rhs):
    return jnp.dot(lhs, rhs, preferred_element_type=F32)


def pack_kernel(live_ref, own_ref, lat_ref, lon_ref, pos_ref, rows_ref, out_ref):
    count = own_ref.shape[1]
    lane = lax.broadcasted_iota(jnp.int32, (1, count), 1)
    own = jnp.where(lane < live_ref[0], own_ref[...], TILES)
    tile_line = lax.broadcasted_iota(jnp.int32, (TILES, count), 0)
    named = jnp.where(own == tile_line, 1.0, 0.0)
    named_b = named.astype(BF16)
    block = 256
    upper = jnp.where(
        lax.broadcasted_iota(jnp.int32, (block, block), 0)
        < lax.broadcasted_iota(jnp.int32, (block, block), 1),
        1.0,
        0.0,
    ).astype(BF16)
    ones = jnp.ones((block, block), BF16)
    before = jnp.zeros((TILES, block), F32)
    ranks = []
    for b in range(count // block):
        part = named_b[:, b * block : (b + 1) * block]
        earlier = mm(part, upper) + before
        ranks.append(
            jnp.sum(earlier * named[:, b * block : (b + 1) * block], axis=0, keepdims=True)
        )
        before = before + mm(part, ones)
    rank = jnp.concatenate(ranks, axis=1).astype(jnp.int32)
    at_rank = lax.broadcasted_iota(jnp.int32, (SLOTS, count), 0) == rank
    pos = pos_ref[...].astype(F32)
    fields = (
        lat_ref[...].astype(F32),
        lon_ref[...].astype(F32),
        pos[0:1, :],
        pos[1:2, :],
    )
    spots = [jnp.where(at_rank, f, 0.0) for f in fields]
    spots.append(jnp.zeros((128 - SLOTS * len(fields), count), F32))
    cells = nt(named_b, jnp.concatenate(spots, axis=0).astype(BF16)).astype(BF16)
    slot = own * CHUNK + rank
    rows = rows_ref[...]
    step = 64 * CHUNK
    for q in range(TILES // 64):
        line = lax.broadcasted_iota(jnp.int32, (step, count), 0) + q * step
        picked = jnp.where(slot == line, 1.0, 0.0).astype(BF16)
        line = lax.broadcasted_iota(jnp.int32, (step, TILES), 0) + q * step
        tile = lax.broadcasted_iota(jnp.int32, (step, TILES), 1)
        cell_row = jnp.where(line == tile * CHUNK + SLOTS, 1.0, 0.0).astype(BF16)
        out_ref[q * step : (q + 1) * step, :] = (mm(picked, rows) + mm(cell_row, cells)).astype(
            BF16
        )


def pack(live, own, lat, lon, pos, rows):
    vmem = pl.BlockSpec(memory_space=pltpu.VMEM)
    return pl.pallas_call(
        pack_kernel,
        out_shape=jax.ShapeDtypeStruct((TILES * CHUNK, 128), BF16),
        in_specs=[pl.BlockSpec(memory_space=pltpu.SMEM)] + [vmem] * 5,
        out_specs=vmem,
        cost_estimate=pl.CostEstimate(flops=700_000_000, bytes_accessed=1_500_000, transcendentals=0),
        name="pack",
    )(live, own, lat, lon, pos, rows)


def tap_weights(cell, frac, offset):
    tap = offset - cell + 3.0
    dist = tap - 3.0 - frac
    weight = jnp.exp(-(dist * dist) / GAUSS)
    return jnp.where((tap >= 0.0) & (tap <= 7.0), weight, 0.0)


def picks():
    eye = np.eye(128, dtype=np.float32)
    shift = np.concatenate([np.eye(128, k=1), np.eye(128, k=-1)], axis=1)
    wanted = (
        {0: 3, 1: 4, 2: 5, 3: 6, 4: 31, 5: 8, 6: 9, 7: 10, 8: 7},
        {0: 4, 1: 5, 2: 6, 3: 7, 4: 8, 5: 9, 6: 10, 7: 11},
        {0: 5, 1: 6, 2: 7, 3: 16, 4: 9, 5: 10, 6: 11, 7: 12, 9: 8},
    )
    side = np.zeros((8, 32, 3, 8, 16), np.float32)
    for b in range(3):
        for target, source in wanted[b].items():
            for line in range(8):
                side[line, source, b, line, target] = 1.0
    return [jnp.asarray(x, BF16) for x in (eye, shift, side.reshape(256, 384))]


def prep_kernel(shift_ref, feat_ref, out_ref):
    count = feat_ref.shape[0]
    turned = jnp.concatenate([feat_ref[i].T for i in range(count)], axis=0)
    moved = mm(turned, shift_ref[...]).astype(BF16)
    out_ref[:, 0] = moved[:, 0:128].reshape(count, 128, 128)
    out_ref[:, 1] = turned.reshape(count, 128, 128)
    out_ref[:, 2] = moved[:, 128:256].reshape(count, 128, 128)


def prep(shift, features):
    return pl.pallas_call(
        prep_kernel,
        grid=(4,),
        out_shape=jax.ShapeDtypeStruct((64, 3, 128, 128), BF16),
        in_specs=[
            pl.BlockSpec((128, 256), lambda i: (0, 0)),
            pl.BlockSpec((16, 128, 128), lambda i: (i, 0, 0)),
        ],
        out_specs=pl.BlockSpec((16, 3, 128, 128), lambda i: (i, 0, 0, 0)),
        cost_estimate=pl.CostEstimate(
            flops=2_200_000_000, bytes_accessed=8_000_000, transcendentals=0
        ),
        compiler_params=pltpu.CompilerParams(vmem_limit_bytes=12 << 20),
        name="prep",
    )(shift, features)


def prep_side_kernel(eye_ref, pick_ref, left_ref, right_ref, head_ref, last_ref, side_ref, cells):
    for at, ref in enumerate((left_ref, right_ref, head_ref, last_ref)):
        cells[:, at * 8 : at * 8 + 8, :] = ref[...]
    turned = nt(eye_ref[...], cells[...].reshape(2048, 128)).astype(BF16)
    for g in range(8):
        moved = mm(turned[:, g * 256 : (g + 1) * 256], pick_ref[...]).astype(BF16)
        for b in range(3):
            side_ref[b * 128 : (b + 1) * 128, g * 128 : (g + 1) * 128] = moved[
                :, b * 128 : (b + 1) * 128
            ]


def prep_side(eye, pick, left, right, head, last):
    vmem = pl.BlockSpec(memory_space=pltpu.VMEM)
    return pl.pallas_call(
        prep_side_kernel,
        out_shape=jax.ShapeDtypeStruct((384, 1024), BF16),
        in_specs=[vmem] * 6,
        out_specs=vmem,
        scratch_shapes=[pltpu.VMEM((64, 32, 128), BF16)],
        cost_estimate=pl.CostEstimate(
            flops=300_000_000, bytes_accessed=1_500_000, transcendentals=0
        ),
        compiler_params=pltpu.CompilerParams(vmem_limit_bytes=6 << 20),
        name="prep_side",
    )(eye, pick, left, right, head, last)


def scatter_kernel(
    in_ref,
    canvas_hbm,
    side_hbm,
    rim_hbm,
    up_hbm,
    down_hbm,
    rows_ref,
    lat_w,
    lon_w,
    side_w,
    canvas_ref,
    side_ref,
    rim_ref,
    block_sem,
    store_sem,
):
    def block_store(step):
        lines = pl.ds(pl.multiple_of(step * 8, 8), 8)
        return pltpu.make_async_copy(
            canvas_ref.at[lines], canvas_hbm.at[lines], block_sem.at[step]
        )

    total = TILES * SLOTS
    for source in range(TILES):
        rows_ref[source * SLOTS : (source + 1) * SLOTS, :] = in_ref[
            source * CHUNK : source * CHUNK + SLOTS, :
        ]
    first = jnp.where(
        lax.broadcasted_iota(jnp.int32, (TILES, TILES * CHUNK), 1)
        == CHUNK * lax.broadcasted_iota(jnp.int32, (TILES, TILES * CHUNK), 0) + SLOTS,
        1.0,
        0.0,
    ).astype(BF16)
    cells = mm(first, in_ref[...])
    cells_t = cells.T.astype(BF16)[: 4 * SLOTS]
    slot_lane = lax.broadcasted_iota(jnp.int32, (TILES, total), 1)
    spread = jnp.where(
        lax.shift_right_logical(slot_lane, 4) == lax.broadcasted_iota(jnp.int32, (TILES, total), 0), 1.0, 0.0
    ).astype(BF16)
    wide = mm(cells_t, spread)
    own_slot = (
        (lax.broadcasted_iota(jnp.int32, (SLOTS, total), 1) & (SLOTS - 1))
        == lax.broadcasted_iota(jnp.int32, (SLOTS, total), 0)
    )
    cell_lat, cell_lon, frac_lat, frac_lon = [
        jnp.sum(
            jnp.where(own_slot, wide[f * SLOTS : (f + 1) * SLOTS], 0.0), axis=0, keepdims=True
        )
        for f in range(4)
    ]
    line = lax.broadcasted_iota(jnp.int32, (72, total), 0)
    lat_index = lax.axis_index("lat")
    first_line = jnp.where(lat_index == 0, 4, 0)
    end_line = jnp.where(lat_index == lax.axis_size("lat") - 1, 68, 72)
    kept = (line >= first_line) & (line < end_line)
    lat_w[...] = jnp.where(
        kept, tap_weights(cell_lat, frac_lat, line.astype(F32) - 4.0), 0.0
    )
    column = lax.broadcasted_iota(jnp.int32, (128, total), 0).astype(F32)
    lon_w[...] = tap_weights(cell_lon, frac_lon, column).astype(BF16)
    line8 = lax.broadcasted_iota(jnp.int32, (8, total), 0)
    column = jnp.where(line8 < 4, line8 - 4, line8 + 124).astype(F32)
    side_w[...] = tap_weights(cell_lon, frac_lon, column).astype(BF16).astype(F32)
    def eight_lines(step, carry):
        start = pl.multiple_of(step * 8, 8)
        lat8 = lat_w[pl.ds(start, 8), :]
        acc = jnp.zeros((8 * 128, 128), F32)
        side = jnp.zeros((8 * 8, 128), F32)
        for k in range(total // 256):
            cols = slice(k * 256, (k + 1) * 256)
            lon = lon_w[:, cols].reshape(8, 16, 256)
            parts = []
            side_parts = []
            side_lon = side_w[:, cols]
            for i in range(8):
                one = jnp.broadcast_to(lat8[i : i + 1, cols], (16, 256)).astype(BF16)
                parts.append((lon * one[None]).reshape(128, 256))
                one8 = jnp.broadcast_to(
                    lat8[i : i + 1, cols].astype(BF16).astype(F32), (8, 256)
                )
                side_parts.append(side_lon * one8)
            rows = rows_ref[cols, :]
            acc = acc + mm(jnp.concatenate(parts, axis=0), rows)
            side = side + mm(jnp.concatenate(side_parts, axis=0).astype(BF16), rows)
        ends = acc.reshape(8, 128, 128)
        side = side.reshape(8, 8, 128)
        lines = pl.ds(start, 8)
        canvas_ref[lines, 0:128, :] = ends.astype(BF16)
        canvas_ref[lines, 128:136, :] = side.astype(BF16)
        block_store(step).start()
        side_ref[lines] = jnp.concatenate(
            [side, ends[:, 0:1], ends[:, 127:128], jnp.zeros((8, 6, 128), F32)], axis=1
        ).astype(BF16)
        rim_ref[lines, 0:8, :] = ends[:, 0:8].astype(BF16)
        rim_ref[lines, 8:16, :] = ends[:, 120:128].astype(BF16)
        rim_ref[lines, 16:24, :] = side.astype(BF16)
        return carry

    lax.fori_loop(0, 9, eight_lines, 0)
    stores = [
        pltpu.make_async_copy(canvas_ref.at[1:5], up_hbm, store_sem.at[0]),
        pltpu.make_async_copy(canvas_ref.at[67:72], down_hbm, store_sem.at[1]),
        pltpu.make_async_copy(side_ref, side_hbm, store_sem.at[2]),
        pltpu.make_async_copy(rim_ref, rim_hbm, store_sem.at[3]),
    ]
    for copy in stores:
        copy.start()
    for step in range(9):
        block_store(step).wait()
    for copy in stores:
        copy.wait()


def scatter(incoming):
    vmem = pl.BlockSpec(memory_space=pltpu.VMEM)
    hbm = pl.BlockSpec(memory_space=pltpu.HBM)
    total = TILES * SLOTS
    return pl.pallas_call(
        scatter_kernel,
        out_shape=(
            jax.ShapeDtypeStruct((72, 136, 128), BF16),
            jax.ShapeDtypeStruct((72, 16, 128), BF16),
            jax.ShapeDtypeStruct((72, 24, 128), BF16),
            jax.ShapeDtypeStruct((4, 136, 128), BF16),
            jax.ShapeDtypeStruct((5, 136, 128), BF16),
        ),
        in_specs=[vmem],
        out_specs=(hbm,) * 5,
        scratch_shapes=[
            pltpu.VMEM((total, 128), BF16),
            pltpu.VMEM((72, total), F32),
            pltpu.VMEM((128, total), BF16),
            pltpu.VMEM((8, total), F32),
            pltpu.VMEM((72, 136, 128), BF16),
            pltpu.VMEM((72, 16, 128), BF16),
            pltpu.VMEM((72, 24, 128), BF16),
            pltpu.SemaphoreType.DMA((9,)),
            pltpu.SemaphoreType.DMA((4,)),
        ],
        compiler_params=pltpu.CompilerParams(vmem_limit_bytes=24 << 20),
        cost_estimate=pl.CostEstimate(
            flops=5_200_000_000, bytes_accessed=4_000_000, transcendentals=500_000
        ),
        name="scatter",
    )(incoming)


def own_grad_kernel(
    canvas_hbm, side_hbm, feat_hbm, feat_side_hbm, acc_ref, canvas, side, feat, feat_side, sem
):
    step = 16
    ends = (0, 18, 34, 50, 66)
    parts = [
        (
            pltpu.make_async_copy(
                canvas_hbm.at[3 + ends[k] : 3 + ends[k + 1]],
                canvas.at[ends[k] : ends[k + 1]],
                sem.at[2 * k],
            ),
            pltpu.make_async_copy(
                feat_hbm.at[k * step : (k + 1) * step],
                feat.at[k * step : (k + 1) * step],
                sem.at[2 * k + 1],
            ),
        )
        for k in range(4)
    ]
    rest = [
        pltpu.make_async_copy(side_hbm.at[3:69], side, sem.at[8]),
        pltpu.make_async_copy(feat_side_hbm, feat_side, sem.at[9]),
    ]
    for pair in parts:
        for copy in pair:
            copy.start()
    for copy in rest:
        copy.start()
    total = jnp.zeros((384, 384), F32)
    for k in range(4):
        for copy in parts[k]:
            copy.wait()
        lines = range(k * step, (k + 1) * step)
        lhs = jnp.concatenate(
            [jnp.concatenate([feat[i, b] for i in lines], axis=1) for b in range(3)], axis=0
        )
        rhs = jnp.concatenate(
            [
                canvas[k * step + 2 - a : (k + 1) * step + 2 - a, 0:128, :].reshape(
                    step * 128, 128
                )
                for a in range(3)
            ],
            axis=1,
        )
        total = total + mm(lhs, rhs)
    for copy in rest:
        copy.wait()
    rhs = jnp.concatenate(
        [side[2 - a : 66 - a].reshape(1024, 128) for a in range(3)], axis=1
    )
    acc_ref[...] = total + mm(feat_side[...], rhs)


def own_grad(canvas, side, feat, feat_side):
    hbm = pl.BlockSpec(memory_space=pltpu.HBM)
    return pl.pallas_call(
        own_grad_kernel,
        out_shape=jax.ShapeDtypeStruct((384, 384), F32),
        in_specs=[hbm] * 4,
        out_specs=pl.BlockSpec(memory_space=pltpu.VMEM),
        scratch_shapes=[
            pltpu.VMEM((66, 136, 128), BF16),
            pltpu.VMEM((66, 16, 128), BF16),
            pltpu.VMEM((64, 3, 128, 128), BF16),
            pltpu.VMEM((384, 1024), BF16),
            pltpu.SemaphoreType.DMA((10,)),
        ],
        cost_estimate=pl.CostEstimate(
            flops=2_800_000_000, bytes_accessed=10_000_000, transcendentals=0
        ),
        compiler_params=pltpu.CompilerParams(vmem_limit_bytes=20 << 20),
        name="own_grad",
    )(canvas, side, feat, feat_side)


def halo_grad_kernel(
    acc_ref, above_ref, below_ref, feat_hbm, feat_side_ref, sum_hbm, feat, sums, sem
):
    top = pltpu.make_async_copy(feat_hbm.at[0:5], feat.at[0:5], sem.at[0])
    bottom = pltpu.make_async_copy(feat_hbm.at[60:64], feat.at[5:9], sem.at[1])
    top.start()
    bottom.start()
    sums[1152:, :] = jnp.zeros((TILES * SHARE - 1152, 128), BF16)

    def beside(ref, count):
        eight = ref[:, 128:136, :].astype(F32)
        first = ref[:, 0:8, :].astype(F32)
        last = ref[:, 120:128, :].astype(F32)
        return jnp.concatenate(
            [eight, first[:, 0:1], last[:, 7:8], jnp.zeros((count, 6, 128), F32)], axis=1
        ).astype(BF16)

    def lines(count, width):
        return jnp.zeros((count, width, 128), BF16)

    above = jnp.concatenate([above_ref[:, 0:128, :], lines(2, 128)], axis=0)
    below = jnp.concatenate([lines(2, 128), below_ref[:, 0:128, :]], axis=0)
    rhs = jnp.concatenate(
        [
            jnp.concatenate([above[2 - a : 7 - a], below[2 - a : 6 - a]], axis=0).reshape(
                9 * 128, 128
            )
            for a in range(3)
        ],
        axis=1,
    )
    above = jnp.concatenate([beside(above_ref, 5), lines(5, 16)], axis=0)
    below = jnp.concatenate([lines(6, 16), beside(below_ref, 4)], axis=0)
    rhs_side = jnp.concatenate(
        [
            jnp.concatenate([above[2 - a : 10 - a], below[2 - a : 10 - a]], axis=0).reshape(
                256, 128
            )
            for a in range(3)
        ],
        axis=1,
    )
    lhs_side = jnp.concatenate([feat_side_ref[:, 0:128], feat_side_ref[:, 896:1024]], axis=1)
    total = acc_ref[...] + mm(lhs_side, rhs_side)
    top.wait()
    bottom.wait()
    lhs = jnp.concatenate(
        [jnp.concatenate([feat[i, b] for i in range(9)], axis=1) for b in range(3)], axis=0
    )
    total = total + mm(lhs, rhs)
    for a in range(3):
        for b in range(3):
            at = (a * 3 + b) * 128
            sums[at : at + 128, :] = total[
                b * 128 : (b + 1) * 128, a * 128 : (a + 1) * 128
            ].astype(BF16)
    store = pltpu.make_async_copy(sums, sum_hbm, sem.at[2])
    store.start()
    store.wait()


def halo_grad(acc, above, below, feat, feat_side):
    vmem = pl.BlockSpec(memory_space=pltpu.VMEM)
    hbm = pl.BlockSpec(memory_space=pltpu.HBM)
    return pl.pallas_call(
        halo_grad_kernel,
        out_shape=jax.ShapeDtypeStruct((TILES * SHARE, 128), BF16),
        in_specs=[vmem, vmem, vmem, hbm, vmem],
        out_specs=hbm,
        scratch_shapes=[
            pltpu.VMEM((9, 3, 128, 128), BF16),
            pltpu.VMEM((TILES * SHARE, 128), BF16),
            pltpu.SemaphoreType.DMA((3,)),
        ],
        cost_estimate=pl.CostEstimate(
            flops=420_000_000, bytes_accessed=3_500_000, transcendentals=0
        ),
        compiler_params=pltpu.CompilerParams(vmem_limit_bytes=12 << 20),
        name="halo_grad",
    )(acc, above, below, feat, feat_side)


def sides_kernel(rim_ref, above_ref, below_ref, right_ref, left_ref):
    def tall(at, cols):
        block = rim_ref[3:69, at : at + 8, :].astype(F32)
        return jnp.concatenate(
            [
                block[0:5] + above_ref[:, cols : cols + 8, :].astype(F32),
                block[5:62],
                block[62:66] + below_ref[:, cols : cols + 8, :].astype(F32),
            ],
            axis=0,
        )

    head = tall(0, 0)
    last = tall(8, 120)
    side = tall(16, 128)
    blank = jnp.zeros((66, 4, 128), F32)
    right_ref[...] = jnp.concatenate([last[:, 7:8], side[:, 4:8], blank[:, :3]], axis=1).astype(
        BF16
    )
    left_ref[...] = jnp.concatenate([side[:, 1:4], head[:, 0:1], blank], axis=1).astype(BF16)


def sides(rim, above, below):
    vmem = pl.BlockSpec(memory_space=pltpu.VMEM)
    shape = jax.ShapeDtypeStruct((66, 8, 128), BF16)
    return pl.pallas_call(
        sides_kernel,
        out_shape=(shape, shape),
        in_specs=[vmem] * 3,
        out_specs=(vmem, vmem),
        cost_estimate=pl.CostEstimate(flops=1_000_000, bytes_accessed=1_000_000, transcendentals=0),
        compiler_params=pltpu.CompilerParams(vmem_limit_bytes=4 << 20),
        name="sides",
    )(rim, above, below)


def conv_kernel(canvas_ref, above_ref, below_ref, left_ref, right_ref, weight_ref, out_ref, grid):
    @pl.when(pl.program_id(0) == 0)
    def _():
        grid[5:62, 0:128, :] = canvas_ref[8:65, 0:128, :]
        grid[0:5, 0:128, :] = (
            canvas_ref[3:8, 0:128, :].astype(F32) + above_ref[:, 0:128, :].astype(F32)
        ).astype(BF16)
        grid[62:66, 0:128, :] = (
            canvas_ref[65:69, 0:128, :].astype(F32) + below_ref[:, 0:128, :].astype(F32)
        ).astype(BF16)
        left = left_ref[...].astype(F32)
        right = right_ref[...].astype(F32)
        blank = jnp.zeros((66, 14, 128), F32)
        grid[:, 0:16, :] = (
            grid[:, 0:16, :].astype(F32)
            + jnp.concatenate([left[:, 1:5], blank[:, :12]], axis=1)
        ).astype(BF16)
        grid[:, 112:128, :] = (
            grid[:, 112:128, :].astype(F32)
            + jnp.concatenate([blank[:, :13], right[:, 0:3]], axis=1)
        ).astype(BF16)
        side = canvas_ref[3:69, 128:136, :].astype(F32)
        side = jnp.concatenate(
            [
                side[0:5] + above_ref[:, 128:136, :].astype(F32),
                side[5:62],
                side[62:66] + below_ref[:, 128:136, :].astype(F32),
            ],
            axis=0,
        )
        grid[:, 128:144, :] = jnp.concatenate(
            [side[:, 4:5] + right[:, 3:4], blank, side[:, 3:4] + left[:, 0:1]], axis=1
        ).astype(BF16)

    start = pl.program_id(0) * 8
    taps = jnp.concatenate(
        [grid[pl.ds(start + 2 - a, 8)].reshape(8 * 144, 128) for a in range(3)], axis=1
    )
    weight = jnp.concatenate([weight_ref[a].reshape(384, 128) for a in range(3)], axis=1)
    every = nt(taps, weight).reshape(8, 144, 384)
    for i in range(8):
        one = every[i]
        got = (
            one[:, 128:256]
            + pltpu.roll(one[:, 0:128], 143, 0)
            + pltpu.roll(one[:, 256:384], 1, 0)
        )
        out_ref[i] = got[0:128].astype(BF16)


def conv(canvas, above, below, left, right, weight):
    def whole(x):
        return pl.BlockSpec(
            x.shape, lambda i: (0,) * x.ndim, pipeline_mode=pl.Buffered(1)
        )

    args = (canvas, above, below, left, right, weight)
    return pl.pallas_call(
        conv_kernel,
        grid=(8,),
        out_shape=jax.ShapeDtypeStruct((64, 128, 128), BF16),
        in_specs=[whole(x) for x in args],
        out_specs=pl.BlockSpec((8, 128, 128), lambda i: (i, 0, 0)),
        scratch_shapes=[pltpu.VMEM((66, 144, 128), BF16)],
        compiler_params=pltpu.CompilerParams(vmem_limit_bytes=16 << 20),
        cost_estimate=pl.CostEstimate(
            flops=2_700_000_000, bytes_accessed=4_500_000, transcendentals=0
        ),
        name="conv",
    )(*args)


def share_rows():
    which = np.arange(TILES * SHARE)[:, None] % SHARE == np.arange(16)[None, :]
    return jnp.asarray(which.astype(np.float32), BF16)


def share_kernel(spread_ref, in_ref, out_ref):
    shape = (16, TILES * SHARE)
    row = lax.broadcasted_iota(jnp.int32, shape, 1)
    pick = jnp.where(
        lax.rem(row, SHARE) == lax.broadcasted_iota(jnp.int32, shape, 0), 1.0, 0.0
    ).astype(BF16)
    mine = mm(pick, in_ref[...]).astype(BF16)
    out_ref[...] = mm(spread_ref[...], mine).astype(BF16)


def share(got):
    vmem = pl.BlockSpec(memory_space=pltpu.VMEM)
    return pl.pallas_call(
        share_kernel,
        out_shape=jax.ShapeDtypeStruct(got.shape, BF16),
        in_specs=[vmem] * 2,
        out_specs=vmem,
        compiler_params=pltpu.CompilerParams(vmem_limit_bytes=3 << 20),
        cost_estimate=pl.CostEstimate(flops=10_000_000, bytes_accessed=1_000_000, transcendentals=0),
        name="share",
    )(share_rows(), got)


def finish_kernel(in_ref, out_ref):
    out_ref[...] = in_ref[0:1152, :].astype(F32)


def finish(every):
    vmem = pl.BlockSpec(memory_space=pltpu.VMEM)
    return pl.pallas_call(
        finish_kernel,
        out_shape=jax.ShapeDtypeStruct((1152, 128), F32),
        in_specs=[vmem],
        out_specs=vmem,
        compiler_params=pltpu.CompilerParams(vmem_limit_bytes=2 << 20),
        cost_estimate=pl.CostEstimate(flops=0, bytes_accessed=900_000, transcendentals=0),
        name="finish",
    )(every)


def exchange(rows):
    pairs = rows.reshape(TILES, -1, 2, rows.shape[1])
    return lax.all_to_all(pairs, AXES, 0, 0, tiled=True).reshape(rows.shape)


def both_ways(forth, back, axis, closed):
    count = lax.axis_size(axis)
    ends = count if closed else count - 1
    return (
        lax.ppermute(forth, axis, [(i, (i + 1) % count) for i in range(ends)]),
        lax.ppermute(back, axis, [((i + 1) % count, i) for i in range(ends)]),
    )


def shards(grad_rows, owner, lat_offset, lon_offset, position, live_count, features, conv_weight):
    count = grad_rows.shape[0]
    outgoing = pack(
        live_count,
        owner.reshape(1, count),
        lat_offset.reshape(1, count),
        lon_offset.reshape(1, count),
        position.T,
        grad_rows,
    )
    incoming = exchange(outgoing)
    eye, shift, pick = picks()
    last, head = features[:, 120:128], features[:, 0:8]
    left, right = both_ways(last, head, "lon", True)
    feat = prep(shift, features)
    canvas, side, rim, up, down = scatter(incoming)
    side, left, right = lax.optimization_barrier((side, left, right))
    feat_side = prep_side(eye, pick, left, right, head, last)
    grid_above, grid_below = both_ways(down, up, "lat", False)
    acc = own_grad(canvas, side, feat, feat_side)
    part = halo_grad(acc, grid_above, grid_below, feat, feat_side)
    got = exchange(part)
    send_right, send_left = sides(rim, grid_above, grid_below)
    from_left, from_right = both_ways(send_right, send_left, "lon", True)
    got, _, _ = lax.optimization_barrier((got, send_right, send_left))
    every = exchange(share(got))
    input_grad = conv(canvas, grid_above, grid_below, from_left, from_right, conv_weight)
    weight_grad = finish(every)
    return input_grad, weight_grad.reshape(3, 3, 128, 128)


def solution(mesh):
    placed = (
        P(("lat", "lon"), None),
        P(("lat", "lon"), None),
        P(("lat", "lon")),
        P(("lat", "lon")),
        P(("lat", "lon"), None),
        P(("lat", "lon")),
        P("lat", "lon", None),
        P(),
    )
    return jax.shard_map(
        shards, mesh=mesh, in_specs=placed, out_specs=(P("lat", "lon", None), P()), check_vma=False
    )
```

```python
import functools

import jax
import jax.numpy as jnp
import numpy as np
from jax import lax
from jax.experimental import pallas as pl
from jax.experimental.pallas import tpu as pltpu
from jax.sharding import PartitionSpec as P

AXES = ("lat", "lon")
BF16 = jnp.bfloat16
F32 = jnp.float32
SLOTS = 16
CHUNK = 18
SHARE = 10
TILES = 128
GAUSS = 2.0 * 1.5 * 1.5


def nt(lhs, rhs):
    return lax.dot_general(lhs, rhs, (((1,), (1,)), ((), ())), preferred_element_type=F32)


def mm(lhs, rhs):
    return jnp.dot(lhs, rhs, preferred_element_type=F32)


def pack_kernel(live_ref, own_ref, lat_ref, lon_ref, pos_ref, rows_ref, out_ref):
    count = own_ref.shape[1]
    lane = lax.broadcasted_iota(jnp.int32, (1, count), 1)
    own = jnp.where(lane < live_ref[0], own_ref[...], TILES)
    tile_line = lax.broadcasted_iota(jnp.int32, (TILES, count), 0)
    named = jnp.where(own == tile_line, 1.0, 0.0)
    named_b = named.astype(BF16)
    block = 256
    upper = jnp.where(
        lax.broadcasted_iota(jnp.int32, (block, block), 0)
        < lax.broadcasted_iota(jnp.int32, (block, block), 1),
        1.0,
        0.0,
    ).astype(BF16)
    ones = jnp.ones((block, block), BF16)
    before = jnp.zeros((TILES, block), F32)
    ranks = []
    for b in range(count // block):
        part = named_b[:, b * block : (b + 1) * block]
        earlier = mm(part, upper) + before
        ranks.append(
            jnp.sum(earlier * named[:, b * block : (b + 1) * block], axis=0, keepdims=True)
        )
        before = before + mm(part, ones)
    rank = jnp.concatenate(ranks, axis=1).astype(jnp.int32)
    at_rank = lax.broadcasted_iota(jnp.int32, (SLOTS, count), 0) == rank
    pos = pos_ref[...].astype(F32)
    fields = (
        lat_ref[...].astype(F32),
        lon_ref[...].astype(F32),
        pos[0:1, :],
        pos[1:2, :],
    )
    spots = [jnp.where(at_rank, f, 0.0) for f in fields]
    spots.append(jnp.zeros((128 - SLOTS * len(fields), count), F32))
    cells = nt(named_b, jnp.concatenate(spots, axis=0).astype(BF16)).astype(BF16)
    slot = own * CHUNK + rank
    rows = rows_ref[...]
    step = 64 * CHUNK
    for q in range(TILES // 64):
        line = lax.broadcasted_iota(jnp.int32, (step, count), 0) + q * step
        picked = jnp.where(slot == line, 1.0, 0.0).astype(BF16)
        line = lax.broadcasted_iota(jnp.int32, (step, TILES), 0) + q * step
        tile = lax.broadcasted_iota(jnp.int32, (step, TILES), 1)
        cell_row = jnp.where(line == tile * CHUNK + SLOTS, 1.0, 0.0).astype(BF16)
        out_ref[q * step : (q + 1) * step, :] = (mm(picked, rows) + mm(cell_row, cells)).astype(
            BF16
        )


def pack(live, own, lat, lon, pos, rows):
    vmem = pl.BlockSpec(memory_space=pltpu.VMEM)
    return pl.pallas_call(
        pack_kernel,
        out_shape=jax.ShapeDtypeStruct((TILES * CHUNK, 128), BF16),
        in_specs=[pl.BlockSpec(memory_space=pltpu.SMEM)] + [vmem] * 5,
        out_specs=vmem,
        cost_estimate=pl.CostEstimate(flops=700_000_000, bytes_accessed=1_500_000, transcendentals=0),
        name="pack",
    )(live, own, lat, lon, pos, rows)


def tap_weights(cell, frac, offset):
    tap = offset - cell + 3.0
    dist = tap - 3.0 - frac
    weight = jnp.exp(-(dist * dist) / GAUSS)
    return jnp.where((tap >= 0.0) & (tap <= 7.0), weight, 0.0)


def picks():
    eye = np.eye(128, dtype=np.float32)
    shift = np.concatenate([np.eye(128, k=1), np.eye(128, k=-1)], axis=1)
    wanted = (
        {0: 3, 1: 4, 2: 5, 3: 6, 4: 31, 5: 8, 6: 9, 7: 10, 8: 7},
        {0: 4, 1: 5, 2: 6, 3: 7, 4: 8, 5: 9, 6: 10, 7: 11},
        {0: 5, 1: 6, 2: 7, 3: 16, 4: 9, 5: 10, 6: 11, 7: 12, 9: 8},
    )
    side = np.zeros((8, 32, 3, 8, 16), np.float32)
    for b in range(3):
        for target, source in wanted[b].items():
            for line in range(8):
                side[line, source, b, line, target] = 1.0
    return [jnp.asarray(x, BF16) for x in (eye, shift, side.reshape(256, 384))]


def prep_kernel(shift_ref, feat_ref, out_ref):
    count = feat_ref.shape[0]
    turned = jnp.concatenate([feat_ref[i].T for i in range(count)], axis=0)
    moved = mm(turned, shift_ref[...]).astype(BF16)
    out_ref[:, 0] = moved[:, 0:128].reshape(count, 128, 128)
    out_ref[:, 1] = turned.reshape(count, 128, 128)
    out_ref[:, 2] = moved[:, 128:256].reshape(count, 128, 128)


def prep(shift, features):
    return pl.pallas_call(
        prep_kernel,
        grid=(4,),
        out_shape=jax.ShapeDtypeStruct((64, 3, 128, 128), BF16),
        in_specs=[
            pl.BlockSpec((128, 256), lambda i: (0, 0)),
            pl.BlockSpec((16, 128, 128), lambda i: (i, 0, 0)),
        ],
        out_specs=pl.BlockSpec((16, 3, 128, 128), lambda i: (i, 0, 0, 0)),
        cost_estimate=pl.CostEstimate(
            flops=2_200_000_000, bytes_accessed=8_000_000, transcendentals=0
        ),
        compiler_params=pltpu.CompilerParams(vmem_limit_bytes=12 << 20),
        name="prep",
    )(shift, features)


def prep_side_kernel(eye_ref, pick_ref, left_ref, right_ref, head_ref, last_ref, side_ref, cells):
    for at, ref in enumerate((left_ref, right_ref, head_ref, last_ref)):
        cells[:, at * 8 : at * 8 + 8, :] = ref[...]
    turned = nt(eye_ref[...], cells[...].reshape(2048, 128)).astype(BF16)
    for g in range(8):
        moved = mm(turned[:, g * 256 : (g + 1) * 256], pick_ref[...]).astype(BF16)
        for b in range(3):
            side_ref[b * 128 : (b + 1) * 128, g * 128 : (g + 1) * 128] = moved[
                :, b * 128 : (b + 1) * 128
            ]


def prep_side(eye, pick, left, right, head, last):
    vmem = pl.BlockSpec(memory_space=pltpu.VMEM)
    return pl.pallas_call(
        prep_side_kernel,
        out_shape=jax.ShapeDtypeStruct((384, 1024), BF16),
        in_specs=[vmem] * 6,
        out_specs=vmem,
        scratch_shapes=[pltpu.VMEM((64, 32, 128), BF16)],
        cost_estimate=pl.CostEstimate(
            flops=300_000_000, bytes_accessed=1_500_000, transcendentals=0
        ),
        compiler_params=pltpu.CompilerParams(vmem_limit_bytes=6 << 20),
        name="prep_side",
    )(eye, pick, left, right, head, last)


def scatter_kernel(
    in_ref,
    canvas_hbm,
    side_hbm,
    rim_hbm,
    up_hbm,
    down_hbm,
    rows_ref,
    lat_w,
    lon_w,
    side_w,
    canvas_ref,
    side_ref,
    rim_ref,
    block_sem,
    store_sem,
):
    def block_store(step):
        lines = pl.ds(pl.multiple_of(step * 8, 8), 8)
        return pltpu.make_async_copy(
            canvas_ref.at[lines], canvas_hbm.at[lines], block_sem.at[step]
        )

    total = TILES * SLOTS
    for source in range(TILES):
        rows_ref[source * SLOTS : (source + 1) * SLOTS, :] = in_ref[
            source * CHUNK : source * CHUNK + SLOTS, :
        ]
    first = jnp.where(
        lax.broadcasted_iota(jnp.int32, (TILES, TILES * CHUNK), 1)
        == CHUNK * lax.broadcasted_iota(jnp.int32, (TILES, TILES * CHUNK), 0) + SLOTS,
        1.0,
        0.0,
    ).astype(BF16)
    cells = mm(first, in_ref[...])
    cells_t = cells.T.astype(BF16)[: 4 * SLOTS]
    slot_lane = lax.broadcasted_iota(jnp.int32, (TILES, total), 1)
    spread = jnp.where(
        lax.shift_right_logical(slot_lane, 4) == lax.broadcasted_iota(jnp.int32, (TILES, total), 0), 1.0, 0.0
    ).astype(BF16)
    wide = mm(cells_t, spread)
    own_slot = (
        (lax.broadcasted_iota(jnp.int32, (SLOTS, total), 1) & (SLOTS - 1))
        == lax.broadcasted_iota(jnp.int32, (SLOTS, total), 0)
    )
    cell_lat, cell_lon, frac_lat, frac_lon = [
        jnp.sum(
            jnp.where(own_slot, wide[f * SLOTS : (f + 1) * SLOTS], 0.0), axis=0, keepdims=True
        )
        for f in range(4)
    ]
    line = lax.broadcasted_iota(jnp.int32, (72, total), 0)
    lat_index = lax.axis_index("lat")
    first_line = jnp.where(lat_index == 0, 4, 0)
    end_line = jnp.where(lat_index == lax.axis_size("lat") - 1, 68, 72)
    kept = (line >= first_line) & (line < end_line)
    lat_w[...] = jnp.where(
        kept, tap_weights(cell_lat, frac_lat, line.astype(F32) - 4.0), 0.0
    )
    column = lax.broadcasted_iota(jnp.int32, (128, total), 0).astype(F32)
    lon_w[...] = tap_weights(cell_lon, frac_lon, column).astype(BF16)
    line8 = lax.broadcasted_iota(jnp.int32, (8, total), 0)
    column = jnp.where(line8 < 4, line8 - 4, line8 + 124).astype(F32)
    side_w[...] = tap_weights(cell_lon, frac_lon, column).astype(BF16).astype(F32)
    def eight_lines(step, carry):
        start = pl.multiple_of(step * 8, 8)
        lat8 = lat_w[pl.ds(start, 8), :]
        acc = jnp.zeros((8 * 136, 128), F32)
        for k in range(total // 256):
            cols = slice(k * 256, (k + 1) * 256)
            lon = lon_w[:, cols].reshape(8, 16, 256)
            parts = []
            side_parts = []
            side_lon = side_w[:, cols]
            for i in range(8):
                one = jnp.broadcast_to(lat8[i : i + 1, cols], (16, 256)).astype(BF16)
                parts.append((lon * one[None]).reshape(128, 256))
                one8 = jnp.broadcast_to(
                    lat8[i : i + 1, cols].astype(BF16).astype(F32), (8, 256)
                )
                side_parts.append(side_lon * one8)
            parts.append(jnp.concatenate(side_parts, axis=0).astype(BF16))
            acc = acc + mm(jnp.concatenate(parts, axis=0), rows_ref[cols, :])
        ends = acc[0:1024].reshape(8, 128, 128)
        side = acc[1024:1088].reshape(8, 8, 128)
        lines = pl.ds(start, 8)
        canvas_ref[lines, 0:128, :] = ends.astype(BF16)
        canvas_ref[lines, 128:136, :] = side.astype(BF16)
        block_store(step).start()
        side_ref[lines] = jnp.concatenate(
            [side, ends[:, 0:1], ends[:, 127:128], jnp.zeros((8, 6, 128), F32)], axis=1
        ).astype(BF16)
        rim_ref[lines, 0:8, :] = ends[:, 0:8].astype(BF16)
        rim_ref[lines, 8:16, :] = ends[:, 120:128].astype(BF16)
        rim_ref[lines, 16:24, :] = side.astype(BF16)
        return carry

    lax.fori_loop(0, 9, eight_lines, 0)
    stores = [
        pltpu.make_async_copy(canvas_ref.at[1:5], up_hbm, store_sem.at[0]),
        pltpu.make_async_copy(canvas_ref.at[67:72], down_hbm, store_sem.at[1]),
        pltpu.make_async_copy(side_ref, side_hbm, store_sem.at[2]),
        pltpu.make_async_copy(rim_ref, rim_hbm, store_sem.at[3]),
    ]
    for copy in stores:
        copy.start()
    for step in range(9):
        block_store(step).wait()
    for copy in stores:
        copy.wait()


def scatter(incoming):
    vmem = pl.BlockSpec(memory_space=pltpu.VMEM)
    hbm = pl.BlockSpec(memory_space=pltpu.HBM)
    total = TILES * SLOTS
    return pl.pallas_call(
        scatter_kernel,
        out_shape=(
            jax.ShapeDtypeStruct((72, 136, 128), BF16),
            jax.ShapeDtypeStruct((72, 16, 128), BF16),
            jax.ShapeDtypeStruct((72, 24, 128), BF16),
            jax.ShapeDtypeStruct((4, 136, 128), BF16),
            jax.ShapeDtypeStruct((5, 136, 128), BF16),
        ),
        in_specs=[vmem],
        out_specs=(hbm,) * 5,
        scratch_shapes=[
            pltpu.VMEM((total, 128), BF16),
            pltpu.VMEM((72, total), F32),
            pltpu.VMEM((128, total), BF16),
            pltpu.VMEM((8, total), F32),
            pltpu.VMEM((72, 136, 128), BF16),
            pltpu.VMEM((72, 16, 128), BF16),
            pltpu.VMEM((72, 24, 128), BF16),
            pltpu.SemaphoreType.DMA((9,)),
            pltpu.SemaphoreType.DMA((4,)),
        ],
        compiler_params=pltpu.CompilerParams(vmem_limit_bytes=24 << 20),
        cost_estimate=pl.CostEstimate(
            flops=5_200_000_000, bytes_accessed=4_000_000, transcendentals=500_000
        ),
        name="scatter",
    )(incoming)


def own_grad_kernel(
    canvas_hbm, side_hbm, feat_hbm, feat_side_hbm, acc_ref, canvas, side, feat, feat_side, sem
):
    step = 16
    ends = (0, 18, 34, 50, 66)
    parts = [
        (
            pltpu.make_async_copy(
                canvas_hbm.at[3 + ends[k] : 3 + ends[k + 1]],
                canvas.at[ends[k] : ends[k + 1]],
                sem.at[2 * k],
            ),
            pltpu.make_async_copy(
                feat_hbm.at[k * step : (k + 1) * step],
                feat.at[k * step : (k + 1) * step],
                sem.at[2 * k + 1],
            ),
        )
        for k in range(4)
    ]
    rest = [
        pltpu.make_async_copy(side_hbm.at[3:69], side, sem.at[8]),
        pltpu.make_async_copy(feat_side_hbm, feat_side, sem.at[9]),
    ]
    for pair in parts:
        for copy in pair:
            copy.start()
    for copy in rest:
        copy.start()
    total = jnp.zeros((384, 384), F32)
    for k in range(4):
        for copy in parts[k]:
            copy.wait()
        lines = range(k * step, (k + 1) * step)
        lhs = jnp.concatenate(
            [jnp.concatenate([feat[i, b] for i in lines], axis=1) for b in range(3)], axis=0
        )
        rhs = jnp.concatenate(
            [
                canvas[k * step + 2 - a : (k + 1) * step + 2 - a, 0:128, :].reshape(
                    step * 128, 128
                )
                for a in range(3)
            ],
            axis=1,
        )
        total = total + mm(lhs, rhs)
    for copy in rest:
        copy.wait()
    rhs = jnp.concatenate(
        [side[2 - a : 66 - a].reshape(1024, 128) for a in range(3)], axis=1
    )
    acc_ref[...] = total + mm(feat_side[...], rhs)


def own_grad(canvas, side, feat, feat_side):
    hbm = pl.BlockSpec(memory_space=pltpu.HBM)
    return pl.pallas_call(
        own_grad_kernel,
        out_shape=jax.ShapeDtypeStruct((384, 384), F32),
        in_specs=[hbm] * 4,
        out_specs=pl.BlockSpec(memory_space=pltpu.VMEM),
        scratch_shapes=[
            pltpu.VMEM((66, 136, 128), BF16),
            pltpu.VMEM((66, 16, 128), BF16),
            pltpu.VMEM((64, 3, 128, 128), BF16),
            pltpu.VMEM((384, 1024), BF16),
            pltpu.SemaphoreType.DMA((10,)),
        ],
        cost_estimate=pl.CostEstimate(
            flops=2_800_000_000, bytes_accessed=10_000_000, transcendentals=0
        ),
        compiler_params=pltpu.CompilerParams(vmem_limit_bytes=20 << 20),
        name="own_grad",
    )(canvas, side, feat, feat_side)


def halo_grad_kernel(
    acc_ref, above_ref, below_ref, feat_hbm, feat_side_ref, sum_hbm, feat, sums, sem
):
    top = pltpu.make_async_copy(feat_hbm.at[0:5], feat.at[0:5], sem.at[0])
    bottom = pltpu.make_async_copy(feat_hbm.at[60:64], feat.at[5:9], sem.at[1])
    top.start()
    bottom.start()
    sums[1152:, :] = jnp.zeros((TILES * SHARE - 1152, 128), BF16)

    def beside(ref, count):
        eight = ref[:, 128:136, :].astype(F32)
        first = ref[:, 0:8, :].astype(F32)
        last = ref[:, 120:128, :].astype(F32)
        return jnp.concatenate(
            [eight, first[:, 0:1], last[:, 7:8], jnp.zeros((count, 6, 128), F32)], axis=1
        ).astype(BF16)

    def lines(count, width):
        return jnp.zeros((count, width, 128), BF16)

    above = jnp.concatenate([above_ref[:, 0:128, :], lines(2, 128)], axis=0)
    below = jnp.concatenate([lines(2, 128), below_ref[:, 0:128, :]], axis=0)
    rhs = jnp.concatenate(
        [
            jnp.concatenate([above[2 - a : 7 - a], below[2 - a : 6 - a]], axis=0).reshape(
                9 * 128, 128
            )
            for a in range(3)
        ],
        axis=1,
    )
    above = jnp.concatenate([beside(above_ref, 5), lines(5, 16)], axis=0)
    below = jnp.concatenate([lines(6, 16), beside(below_ref, 4)], axis=0)
    rhs_side = jnp.concatenate(
        [
            jnp.concatenate([above[2 - a : 10 - a], below[2 - a : 10 - a]], axis=0).reshape(
                256, 128
            )
            for a in range(3)
        ],
        axis=1,
    )
    lhs_side = jnp.concatenate([feat_side_ref[:, 0:128], feat_side_ref[:, 896:1024]], axis=1)
    total = acc_ref[...] + mm(lhs_side, rhs_side)
    top.wait()
    bottom.wait()
    lhs = jnp.concatenate(
        [jnp.concatenate([feat[i, b] for i in range(9)], axis=1) for b in range(3)], axis=0
    )
    total = total + mm(lhs, rhs)
    for a in range(3):
        for b in range(3):
            at = (a * 3 + b) * 128
            sums[at : at + 128, :] = total[
                b * 128 : (b + 1) * 128, a * 128 : (a + 1) * 128
            ].astype(BF16)
    store = pltpu.make_async_copy(sums, sum_hbm, sem.at[2])
    store.start()
    store.wait()


def halo_grad(acc, above, below, feat, feat_side):
    vmem = pl.BlockSpec(memory_space=pltpu.VMEM)
    hbm = pl.BlockSpec(memory_space=pltpu.HBM)
    return pl.pallas_call(
        halo_grad_kernel,
        out_shape=jax.ShapeDtypeStruct((TILES * SHARE, 128), BF16),
        in_specs=[vmem, vmem, vmem, hbm, vmem],
        out_specs=hbm,
        scratch_shapes=[
            pltpu.VMEM((9, 3, 128, 128), BF16),
            pltpu.VMEM((TILES * SHARE, 128), BF16),
            pltpu.SemaphoreType.DMA((3,)),
        ],
        cost_estimate=pl.CostEstimate(
            flops=420_000_000, bytes_accessed=3_500_000, transcendentals=0
        ),
        compiler_params=pltpu.CompilerParams(vmem_limit_bytes=12 << 20),
        name="halo_grad",
    )(acc, above, below, feat, feat_side)


def sides_kernel(rim_ref, above_ref, below_ref, right_ref, left_ref):
    def tall(at, cols):
        block = rim_ref[3:69, at : at + 8, :].astype(F32)
        return jnp.concatenate(
            [
                block[0:5] + above_ref[:, cols : cols + 8, :].astype(F32),
                block[5:62],
                block[62:66] + below_ref[:, cols : cols + 8, :].astype(F32),
            ],
            axis=0,
        )

    head = tall(0, 0)
    last = tall(8, 120)
    side = tall(16, 128)
    blank = jnp.zeros((66, 4, 128), F32)
    right_ref[...] = jnp.concatenate([last[:, 7:8], side[:, 4:8], blank[:, :3]], axis=1).astype(
        BF16
    )
    left_ref[...] = jnp.concatenate([side[:, 1:4], head[:, 0:1], blank], axis=1).astype(BF16)


def sides(rim, above, below):
    vmem = pl.BlockSpec(memory_space=pltpu.VMEM)
    shape = jax.ShapeDtypeStruct((66, 8, 128), BF16)
    return pl.pallas_call(
        sides_kernel,
        out_shape=(shape, shape),
        in_specs=[vmem] * 3,
        out_specs=(vmem, vmem),
        cost_estimate=pl.CostEstimate(flops=1_000_000, bytes_accessed=1_000_000, transcendentals=0),
        compiler_params=pltpu.CompilerParams(vmem_limit_bytes=4 << 20),
        name="sides",
    )(rim, above, below)


def conv_kernel(canvas_ref, above_ref, below_ref, left_ref, right_ref, weight_ref, out_ref, grid):
    @pl.when(pl.program_id(0) == 0)
    def _():
        grid[5:62, 0:128, :] = canvas_ref[8:65, 0:128, :]
        grid[0:5, 0:128, :] = (
            canvas_ref[3:8, 0:128, :].astype(F32) + above_ref[:, 0:128, :].astype(F32)
        ).astype(BF16)
        grid[62:66, 0:128, :] = (
            canvas_ref[65:69, 0:128, :].astype(F32) + below_ref[:, 0:128, :].astype(F32)
        ).astype(BF16)
        left = left_ref[...].astype(F32)
        right = right_ref[...].astype(F32)
        blank = jnp.zeros((66, 14, 128), F32)
        grid[:, 0:16, :] = (
            grid[:, 0:16, :].astype(F32)
            + jnp.concatenate([left[:, 1:5], blank[:, :12]], axis=1)
        ).astype(BF16)
        grid[:, 112:128, :] = (
            grid[:, 112:128, :].astype(F32)
            + jnp.concatenate([blank[:, :13], right[:, 0:3]], axis=1)
        ).astype(BF16)
        side = canvas_ref[3:69, 128:136, :].astype(F32)
        side = jnp.concatenate(
            [
                side[0:5] + above_ref[:, 128:136, :].astype(F32),
                side[5:62],
                side[62:66] + below_ref[:, 128:136, :].astype(F32),
            ],
            axis=0,
        )
        grid[:, 128:144, :] = jnp.concatenate(
            [side[:, 4:5] + right[:, 3:4], blank, side[:, 3:4] + left[:, 0:1]], axis=1
        ).astype(BF16)

    start = pl.program_id(0) * 8
    taps = jnp.concatenate(
        [grid[pl.ds(start + 2 - a, 8)].reshape(8 * 144, 128) for a in range(3)], axis=1
    )
    weight = jnp.concatenate([weight_ref[a].reshape(384, 128) for a in range(3)], axis=1)
    every = nt(taps, weight).reshape(8, 144, 384)
    for i in range(8):
        one = every[i]
        got = (
            one[:, 128:256]
            + pltpu.roll(one[:, 0:128], 143, 0)
            + pltpu.roll(one[:, 256:384], 1, 0)
        )
        out_ref[i] = got[0:128].astype(BF16)


def conv(canvas, above, below, left, right, weight):
    def whole(x):
        return pl.BlockSpec(
            x.shape, lambda i: (0,) * x.ndim, pipeline_mode=pl.Buffered(1)
        )

    args = (canvas, above, below, left, right, weight)
    return pl.pallas_call(
        conv_kernel,
        grid=(8,),
        out_shape=jax.ShapeDtypeStruct((64, 128, 128), BF16),
        in_specs=[whole(x) for x in args],
        out_specs=pl.BlockSpec((8, 128, 128), lambda i: (i, 0, 0)),
        scratch_shapes=[pltpu.VMEM((66, 144, 128), BF16)],
        compiler_params=pltpu.CompilerParams(vmem_limit_bytes=16 << 20),
        cost_estimate=pl.CostEstimate(
            flops=2_700_000_000, bytes_accessed=4_500_000, transcendentals=0
        ),
        name="conv",
    )(*args)


def share_kernel(in_ref, out_ref):
    def line_of(shape, axis):
        row = lax.broadcasted_iota(jnp.int32, shape, axis)
        line = lax.broadcasted_iota(jnp.int32, shape, 1 - axis)
        return jnp.where(lax.rem(row, SHARE) == line, 1.0, 0.0).astype(BF16)

    mine = mm(line_of((16, TILES * SHARE), 1), in_ref[...]).astype(BF16)
    block = mm(line_of((8 * SHARE, 16), 0), mine).astype(BF16)
    for i in range(TILES // 8):
        out_ref[i * 8 * SHARE : (i + 1) * 8 * SHARE, :] = block


def share(got):
    vmem = pl.BlockSpec(memory_space=pltpu.VMEM)
    return pl.pallas_call(
        share_kernel,
        out_shape=jax.ShapeDtypeStruct(got.shape, BF16),
        in_specs=[vmem],
        out_specs=vmem,
        compiler_params=pltpu.CompilerParams(vmem_limit_bytes=3 << 20),
        cost_estimate=pl.CostEstimate(flops=10_000_000, bytes_accessed=1_000_000, transcendentals=0),
        name="share",
    )(got)


def finish_kernel(in_ref, out_ref):
    out_ref[...] = in_ref[0:1152, :].astype(F32)


def finish(every):
    vmem = pl.BlockSpec(memory_space=pltpu.VMEM)
    return pl.pallas_call(
        finish_kernel,
        out_shape=jax.ShapeDtypeStruct((1152, 128), F32),
        in_specs=[vmem],
        out_specs=vmem,
        compiler_params=pltpu.CompilerParams(vmem_limit_bytes=2 << 20),
        cost_estimate=pl.CostEstimate(flops=0, bytes_accessed=900_000, transcendentals=0),
        name="finish",
    )(every)


def exchange(rows):
    pairs = rows.reshape(TILES, -1, 2, rows.shape[1])
    return lax.all_to_all(pairs, AXES, 0, 0, tiled=True).reshape(rows.shape)


def both_ways(forth, back, axis, closed):
    count = lax.axis_size(axis)
    ends = count if closed else count - 1
    return (
        lax.ppermute(forth, axis, [(i, (i + 1) % count) for i in range(ends)]),
        lax.ppermute(back, axis, [((i + 1) % count, i) for i in range(ends)]),
    )


def shards(grad_rows, owner, lat_offset, lon_offset, position, live_count, features, conv_weight):
    count = grad_rows.shape[0]
    outgoing = pack(
        live_count,
        owner.reshape(1, count),
        lat_offset.reshape(1, count),
        lon_offset.reshape(1, count),
        position.T,
        grad_rows,
    )
    incoming = exchange(outgoing)
    eye, shift, pick = picks()
    last, head = features[:, 120:128], features[:, 0:8]
    left, right = both_ways(last, head, "lon", True)
    feat = prep(shift, features)
    canvas, side, rim, up, down = scatter(incoming)
    side, left, right = lax.optimization_barrier((side, left, right))
    feat_side = prep_side(eye, pick, left, right, head, last)
    grid_above, grid_below = both_ways(down, up, "lat", False)
    acc = own_grad(canvas, side, feat, feat_side)
    part = halo_grad(acc, grid_above, grid_below, feat, feat_side)
    got = exchange(part)
    send_right, send_left = sides(rim, grid_above, grid_below)
    from_left, from_right = both_ways(send_right, send_left, "lon", True)
    got, _, _ = lax.optimization_barrier((got, send_right, send_left))
    every = exchange(share(got))
    input_grad = conv(canvas, grid_above, grid_below, from_left, from_right, conv_weight)
    weight_grad = finish(every)
    return input_grad, weight_grad.reshape(3, 3, 128, 128)


def solution(mesh):
    placed = (
        P(("lat", "lon"), None),
        P(("lat", "lon"), None),
        P(("lat", "lon")),
        P(("lat", "lon")),
        P(("lat", "lon"), None),
        P(("lat", "lon")),
        P("lat", "lon", None),
        P(),
    )
    return jax.shard_map(
        shards, mesh=mesh, in_specs=placed, out_specs=(P("lat", "lon", None), P()), check_vma=False
    )
```

```python
import functools

import jax
import jax.numpy as jnp
import numpy as np
from jax import lax
from jax.experimental import pallas as pl
from jax.experimental.pallas import tpu as pltpu
from jax.sharding import PartitionSpec as P

AXES = ("lat", "lon")
BF16 = jnp.bfloat16
F32 = jnp.float32
SLOTS = 16
CHUNK = 18
SHARE = 10
TILES = 128
GAUSS = 2.0 * 1.5 * 1.5


def nt(lhs, rhs):
    return lax.dot_general(lhs, rhs, (((1,), (1,)), ((), ())), preferred_element_type=F32)


def mm(lhs, rhs):
    return jnp.dot(lhs, rhs, preferred_element_type=F32)


def pack_kernel(live_ref, own_ref, lat_ref, lon_ref, pos_ref, rows_ref, out_ref):
    count = own_ref.shape[1]
    lane = lax.broadcasted_iota(jnp.int32, (1, count), 1)
    own = jnp.where(lane < live_ref[0], own_ref[...], TILES)
    tile_line = lax.broadcasted_iota(jnp.int32, (TILES, count), 0)
    named = jnp.where(own == tile_line, 1.0, 0.0)
    named_b = named.astype(BF16)
    block = 256
    upper = jnp.where(
        lax.broadcasted_iota(jnp.int32, (block, block), 0)
        < lax.broadcasted_iota(jnp.int32, (block, block), 1),
        1.0,
        0.0,
    ).astype(BF16)
    ones = jnp.ones((block, block), BF16)
    before = jnp.zeros((TILES, block), F32)
    ranks = []
    for b in range(count // block):
        part = named_b[:, b * block : (b + 1) * block]
        earlier = mm(part, upper) + before
        ranks.append(
            jnp.sum(earlier * named[:, b * block : (b + 1) * block], axis=0, keepdims=True)
        )
        before = before + mm(part, ones)
    rank = jnp.concatenate(ranks, axis=1).astype(jnp.int32)
    at_rank = lax.broadcasted_iota(jnp.int32, (SLOTS, count), 0) == rank
    pos = pos_ref[...].astype(F32)
    fields = (
        lat_ref[...].astype(F32),
        lon_ref[...].astype(F32),
        pos[0:1, :],
        pos[1:2, :],
    )
    spots = [jnp.where(at_rank, f, 0.0) for f in fields]
    spots.append(jnp.zeros((128 - SLOTS * len(fields), count), F32))
    cells = nt(named_b, jnp.concatenate(spots, axis=0).astype(BF16)).astype(BF16)
    slot = own * CHUNK + rank
    rows = rows_ref[...]
    step = 64 * CHUNK
    for q in range(TILES // 64):
        line = lax.broadcasted_iota(jnp.int32, (step, count), 0) + q * step
        picked = jnp.where(slot == line, 1.0, 0.0).astype(BF16)
        line = lax.broadcasted_iota(jnp.int32, (step, TILES), 0) + q * step
        tile = lax.broadcasted_iota(jnp.int32, (step, TILES), 1)
        cell_row = jnp.where(line == tile * CHUNK + SLOTS, 1.0, 0.0).astype(BF16)
        out_ref[q * step : (q + 1) * step, :] = (mm(picked, rows) + mm(cell_row, cells)).astype(
            BF16
        )


def pack(live, own, lat, lon, pos, rows):
    vmem = pl.BlockSpec(memory_space=pltpu.VMEM)
    return pl.pallas_call(
        pack_kernel,
        out_shape=jax.ShapeDtypeStruct((TILES * CHUNK, 128), BF16),
        in_specs=[pl.BlockSpec(memory_space=pltpu.SMEM)] + [vmem] * 5,
        out_specs=vmem,
        cost_estimate=pl.CostEstimate(flops=700_000_000, bytes_accessed=1_500_000, transcendentals=0),
        name="pack",
    )(live, own, lat, lon, pos, rows)


def tap_weights(cell, frac, offset):
    tap = offset - cell + 3.0
    dist = tap - 3.0 - frac
    weight = jnp.exp(-(dist * dist) / GAUSS)
    return jnp.where((tap >= 0.0) & (tap <= 7.0), weight, 0.0)


def picks():
    eye = np.eye(128, dtype=np.float32)
    shift = np.concatenate([np.eye(128, k=1), np.eye(128, k=-1)], axis=1)
    wanted = (
        {0: 3, 1: 4, 2: 5, 3: 6, 4: 31, 5: 8, 6: 9, 7: 10, 8: 7},
        {0: 4, 1: 5, 2: 6, 3: 7, 4: 8, 5: 9, 6: 10, 7: 11},
        {0: 5, 1: 6, 2: 7, 3: 16, 4: 9, 5: 10, 6: 11, 7: 12, 9: 8},
    )
    side = np.zeros((8, 32, 3, 8, 16), np.float32)
    for b in range(3):
        for target, source in wanted[b].items():
            for line in range(8):
                side[line, source, b, line, target] = 1.0
    return [jnp.asarray(x, BF16) for x in (eye, shift, side.reshape(256, 384))]


def prep_kernel(shift_ref, feat_ref, out_ref):
    count = feat_ref.shape[0]
    turned = jnp.concatenate([feat_ref[i].T for i in range(count)], axis=0)
    moved = mm(turned, shift_ref[...]).astype(BF16)
    out_ref[:, 0] = moved[:, 0:128].reshape(count, 128, 128)
    out_ref[:, 1] = turned.reshape(count, 128, 128)
    out_ref[:, 2] = moved[:, 128:256].reshape(count, 128, 128)


def prep(shift, features):
    return pl.pallas_call(
        prep_kernel,
        grid=(4,),
        out_shape=jax.ShapeDtypeStruct((64, 3, 128, 128), BF16),
        in_specs=[
            pl.BlockSpec((128, 256), lambda i: (0, 0)),
            pl.BlockSpec((16, 128, 128), lambda i: (i, 0, 0)),
        ],
        out_specs=pl.BlockSpec((16, 3, 128, 128), lambda i: (i, 0, 0, 0)),
        cost_estimate=pl.CostEstimate(
            flops=2_200_000_000, bytes_accessed=8_000_000, transcendentals=0
        ),
        compiler_params=pltpu.CompilerParams(vmem_limit_bytes=12 << 20),
        name="prep",
    )(shift, features)


def prep_side_kernel(eye_ref, pick_ref, left_ref, right_ref, head_ref, last_ref, side_ref, cells):
    for at, ref in enumerate((left_ref, right_ref, head_ref, last_ref)):
        cells[:, at * 8 : at * 8 + 8, :] = ref[...]
    turned = nt(eye_ref[...], cells[...].reshape(2048, 128)).astype(BF16)
    for g in range(8):
        moved = mm(turned[:, g * 256 : (g + 1) * 256], pick_ref[...]).astype(BF16)
        for b in range(3):
            side_ref[b * 128 : (b + 1) * 128, g * 128 : (g + 1) * 128] = moved[
                :, b * 128 : (b + 1) * 128
            ]


def prep_side(eye, pick, left, right, head, last):
    vmem = pl.BlockSpec(memory_space=pltpu.VMEM)
    return pl.pallas_call(
        prep_side_kernel,
        out_shape=jax.ShapeDtypeStruct((384, 1024), BF16),
        in_specs=[vmem] * 6,
        out_specs=vmem,
        scratch_shapes=[pltpu.VMEM((64, 32, 128), BF16)],
        cost_estimate=pl.CostEstimate(
            flops=300_000_000, bytes_accessed=1_500_000, transcendentals=0
        ),
        compiler_params=pltpu.CompilerParams(vmem_limit_bytes=6 << 20),
        name="prep_side",
    )(eye, pick, left, right, head, last)


def scatter_kernel(
    in_ref,
    canvas_hbm,
    side_hbm,
    rim_hbm,
    up_hbm,
    down_hbm,
    rows_ref,
    lat_w,
    lon_w,
    side_w,
    canvas_ref,
    side_ref,
    rim_ref,
    block_sem,
    store_sem,
):
    def block_store(step):
        lines = pl.ds(pl.multiple_of(step * 8, 8), 8)
        return pltpu.make_async_copy(
            canvas_ref.at[lines], canvas_hbm.at[lines], block_sem.at[step]
        )

    total = TILES * SLOTS
    for source in range(TILES):
        rows_ref[source * SLOTS : (source + 1) * SLOTS, :] = in_ref[
            source * CHUNK : source * CHUNK + SLOTS, :
        ]
    first = jnp.where(
        lax.broadcasted_iota(jnp.int32, (TILES, TILES * CHUNK), 1)
        == CHUNK * lax.broadcasted_iota(jnp.int32, (TILES, TILES * CHUNK), 0) + SLOTS,
        1.0,
        0.0,
    ).astype(BF16)
    cells = mm(first, in_ref[...])
    cells_t = cells.T.astype(BF16)[: 4 * SLOTS]
    slot_lane = lax.broadcasted_iota(jnp.int32, (TILES, total), 1)
    spread = jnp.where(
        lax.shift_right_logical(slot_lane, 4) == lax.broadcasted_iota(jnp.int32, (TILES, total), 0), 1.0, 0.0
    ).astype(BF16)
    wide = mm(cells_t, spread)
    own_slot = (
        (lax.broadcasted_iota(jnp.int32, (SLOTS, total), 1) & (SLOTS - 1))
        == lax.broadcasted_iota(jnp.int32, (SLOTS, total), 0)
    )
    cell_lat, cell_lon, frac_lat, frac_lon = [
        jnp.sum(
            jnp.where(own_slot, wide[f * SLOTS : (f + 1) * SLOTS], 0.0), axis=0, keepdims=True
        )
        for f in range(4)
    ]
    line = lax.broadcasted_iota(jnp.int32, (72, total), 0)
    lat_index = lax.axis_index("lat")
    first_line = jnp.where(lat_index == 0, 4, 0)
    end_line = jnp.where(lat_index == lax.axis_size("lat") - 1, 68, 72)
    kept = (line >= first_line) & (line < end_line)
    lat_w[...] = jnp.where(
        kept, tap_weights(cell_lat, frac_lat, line.astype(F32) - 4.0), 0.0
    )
    column = lax.broadcasted_iota(jnp.int32, (128, total), 0).astype(F32)
    lon_w[...] = tap_weights(cell_lon, frac_lon, column).astype(BF16)
    line8 = lax.broadcasted_iota(jnp.int32, (8, total), 0)
    column = jnp.where(line8 < 4, line8 - 4, line8 + 124).astype(F32)
    side_w[...] = tap_weights(cell_lon, frac_lon, column).astype(BF16).astype(F32)
    def eight_lines(step, carry):
        start = pl.multiple_of(step * 8, 8)
        lat8 = lat_w[pl.ds(start, 8), :]
        acc = jnp.zeros((8 * 136, 128), F32)
        for k in range(total // 256):
            cols = slice(k * 256, (k + 1) * 256)
            lon = lon_w[:, cols].reshape(8, 16, 256)
            parts = []
            side_parts = []
            side_lon = side_w[:, cols]
            for i in range(8):
                one = jnp.broadcast_to(lat8[i : i + 1, cols], (16, 256)).astype(BF16)
                parts.append((lon * one[None]).reshape(128, 256))
                one8 = jnp.broadcast_to(
                    lat8[i : i + 1, cols].astype(BF16).astype(F32), (8, 256)
                )
                side_parts.append(side_lon * one8)
            parts.append(jnp.concatenate(side_parts, axis=0).astype(BF16))
            acc = acc + mm(jnp.concatenate(parts, axis=0), rows_ref[cols, :])
        ends = acc[0:1024].reshape(8, 128, 128)
        side = acc[1024:1088].reshape(8, 8, 128)
        lines = pl.ds(start, 8)
        canvas_ref[lines, 0:128, :] = ends.astype(BF16)
        canvas_ref[lines, 128:136, :] = side.astype(BF16)
        block_store(step).start()
        side_ref[lines] = jnp.concatenate(
            [side, ends[:, 0:1], ends[:, 127:128], jnp.zeros((8, 6, 128), F32)], axis=1
        ).astype(BF16)
        rim_ref[lines, 0:8, :] = ends[:, 0:8].astype(BF16)
        rim_ref[lines, 8:16, :] = ends[:, 120:128].astype(BF16)
        rim_ref[lines, 16:24, :] = side.astype(BF16)
        return carry

    lax.fori_loop(0, 9, eight_lines, 0)
    stores = [
        pltpu.make_async_copy(canvas_ref.at[1:5], up_hbm, store_sem.at[0]),
        pltpu.make_async_copy(canvas_ref.at[67:72], down_hbm, store_sem.at[1]),
        pltpu.make_async_copy(side_ref, side_hbm, store_sem.at[2]),
        pltpu.make_async_copy(rim_ref, rim_hbm, store_sem.at[3]),
    ]
    for copy in stores:
        copy.start()
    for step in range(9):
        block_store(step).wait()
    for copy in stores:
        copy.wait()


def scatter(incoming):
    vmem = pl.BlockSpec(memory_space=pltpu.VMEM)
    hbm = pl.BlockSpec(memory_space=pltpu.HBM)
    total = TILES * SLOTS
    return pl.pallas_call(
        scatter_kernel,
        out_shape=(
            jax.ShapeDtypeStruct((72, 136, 128), BF16),
            jax.ShapeDtypeStruct((72, 16, 128), BF16),
            jax.ShapeDtypeStruct((72, 24, 128), BF16),
            jax.ShapeDtypeStruct((4, 136, 128), BF16),
            jax.ShapeDtypeStruct((5, 136, 128), BF16),
        ),
        in_specs=[vmem],
        out_specs=(hbm,) * 5,
        scratch_shapes=[
            pltpu.VMEM((total, 128), BF16),
            pltpu.VMEM((72, total), F32),
            pltpu.VMEM((128, total), BF16),
            pltpu.VMEM((8, total), F32),
            pltpu.VMEM((72, 136, 128), BF16),
            pltpu.VMEM((72, 16, 128), BF16),
            pltpu.VMEM((72, 24, 128), BF16),
            pltpu.SemaphoreType.DMA((9,)),
            pltpu.SemaphoreType.DMA((4,)),
        ],
        compiler_params=pltpu.CompilerParams(vmem_limit_bytes=24 << 20),
        cost_estimate=pl.CostEstimate(
            flops=5_200_000_000, bytes_accessed=4_000_000, transcendentals=500_000
        ),
        name="scatter",
    )(incoming)


def own_grad_kernel(canvas, side, feat, feat_side, acc_ref):
    step = 32
    rhs = jnp.concatenate(
        [side[5 - a : 69 - a].reshape(1024, 128) for a in range(3)], axis=1
    )
    total = mm(feat_side[...], rhs)
    for k in range(64 // step):
        lines = range(k * step, (k + 1) * step)
        lhs = jnp.concatenate(
            [jnp.concatenate([feat[i, b] for i in lines], axis=1) for b in range(3)], axis=0
        )
        rhs = jnp.concatenate(
            [
                canvas[k * step + 5 - a : (k + 1) * step + 5 - a, 0:128, :].reshape(
                    step * 128, 128
                )
                for a in range(3)
            ],
            axis=1,
        )
        total = total + mm(lhs, rhs)
    acc_ref[...] = total


def own_grad(canvas, side, feat, feat_side):
    vmem = pl.BlockSpec(memory_space=pltpu.VMEM)
    return pl.pallas_call(
        own_grad_kernel,
        out_shape=jax.ShapeDtypeStruct((384, 384), F32),
        in_specs=[vmem] * 4,
        out_specs=vmem,
        compiler_params=pltpu.CompilerParams(vmem_limit_bytes=20 << 20),
        cost_estimate=pl.CostEstimate(
            flops=2_800_000_000, bytes_accessed=10_000_000, transcendentals=0
        ),
        name="own_grad",
    )(canvas, side, feat, feat_side)


def halo_grad_kernel(
    acc_ref, above_ref, below_ref, feat_hbm, feat_side_ref, sum_hbm, feat, sums, sem
):
    top = pltpu.make_async_copy(feat_hbm.at[0:5], feat.at[0:5], sem.at[0])
    bottom = pltpu.make_async_copy(feat_hbm.at[60:64], feat.at[5:9], sem.at[1])
    top.start()
    bottom.start()
    sums[1152:, :] = jnp.zeros((TILES * SHARE - 1152, 128), BF16)

    def beside(ref, count):
        eight = ref[:, 128:136, :].astype(F32)
        first = ref[:, 0:8, :].astype(F32)
        last = ref[:, 120:128, :].astype(F32)
        return jnp.concatenate(
            [eight, first[:, 0:1], last[:, 7:8], jnp.zeros((count, 6, 128), F32)], axis=1
        ).astype(BF16)

    def lines(count, width):
        return jnp.zeros((count, width, 128), BF16)

    above = jnp.concatenate([above_ref[:, 0:128, :], lines(2, 128)], axis=0)
    below = jnp.concatenate([lines(2, 128), below_ref[:, 0:128, :]], axis=0)
    rhs = jnp.concatenate(
        [
            jnp.concatenate([above[2 - a : 7 - a], below[2 - a : 6 - a]], axis=0).reshape(
                9 * 128, 128
            )
            for a in range(3)
        ],
        axis=1,
    )
    above = jnp.concatenate([beside(above_ref, 5), lines(5, 16)], axis=0)
    below = jnp.concatenate([lines(6, 16), beside(below_ref, 4)], axis=0)
    rhs_side = jnp.concatenate(
        [
            jnp.concatenate([above[2 - a : 10 - a], below[2 - a : 10 - a]], axis=0).reshape(
                256, 128
            )
            for a in range(3)
        ],
        axis=1,
    )
    lhs_side = jnp.concatenate([feat_side_ref[:, 0:128], feat_side_ref[:, 896:1024]], axis=1)
    total = acc_ref[...] + mm(lhs_side, rhs_side)
    top.wait()
    bottom.wait()
    lhs = jnp.concatenate(
        [jnp.concatenate([feat[i, b] for i in range(9)], axis=1) for b in range(3)], axis=0
    )
    total = total + mm(lhs, rhs)
    for a in range(3):
        for b in range(3):
            at = (a * 3 + b) * 128
            sums[at : at + 128, :] = total[
                b * 128 : (b + 1) * 128, a * 128 : (a + 1) * 128
            ].astype(BF16)
    store = pltpu.make_async_copy(sums, sum_hbm, sem.at[2])
    store.start()
    store.wait()


def halo_grad(acc, above, below, feat, feat_side):
    vmem = pl.BlockSpec(memory_space=pltpu.VMEM)
    hbm = pl.BlockSpec(memory_space=pltpu.HBM)
    return pl.pallas_call(
        halo_grad_kernel,
        out_shape=jax.ShapeDtypeStruct((TILES * SHARE, 128), BF16),
        in_specs=[vmem, vmem, vmem, hbm, vmem],
        out_specs=hbm,
        scratch_shapes=[
            pltpu.VMEM((9, 3, 128, 128), BF16),
            pltpu.VMEM((TILES * SHARE, 128), BF16),
            pltpu.SemaphoreType.DMA((3,)),
        ],
        cost_estimate=pl.CostEstimate(
            flops=420_000_000, bytes_accessed=3_500_000, transcendentals=0
        ),
        compiler_params=pltpu.CompilerParams(vmem_limit_bytes=12 << 20),
        name="halo_grad",
    )(acc, above, below, feat, feat_side)


def sides_kernel(rim_ref, above_ref, below_ref, right_ref, left_ref):
    def tall(at, cols):
        block = rim_ref[3:69, at : at + 8, :].astype(F32)
        return jnp.concatenate(
            [
                block[0:5] + above_ref[:, cols : cols + 8, :].astype(F32),
                block[5:62],
                block[62:66] + below_ref[:, cols : cols + 8, :].astype(F32),
            ],
            axis=0,
        )

    head = tall(0, 0)
    last = tall(8, 120)
    side = tall(16, 128)
    blank = jnp.zeros((66, 4, 128), F32)
    right_ref[...] = jnp.concatenate([last[:, 7:8], side[:, 4:8], blank[:, :3]], axis=1).astype(
        BF16
    )
    left_ref[...] = jnp.concatenate([side[:, 1:4], head[:, 0:1], blank], axis=1).astype(BF16)


def sides(rim, above, below):
    vmem = pl.BlockSpec(memory_space=pltpu.VMEM)
    shape = jax.ShapeDtypeStruct((66, 8, 128), BF16)
    return pl.pallas_call(
        sides_kernel,
        out_shape=(shape, shape),
        in_specs=[vmem] * 3,
        out_specs=(vmem, vmem),
        cost_estimate=pl.CostEstimate(flops=1_000_000, bytes_accessed=1_000_000, transcendentals=0),
        compiler_params=pltpu.CompilerParams(vmem_limit_bytes=4 << 20),
        name="sides",
    )(rim, above, below)


def conv_kernel(canvas_ref, above_ref, below_ref, left_ref, right_ref, weight_ref, out_ref, grid):
    @pl.when(pl.program_id(0) == 0)
    def _():
        grid[5:62, 0:128, :] = canvas_ref[8:65, 0:128, :]
        grid[0:5, 0:128, :] = (
            canvas_ref[3:8, 0:128, :].astype(F32) + above_ref[:, 0:128, :].astype(F32)
        ).astype(BF16)
        grid[62:66, 0:128, :] = (
            canvas_ref[65:69, 0:128, :].astype(F32) + below_ref[:, 0:128, :].astype(F32)
        ).astype(BF16)
        left = left_ref[...].astype(F32)
        right = right_ref[...].astype(F32)
        blank = jnp.zeros((66, 14, 128), F32)
        grid[:, 0:16, :] = (
            grid[:, 0:16, :].astype(F32)
            + jnp.concatenate([left[:, 1:5], blank[:, :12]], axis=1)
        ).astype(BF16)
        grid[:, 112:128, :] = (
            grid[:, 112:128, :].astype(F32)
            + jnp.concatenate([blank[:, :13], right[:, 0:3]], axis=1)
        ).astype(BF16)
        side = canvas_ref[3:69, 128:136, :].astype(F32)
        side = jnp.concatenate(
            [
                side[0:5] + above_ref[:, 128:136, :].astype(F32),
                side[5:62],
                side[62:66] + below_ref[:, 128:136, :].astype(F32),
            ],
            axis=0,
        )
        grid[:, 128:144, :] = jnp.concatenate(
            [side[:, 4:5] + right[:, 3:4], blank, side[:, 3:4] + left[:, 0:1]], axis=1
        ).astype(BF16)

    start = pl.program_id(0) * 8
    taps = jnp.concatenate(
        [grid[pl.ds(start + 2 - a, 8)].reshape(8 * 144, 128) for a in range(3)], axis=1
    )
    weight = jnp.concatenate([weight_ref[a].reshape(384, 128) for a in range(3)], axis=1)
    every = nt(taps, weight).reshape(8, 144, 384)
    for i in range(8):
        one = every[i]
        got = (
            one[:, 128:256]
            + pltpu.roll(one[:, 0:128], 143, 0)
            + pltpu.roll(one[:, 256:384], 1, 0)
        )
        out_ref[i] = got[0:128].astype(BF16)


def conv(canvas, above, below, left, right, weight):
    def whole(x):
        return pl.BlockSpec(
            x.shape, lambda i: (0,) * x.ndim, pipeline_mode=pl.Buffered(1)
        )

    args = (canvas, above, below, left, right, weight)
    return pl.pallas_call(
        conv_kernel,
        grid=(8,),
        out_shape=jax.ShapeDtypeStruct((64, 128, 128), BF16),
        in_specs=[whole(x) for x in args],
        out_specs=pl.BlockSpec((8, 128, 128), lambda i: (i, 0, 0)),
        scratch_shapes=[pltpu.VMEM((66, 144, 128), BF16)],
        compiler_params=pltpu.CompilerParams(vmem_limit_bytes=16 << 20),
        cost_estimate=pl.CostEstimate(
            flops=2_700_000_000, bytes_accessed=4_500_000, transcendentals=0
        ),
        name="conv",
    )(*args)


def share_kernel(in_ref, out_ref):
    def line_of(shape, axis):
        row = lax.broadcasted_iota(jnp.int32, shape, axis)
        line = lax.broadcasted_iota(jnp.int32, shape, 1 - axis)
        return jnp.where(lax.rem(row, SHARE) == line, 1.0, 0.0).astype(BF16)

    mine = mm(line_of((16, TILES * SHARE), 1), in_ref[...]).astype(BF16)
    block = mm(line_of((8 * SHARE, 16), 0), mine).astype(BF16)
    for i in range(TILES // 8):
        out_ref[i * 8 * SHARE : (i + 1) * 8 * SHARE, :] = block


def share(got):
    vmem = pl.BlockSpec(memory_space=pltpu.VMEM)
    return pl.pallas_call(
        share_kernel,
        out_shape=jax.ShapeDtypeStruct(got.shape, BF16),
        in_specs=[vmem],
        out_specs=vmem,
        compiler_params=pltpu.CompilerParams(vmem_limit_bytes=3 << 20),
        cost_estimate=pl.CostEstimate(flops=10_000_000, bytes_accessed=1_000_000, transcendentals=0),
        name="share",
    )(got)


def finish_kernel(in_ref, out_ref):
    out_ref[...] = in_ref[0:1152, :].astype(F32)


def finish(every):
    vmem = pl.BlockSpec(memory_space=pltpu.VMEM)
    return pl.pallas_call(
        finish_kernel,
        out_shape=jax.ShapeDtypeStruct((1152, 128), F32),
        in_specs=[vmem],
        out_specs=vmem,
        compiler_params=pltpu.CompilerParams(vmem_limit_bytes=2 << 20),
        cost_estimate=pl.CostEstimate(flops=0, bytes_accessed=900_000, transcendentals=0),
        name="finish",
    )(every)


def exchange(rows):
    pairs = rows.reshape(TILES, -1, 2, rows.shape[1])
    return lax.all_to_all(pairs, AXES, 0, 0, tiled=True).reshape(rows.shape)


def both_ways(forth, back, axis, closed):
    count = lax.axis_size(axis)
    ends = count if closed else count - 1
    return (
        lax.ppermute(forth, axis, [(i, (i + 1) % count) for i in range(ends)]),
        lax.ppermute(back, axis, [((i + 1) % count, i) for i in range(ends)]),
    )


def shards(grad_rows, owner, lat_offset, lon_offset, position, live_count, features, conv_weight):
    count = grad_rows.shape[0]
    outgoing = pack(
        live_count,
        owner.reshape(1, count),
        lat_offset.reshape(1, count),
        lon_offset.reshape(1, count),
        position.T,
        grad_rows,
    )
    incoming = exchange(outgoing)
    eye, shift, pick = picks()
    last, head = features[:, 120:128], features[:, 0:8]
    left, right = both_ways(last, head, "lon", True)
    feat = prep(shift, features)
    canvas, side, rim, up, down = scatter(incoming)
    side, left, right = lax.optimization_barrier((side, left, right))
    feat_side = prep_side(eye, pick, left, right, head, last)
    grid_above, grid_below = both_ways(down, up, "lat", False)
    acc = own_grad(canvas, side, feat, feat_side)
    part = halo_grad(acc, grid_above, grid_below, feat, feat_side)
    got = exchange(part)
    send_right, send_left = sides(rim, grid_above, grid_below)
    from_left, from_right = both_ways(send_right, send_left, "lon", True)
    got, _, _ = lax.optimization_barrier((got, send_right, send_left))
    every = exchange(share(got))
    input_grad = conv(canvas, grid_above, grid_below, from_left, from_right, conv_weight)
    weight_grad = finish(every)
    return input_grad, weight_grad.reshape(3, 3, 128, 128)


def solution(mesh):
    placed = (
        P(("lat", "lon"), None),
        P(("lat", "lon"), None),
        P(("lat", "lon")),
        P(("lat", "lon")),
        P(("lat", "lon"), None),
        P(("lat", "lon")),
        P("lat", "lon", None),
        P(),
    )
    return jax.shard_map(
        shards, mesh=mesh, in_specs=placed, out_specs=(P("lat", "lon", None), P()), check_vma=False
    )
```
